32 devices in a mesh: dp: 8 (over y, x, core), tensor: 4 (over z).
Axes of the slice: x: 2, y: 2, z: 4, core: 2. Of those that a mesh axis runs over, the one named last changes fastest.
Arguments:
- hidden_in: bfloat16 [16, 1024, 768], P('dp', 'tensor'), may hold values from -6 to 6
- cotangent: bfloat16 [16, 1024, 768], P('dp', 'tensor'), may hold values from -6 to 6
- segment_ids: int32 [16, 1024], P('dp'), may hold values from 0 to 6, as said below
- w_qkv: bfloat16 [3, 768, 768], P(None, 'dp', 'tensor'), may hold values from -0.21875 to 0.21875
- w_out: bfloat16 [768, 768], P('tensor', 'dp'), may hold values from -1.25 to 1.25
- w_in: bfloat16 [2, 768, 1152], P(None, 'dp', 'tensor'), may hold values from -0.21875 to 0.21875
- w_down: bfloat16 [1152, 768], P('tensor', 'dp'), may hold values from -0.1875 to 0.1875
- norm_gains: bfloat16 [2, 768], P(None, 'dp'), may hold values from 0.099609375 to 1.8984375
Outputs:
- layer_out: bfloat16 [16, 1024, 768], P('dp', 'tensor')
- grad_input: bfloat16 [16, 1024, 768], P('dp', 'tensor')
- grad_qkv: float32 [3, 768, 768], P(None, 'dp', 'tensor')
- grad_out: float32 [768, 768], P('tensor', 'dp')
- grad_in: float32 [2, 768, 1152], P(None, 'dp', 'tensor')
- grad_down: float32 [1152, 768], P('tensor', 'dp')
- grad_gains: float32 [2, 768], P(None, 'dp')
The draws below stay inside these ranges and needn't reach their ends.
Inputs may be any that keep to these rules, and one draw needn't show every extreme that they name: `segment_ids`: each row starts with id 0 and its ids never fall, rising by one at each new document; documents are 204 to 2048 tokens long before they are cut at row ends, so only a row's first and last run may be shorter.
All inputs are finite; a program needn't handle non-finite values.
Results may differ from the reference program's by a relative error of at most 0.023.
Values may be sent and summed in bfloat16 or wider, within the bound.
A program may use at most 128 MiB of HBM per device.

```python
import math
import jax
import jax.numpy as jnp
from jax import lax

D = 768
H = 12
HD = 64
FF = 1152
L = 1024
ROWS = 16


def draw_segment_ids(key, part):
    shortest = max(L // 5, 1)
    doc_lengths = jax.random.randint(key, (ROWS, 16), shortest, 2 * L + 1)
    offset = jax.random.randint(jax.random.fold_in(key, 7), (ROWS, 1), 0, doc_lengths[:, :1])
    row_index = jnp.arange(ROWS, dtype=jnp.int32)[:, None]
    doc_lengths = jnp.where(row_index == 0, shortest, doc_lengths).astype(jnp.int32)
    offset = jnp.where(row_index == 0, shortest - 1, offset).astype(jnp.int32)
    ends = jnp.cumsum(doc_lengths, axis=1) - offset
    places = jnp.arange(L, dtype=jnp.int32)
    passed = (ends[:, None, :] <= places[None, :, None]).astype(jnp.int32)
    return jnp.sum(passed, axis=-1).astype(jnp.int32)


def with_spikes(values, stream_key, source, target, blocks, factor):
    def block_of(position):
        return (jnp.arange(values.shape[position]) // (values.shape[position] // blocks)).reshape((-1,) + (1,) * (values.ndim - 1 - position))

    one_side = jax.random.permutation(stream_key, blocks)[block_of(target)]
    other_side = (block_of(target) + blocks // 2) % blocks
    return jnp.where((block_of(source) == one_side) | (block_of(source) == other_side), factor * values, values)


def shard_levels(rng, shape, cuts, least, largest):
    level, own = 1.0, jax.random.fold_in(rng, 6)
    for axis_at, blocks in cuts:
        draws = jnp.exp(jax.random.uniform(jax.random.fold_in(own, axis_at), (blocks,), jnp.float32, least / len(cuts), largest / len(cuts)))
        level = level * jnp.repeat(draws, shape[axis_at] // blocks).reshape([-1 if axis == axis_at else 1 for axis in range(len(shape))])
    return level


def noise(key, shape, scale, limit, split=(), kind=jnp.bfloat16):
    values = jax.random.normal(key, shape, jnp.float32) * scale
    if len(split) > 0:
        values = shard_levels(key, shape, split, -0.22, 0.18) * values
    return jnp.clip(values, min=-limit, max=limit).astype(kind)


def gaussian_with(rng, dims, width, bound, pieces, heavy, kind=jnp.bfloat16):
    drawn = width * jax.random.normal(rng, dims, jnp.float32)
    if pieces:
        drawn = drawn * shard_levels(rng, dims, pieces, -0.22, 0.18)
    return jnp.clip(with_spikes(drawn, jax.random.fold_in(rng, 3), *heavy), -bound, bound).astype(kind)


def setup_inputs(seed: int = 0) -> dict:
    arg_keys = jax.random.split(jax.random.key(seed), 9)
    hidden_in = noise(arg_keys[0], (ROWS, L, D), 1.0, 6.0, ((0, 8), (1, 4)))
    cotangent = gaussian_with(arg_keys[1], (ROWS, L, D), 1.0, 6.0, ((0, 8), (1, 4)), (0, 2, 8, 2.0))
    segment_ids = draw_segment_ids(jax.random.fold_in(arg_keys[8], 71), 0)
    w_qkv = noise(arg_keys[3], (3, D, D), D ** -0.5, 0.21875, ((1, 8), (2, 4)))
    w_out = noise(arg_keys[4], (D, D), (D // 32) ** -0.5, 1.25, ((0, 4), (1, 8)))
    w_in = noise(arg_keys[5], (2, D, FF), D ** -0.5, 0.21875, ((1, 8), (2, 4)))
    w_down = noise(arg_keys[6], (FF, D), FF ** -0.5, 0.1875, ((0, 4), (1, 8)))
    norm_gains = jnp.clip(1.0 + 0.18 * jax.random.normal(arg_keys[7], (2, D), jnp.float32), 0.099609375, 1.8984375).astype(jnp.bfloat16)
    return dict(hidden_in=hidden_in, cotangent=cotangent, segment_ids=segment_ids, w_qkv=w_qkv, w_out=w_out, w_in=w_in, w_down=w_down, norm_gains=norm_gains)


EPS = 1e-05
THETA = 160000.0
HIGH = lax.Precision.HIGHEST

@jax.custom_vjp
def low(v):
    return lax.optimization_barrier(v.astype(jnp.bfloat16)).astype(jnp.float32)

@jax.custom_vjp
def low_back(v):
    return v

def low_keep(v):
    return (low(v), None)

def low_pass(kept, grad):
    return (grad,)

def back_keep(v):
    return (v, None)

def back_low(kept, grad):
    return (low(grad),)
low.defvjp(low_keep, low_pass)
low_back.defvjp(back_keep, back_low)

def layer_norm(value, gain):
    centred = value - lax.optimization_barrier(jnp.mean(value, axis=-1, keepdims=True))
    variance = lax.optimization_barrier(jnp.mean(centred * centred, axis=-1, keepdims=True))
    return centred * lax.rsqrt(variance + EPS) * gain

def positions_of(segments):
    index = lax.broadcasted_iota(jnp.int32, segments.shape, 1)
    change = jnp.concatenate([jnp.ones_like(segments[:, :1]), (segments[:, 1:] != segments[:, :-1]).astype(jnp.int32)], axis=1)
    first = lax.cummax(jnp.where(change > 0, index, 0), axis=1)
    return index - first

def rope_tables(positions, head_size):
    half = head_size // 2
    frequency = THETA ** (-2.0 * jnp.arange(half, dtype=jnp.float32) / head_size)
    angle = positions.astype(jnp.float32)[..., None] * frequency
    cosine = jnp.concatenate([jnp.cos(angle), jnp.cos(angle)], axis=-1)[..., None, :]
    sine = jnp.concatenate([jnp.sin(angle), jnp.sin(angle)], axis=-1)[..., None, :]
    return (cosine, sine)

def rotate(value, cosine, sine):
    half = value.shape[-1] // 2
    turned = jnp.concatenate([-value[..., half:], value[..., :half]], axis=-1)
    return value * cosine + turned * sine

def forward(hidden_row, w_qkv, w_out, w_in, w_down, gains, segment, cosine, sine):
    length = hidden_row.shape[0]
    norm_one = low(layer_norm(hidden_row, gains[0]))
    raw = jnp.einsum('ld,cde->lce', norm_one, w_qkv, precision=HIGH)
    query = low(rotate(low_back(raw[:, 0].reshape(length, H, HD)), cosine, sine))
    keys = low(rotate(low_back(raw[:, 1].reshape(length, H, HD)), cosine, sine))
    values = low(low_back(raw[:, 2].reshape(length, H, HD)))
    scores = low_back(jnp.einsum('qhd,khd->hqk', query, keys, precision=HIGH) * (1.0 / math.sqrt(HD)))
    allowed = (segment[:, None] == segment[None, :])[None]
    scores = jnp.where(allowed, scores, -1e+30)
    top = lax.optimization_barrier(jnp.max(scores, axis=-1, keepdims=True))
    expo = jnp.exp(scores - top)
    probs = low(expo / lax.optimization_barrier(jnp.sum(expo, axis=-1, keepdims=True)))
    mixed = jnp.einsum('hqk,khd->qhd', probs, values, precision=HIGH).reshape(length, H * HD)
    mixed = low_back(low(mixed))
    residual = hidden_row + low_back(jnp.dot(mixed, w_out, precision=HIGH))
    norm_two = low(layer_norm(residual, gains[1]))
    gate_up = low_back(jnp.einsum('ld,cdf->lcf', norm_two, w_in, precision=HIGH))
    product = low(jax.nn.gelu(gate_up[:, 0], approximate=False) * gate_up[:, 1])
    return residual + low_back(jnp.dot(product, w_down, precision=HIGH))

def reference(hidden_in, cotangent, segment_ids, w_qkv, w_out, w_in, w_down, norm_gains):
    weights = tuple((a.astype(jnp.float32) for a in (w_qkv, w_out, w_in, w_down, norm_gains)))
    positions = positions_of(segment_ids)
    cosine, sine = rope_tables(positions, HD)

    def step(totals, item):
        hidden_row, cot_row, seg_row, cos_row, sin_row = item

        def run(h_in, a_w, b_w, c_w, d_w, e_w):
            return forward(h_in, a_w, b_w, c_w, d_w, e_w, seg_row, cos_row, sin_row)
        out_row, back = jax.vjp(run, hidden_row.astype(jnp.float32), *weights)
        grads = back(cot_row.astype(jnp.float32))
        summed = tuple((t + g for t, g in zip(totals, grads[1:])))
        return (summed, (out_row.astype(jnp.bfloat16), grads[0].astype(jnp.bfloat16)))
    zeros = tuple((jnp.zeros(w.shape, jnp.float32) for w in weights))
    totals, (outputs, grad_rows) = lax.scan(step, zeros, (hidden_in, cotangent, segment_ids, cosine, sine))
    return (outputs, grad_rows, totals[0], totals[1], totals[2], totals[3], totals[4])
```

```python
import functools
import math

import jax
import jax.numpy as jnp
from jax import lax
from jax.experimental import pallas as pl
from jax.experimental.pallas import tpu as pltpu
from jax.sharding import PartitionSpec as P

HD = 64
EPS = 1e-05
THETA = 160000.0
BIG = 1e30
SEGS = 8
SPARE = 8
TO_EXP2 = math.log2(math.e) / math.sqrt(HD)
MESH = pl.DeviceIdType.MESH
BF, F32 = jnp.bfloat16, jnp.float32
VM = pltpu.VMEM
WIDE = 60 * 1024 * 1024


def dot(a, b, dims=((1,), (0,))):
    return lax.dot_general(a, b, (dims, ((), ())), preferred_element_type=F32)


NT = ((1,), (1,))


def erf(x):
    x = jnp.clip(x, -3.832506856900711, 3.832506856900711)
    s = x * x
    p = 0.00022905065861350646
    for c in (0.0034082910107109506, 0.050955695062380861, 0.18520832239976145, 1.128379143519084):
        p = p * s + c
    q = -1.1791602954361697e-7
    for c in (
        0.000023547966471313185,
        0.0010179625278914885,
        0.014070470171167667,
        0.11098505178285362,
        0.49746925110067538,
        1.0,
    ):
        q = q * s + c
    return x * p / q


class Place:
    def __init__(self, ndp, nt):
        self.nt = nt
        self.stride = ndp // 8
        self.dp, self.z = lax.axis_index("dp"), lax.axis_index("tensor")
        high = self.dp // self.stride
        self.b = (high % 2, (high // 2) % 2, high // 4)
        self.core = self.dp % 2

    def flip(self, bit):
        return (self.dp + (1 - 2 * self.b[bit]) * self.stride * 2**bit, self.z)

    def along(self, step):
        return (self.dp, (self.z + step) % self.nt)

    def pair(self, core, z):
        return (self.dp - self.core + core, z)

    def barrier(self, group):
        others = [self.along(s) for s in range(1, self.nt)]
        others += [self.flip(1), self.flip(2)]
        if group or self.stride == 1:
            others += [self.pair(1 - self.core, self.z)]
        if self.stride > 1:
            others += [self.flip(0)]
        if group:
            others += [self.pair(1 - self.core, (self.z + s) % self.nt) for s in range(1, self.nt)]
        sem = pltpu.get_barrier_semaphore()
        for device in others:
            pl.semaphore_signal(sem, inc=1, device_id=device, device_id_type=MESH)
        pl.semaphore_wait(sem, len(others))


def remote(src, dst, send, recv, device):
    return pltpu.make_async_remote_copy(
        src_ref=src, dst_ref=dst, send_sem=send, recv_sem=recv, device_id=device, device_id_type=MESH
    )


def enter_copies(me, src, dst, send, recv):
    starts, ends = [], []
    for row in range(2):
        for core in range(2):
            z = 2 * me.core + row
            k = 2 * row + core
            here = jnp.logical_and(z == me.z, core == me.core)
            copy = remote(src.at[row, core], dst.at[me.z], send.at[k], recv.at[me.z], me.pair(core, z))
            local = pltpu.make_async_copy(src.at[row, core], dst.at[me.z], recv.at[me.z])
            starts.append((here, copy, local))
    for z in range(me.nt):
        ends.append(remote(src.at[0, 0], dst.at[z], send.at[0], recv.at[z], me.pair(1 - me.core, z)))
    return starts, ends


def leave_copies(me, src, dst, send, recv):
    starts, ends = [], []
    for z in range(me.nt):
        here = jnp.logical_and(z == me.z, me.z // 2 == me.core)
        k = 2 * (me.z % 2) + me.core
        to = dst.at[me.z % 2, me.core]
        copy = remote(src.at[z], to, send.at[z], recv.at[k], me.pair(me.z // 2, z))
        local = pltpu.make_async_copy(src.at[z], to, recv.at[k])
        starts.append((here, copy, local))
    for k in range(4):
        ends.append(remote(src.at[0], dst.at[k // 2, k % 2], send.at[0], recv.at[k], me.pair(1 - me.core, me.z)))
    return starts, ends


def start_all(starts):
    for here, copy, local in starts:
        pl.when(here)(local.start)
        pl.when(jnp.logical_not(here))(copy.start)


def wait_sends(starts):
    for here, copy, _ in starts:
        pl.when(jnp.logical_not(here))(copy.wait_send)


class Gather:
    COPIES = 12

    def __init__(self, me, shard, out, send, recv, own):
        self.me, self.shard, self.out, self.own = me, shard, out, own
        b0, b1, b2 = me.b
        nt, h = me.nt, me.nt // 2
        lo, hi, both = pl.ds(0, h), pl.ds(h, h), pl.ds(0, 2)

        def pair(k, at, other, device):
            cp = remote(out.at[at], out.at[at], send.at[k], recv.at[k], device)
            back = remote(out.at[other], out.at[other], send.at[k], recv.at[k], device)
            return cp, back

        n = nt - 1
        self.z = []
        for s in range(1, nt):
            at = (b2, b1, b0, me.z)
            frm = (b2, b1, b0, (me.z + nt - s) % nt)
            cp = remote(shard, out.at[at], send.at[s - 1], recv.at[s - 1], me.along(s))
            back = remote(shard, out.at[frm], send.at[s - 1], recv.at[s - 1], me.along(s))
            self.z.append((cp, back))
        x, y, core = me.flip(1), me.flip(2), me.flip(0)
        o0, o1, o2 = 1 - b0, 1 - b1, 1 - b2
        self.one = [
            pair(n, (b2, b1, b0, lo), (b2, o1, b0, lo), x),
            pair(n + 1, (b2, b1, b0, hi), (o2, b1, b0, hi), y),
        ]
        self.two = [
            pair(n + 2, (b2, both, b0, lo), (o2, both, b0, lo), y),
            pair(n + 3, (both, b1, b0, hi), (both, o1, b0, hi), x),
        ]
        self.core_a = [pair(n + 4, (b2, b1, b0), (b2, b1, o0), core)]
        self.core_b = [
            pair(n + 5, (b2, o1, b0, lo), (b2, o1, o0, lo), core),
            pair(n + 6, (o2, b1, b0, hi), (o2, b1, o0, hi), core),
        ]
        self.core_c = [
            pair(n + 7, (o2, both, b0, lo), (o2, both, o0, lo), core),
            pair(n + 8, (both, o1, b0, hi), (both, o1, o0, hi), core),
        ]

    def start_z(self):
        b0, b1, b2 = self.me.b
        self.mine = pltpu.make_async_copy(self.shard, self.out.at[b2, b1, b0, self.me.z], self.own)
        self.mine.start()
        for cp, _ in self.z:
            cp.start()

    @staticmethod
    def start(copies):
        for cp, _ in copies:
            cp.start()

    @staticmethod
    def landed(copies):
        for _, back in copies:
            back.wait_recv()

    def after_z(self):
        self.mine.wait()
        self.landed(self.z)
        self.start(self.one + self.core_a)

    def after_one(self):
        self.landed(self.one)
        self.start(self.two + self.core_b)

    def after_two(self):
        self.landed(self.two)
        self.start(self.core_c)

    def finish(self):
        for group in (self.core_a, self.core_b, self.core_c):
            self.landed(group)
        for group in (self.z, self.one, self.two, self.core_a, self.core_b, self.core_c):
            for cp, _ in group:
                cp.wait_send()


def gather_kernel(ndp, nt, w1, w2, hid, cot, seg, g1, g2, hid_o, cot_o, seg_o, s1, r1, s2, r2, own, se, re, sc, rc, ss):
    me = Place(ndp, nt)
    me.barrier(True)
    first = Gather(me, w1, g1, s1, r1, own.at[0])
    second = Gather(me, w2, g2, s2, r2, own.at[1])
    hs, he = enter_copies(me, hid, hid_o, se, re)
    cs, ce = enter_copies(me, cot, cot_o, sc, rc)
    swap = remote(seg, seg_o, ss.at[0], ss.at[1], me.pair(1 - me.core, me.z))
    swap.start()
    first.start_z()
    start_all(hs)
    second.start_z()
    start_all(cs)
    first.after_z()
    first.after_one()
    second.after_z()
    first.after_two()
    second.after_one()
    second.after_two()
    for e in he + ce:
        e.wait_recv()
    swap.wait()
    first.finish()
    second.finish()
    wait_sends(hs)
    wait_sends(cs)


def anyspace(n):
    return [pl.BlockSpec(memory_space=pl.ANY)] * n


def gather_all(ndp, nt, w1, w2, hid, cot, seg):
    half = hid.shape[2]
    sds = jax.ShapeDtypeStruct
    dma = pltpu.SemaphoreType.DMA
    n = Gather.COPIES
    return pl.pallas_call(
        functools.partial(gather_kernel, ndp, nt),
        in_specs=anyspace(5),
        out_specs=anyspace(5),
        out_shape=[
            sds((2, 2, 2, nt) + w1.shape, BF),
            sds((2, 2, 2, nt) + w2.shape, BF),
            sds((nt, half, hid.shape[3]), BF),
            sds((nt, half, hid.shape[3]), BF),
            sds(seg.shape, seg.dtype),
        ],
        scratch_shapes=[dma((n,)), dma((n,)), dma((n,)), dma((n,)), dma((2,))] + [dma((4,))] * 4 + [dma((2,))],
        compiler_params=pltpu.CompilerParams(collective_id=0, has_side_effects=True),
        name="gather_all",
    )(w1, w2, hid, cot, seg)


class Scatter:
    COPIES = 9

    def __init__(self, me, g, out, bufs, send, recv):
        self.me, self.g, self.out = me, g, out
        self.r0, self.s0, self.r1, self.s1, self.r2, self.s2, self.rz = bufs
        b0, b1, b2 = me.b
        o0, o1, o2 = 1 - b0, 1 - b1, 1 - b2
        h, nt = me.nt // 2, me.nt
        both = pl.ds(0, 2)
        x, y, core = me.flip(1), me.flip(2), me.flip(0)
        part = (pl.ds(0, h), pl.ds(h, h))

        def copy(k, src, dst, device):
            return remote(src, dst, send.at[k], recv.at[k], device)

        self.core = [
            copy(i, g.at[both, both, o0, part[i]], self.r0.at[i], core) for i in range(2)
        ]
        self.one = [
            copy(2, self.s0.at[0, both, o1], self.r1.at[0], x),
            copy(3, self.s0.at[1, o2], self.r1.at[1], y),
        ]
        self.two = [
            copy(4, self.s1.at[0, o2], self.r2.at[0], y),
            copy(5, self.s1.at[1, o1], self.r2.at[1], x),
        ]
        self.z = [
            copy(5 + s, self.s2.at[(me.z + s) % nt], self.rz.at[s - 1], me.along(s)) for s in range(1, nt)
        ]

    def begin(self):
        for cp in self.core:
            cp.start()

    def add_core(self, i):
        b0 = self.me.b[0]
        h = self.me.nt // 2
        self.core[i].wait_recv()
        for a in range(2):
            for b in range(2):
                for t in range(h):
                    total = self.g[a, b, b0, i * h + t].astype(F32) + self.r0[i, a, b, t].astype(F32)
                    self.s0[i, a, b, t] = total.astype(BF)
        self.one[i].start()

    def add_one(self, i):
        _, b1, b2 = self.me.b
        self.one[i].wait_recv()
        for a in range(2):
            for t in range(self.me.nt // 2):
                mine = self.s0[0, a, b1, t] if i == 0 else self.s0[1, b2, a, t]
                self.s1[i, a, t] = (mine.astype(F32) + self.r1[i, a, t].astype(F32)).astype(BF)
        self.two[i].start()

    def add_two(self, i):
        _, b1, b2 = self.me.b
        h = self.me.nt // 2
        self.two[i].wait_recv()
        own = b2 if i == 0 else b1
        for t in range(h):
            total = self.s1[i, own, t].astype(F32) + self.r2[i, t].astype(F32)
            self.s2[i * h + t] = total.astype(BF)

    def send_z(self):
        for cp in self.z:
            cp.start()

    def finish(self):
        total = self.s2[self.me.z].astype(F32)
        for s in range(self.me.nt - 1):
            self.z[s].wait_recv()
            total = total + self.rz[s].astype(F32)
        self.out[...] = total
        for cp in self.core + self.one + self.two + self.z:
            cp.wait_send()


def scatter_scratch(nt, r, c):
    h = nt // 2
    dma = pltpu.SemaphoreType.DMA
    return [
        VM((2, 2, 2, h, r, c), BF),
        VM((2, 2, 2, h, r, c), BF),
        VM((2, 2, h, r, c), BF),
        VM((2, 2, h, r, c), BF),
        VM((2, h, r, c), BF),
        VM((nt, r, c), BF),
        VM((nt - 1, r, c), BF),
        dma((6 + nt - 1,)),
        dma((6 + nt - 1,)),
    ]


def scatter_kernel(ndp, nt, g, act, out, act_o, *scratch):
    bufs, (send, recv, sl, rl) = scratch[:7], scratch[7:]
    me = Place(ndp, nt)
    me.barrier(True)
    rs = Scatter(me, g, out, bufs, send, recv)
    rs.begin()
    ls, le = leave_copies(me, act, act_o, sl, rl)
    start_all(ls)
    for i in range(2):
        rs.add_core(i)
    for i in range(2):
        rs.add_one(i)
    for i in range(2):
        rs.add_two(i)
    rs.send_z()
    rs.finish()
    for e in le:
        e.wait_recv()
    wait_sends(ls)


def scatter_all(ndp, nt, g, act, ident):
    r, c = g.shape[4:]
    sds = jax.ShapeDtypeStruct
    half, width = act.shape[1:]
    dma = pltpu.SemaphoreType.DMA
    vm = pl.BlockSpec(memory_space=VM)
    hbm = pl.BlockSpec(memory_space=pl.ANY)
    return pl.pallas_call(
        functools.partial(scatter_kernel, ndp, nt),
        in_specs=[vm, hbm],
        out_specs=[vm, hbm],
        out_shape=[sds((r, c), F32), sds((2, 2, half, width), BF)],
        scratch_shapes=scatter_scratch(nt, r, c) + [dma((4,)), dma((4,))],
        compiler_params=pltpu.CompilerParams(
            collective_id=ident, has_side_effects=True, vmem_limit_bytes=WIDE
        ),
        name=f"scatter_{ident}",
    )(g, act)


def standard(v):
    centred = v - jnp.mean(v, axis=-1, keepdims=True)
    scale = lax.rsqrt(jnp.mean(centred * centred, axis=-1, keepdims=True) + EPS)
    return centred * scale, scale


def norm_back(grad, xhat, scale, gain):
    e = grad * gain
    inner = jnp.mean(e * xhat, axis=-1, keepdims=True)
    return scale * (e - jnp.mean(e, axis=-1, keepdims=True) - xhat * inner)


def rows_loop(total, step, body):
    def run(i, carry):
        body(pl.ds(pl.multiple_of(i * step, step), step))
        return carry

    lax.fori_loop(0, total // step, run, 0)


def turned(v, cosine, sine):
    lane = lax.broadcasted_iota(jnp.int32, v.shape, 1)
    other = jnp.where(lane % HD < HD // 2, pltpu.roll(v, 128 - HD // 2, 1), pltpu.roll(v, HD // 2, 1))
    return v * cosine + other * sine


def project_kernel(nt, hid, gain, w_ref, cos, sin, q, k, v, n1, wf, raw):
    d = hid.shape[1]
    el = d // nt

    def norm(at):
        xhat, _ = standard(hid[at, :].astype(F32))
        n1[at, :] = (xhat * gain[...]).astype(BF)

    rows_loop(hid.shape[0], 64, norm)
    for t in range(nt):
        for c in range(3):
            block = w_ref[:, t, :, c * el : (c + 1) * el]
            wf[:, c * d + t * el : c * d + (t + 1) * el] = block.reshape(d, el)
    for c, out in enumerate((q, k, v)):
        raw[...] = dot(n1[...], wf[:, c * d : (c + 1) * d])

        def finish(at, c=c, out=out):
            for j in range(0, d, 128):
                value = raw[at, j : j + 128]
                if c < 2:
                    value = turned(value, cos[at, :], sin[at, :])
                out[at, j : j + 128] = value.astype(BF)

        rows_loop(hid.shape[0], 64, finish)


def call(kernel, outs, scratch, *args, name):
    vm = pl.BlockSpec(memory_space=VM)
    return pl.pallas_call(
        kernel,
        in_specs=[vm] * len(args),
        out_specs=[vm] * len(outs),
        out_shape=outs,
        scratch_shapes=scratch,
        compiler_params=pltpu.CompilerParams(vmem_limit_bytes=WIDE),
        name=name,
    )(*args)


def half_lanes(shape):
    return lax.broadcasted_iota(jnp.int32, shape, 1) < HD


def attend_kernel(q, k, k2, v, v2, augk, augq, mixed, lse):
    keys = jnp.concatenate([k[...], k2[...]], axis=0)
    vt = jnp.concatenate([v[...], v2[...]], axis=0).T
    qt = q[...].T
    low = half_lanes(keys.shape)
    ones = jnp.ones((HD, vt.shape[1]), BF)
    outs = []
    for h in range(2):
        if h == 0:
            keys_h = jnp.where(low, keys, augk[...])
            q_h = jnp.concatenate([qt[:HD], augq[...]], axis=0)
            v_h = jnp.concatenate([vt[:HD], ones], axis=0)
        else:
            keys_h = jnp.where(low, augk[...], keys)
            q_h = jnp.concatenate([augq[...], qt[HD:]], axis=0)
            v_h = jnp.concatenate([ones, vt[HD:]], axis=0)
        scores = dot(keys_h, q_h)
        top = jnp.max(scores, axis=0, keepdims=True)
        expo = jnp.exp2((scores - top) * TO_EXP2).astype(BF)
        got = dot(v_h, expo)
        value, total = (got[:HD], got[HD:]) if h == 0 else (got[HD:], got[:HD])
        outs.append(value / total)
        lse[0, h : h + 1, :] = top + jnp.log2(total[:1]) * (1.0 / TO_EXP2)
    mixed[...] = jnp.concatenate(outs, axis=0).T.astype(BF)


def split_rows(value, n, rows):
    parts = []
    for _ in range(n):
        part = value.astype(BF).astype(F32)
        parts.append(part)
        value = value - part
    parts.append(jnp.zeros((rows - n, value.shape[1]), F32))
    return jnp.concatenate(parts, axis=0).astype(BF)


def attend_back_kernel(q, k, k2, v, v2, g, mixed, lse, augk, augq, gq, gk, gk2, gv, gv2):
    rows = q.shape[0]
    gt, qt, mt = g[...].T, q[...].T, mixed[...].T
    grads, query = g[...], q[...]
    prod = gt.astype(F32) * mt.astype(F32)
    tall = (2, rows)
    gq_parts = []
    sides = [(k, v, gk, gv), (k2, v2, gk2, gv2)]
    low = half_lanes((rows, 2 * HD))
    one = jnp.ones((rows, 2 * HD), BF)
    held = {}
    for h in range(2):
        mine = slice(h * HD, (h + 1) * HD)
        inner = jnp.sum(prod[mine], axis=0, keepdims=True)
        neg = split_rows(-lse[0, h : h + 1, :], 3, 2 * SEGS - SEGS)
        extra_q = jnp.concatenate([augq[:SEGS], neg, augq[2 * SEGS :]], axis=0)
        extra_g = jnp.concatenate([split_rows(-inner, 2, 8), jnp.zeros((HD - 8, rows), BF)], axis=0)
        order = (lambda a, b: jnp.concatenate([a, b], axis=0)) if h == 0 else (lambda a, b: jnp.concatenate([b, a], axis=0))
        q_h, g_h = order(qt[mine], extra_q), order(gt[mine], extra_g)
        gq_h = None
        for s, (kr, vr, _, _) in enumerate(sides):
            aug = augk[s * rows : (s + 1) * rows, :]
            keys, values = kr[...], vr[...]
            pick = (lambda a, b: jnp.where(low, a, b)) if h == 0 else (lambda a, b: jnp.where(low, b, a))
            probs = jnp.exp2(dot(pick(keys, aug), q_h) * TO_EXP2)
            grad_p = dot(pick(values, one), g_h)
            held[h, s, "v"] = dot(probs.astype(BF), grads)
            ds = (probs * grad_p).astype(BF)
            held[h, s, "k"] = dot(ds, query)
            part = dot(keys.T[mine], ds)
            gq_h = part if gq_h is None else gq_h + part
        gq_parts.append(gq_h)
    scale = 1.0 / math.sqrt(HD)
    gq[...] = jnp.concatenate(gq_parts, axis=0).T * scale
    for s, (_, _, gkr, gvr) in enumerate(sides):
        gkr[...] = (jnp.where(low, held[0, s, "k"], held[1, s, "k"]) * scale).astype(gkr.dtype)
        gvr[...] = jnp.where(low, held[0, s, "v"], held[1, s, "v"]).astype(gvr.dtype)


def attention(kernel, args, lse, augk, augq, outs, lse_out):
    rows, d = args[0].shape
    pairs = d // (2 * HD)
    sds = jax.ShapeDtypeStruct
    block = pl.BlockSpec((rows, 2 * HD), lambda i: (0, i))
    lse_block = pl.BlockSpec((1, 2, rows), lambda i: (i, 0, 0))
    fixed = lambda a: pl.BlockSpec(a.shape, lambda i: (0, 0))
    out_shape = [sds((rows, d), dtype) for dtype in outs]
    out_specs = [block] * len(outs)
    if lse_out:
        out_shape.append(sds((pairs, 2, rows), F32))
        out_specs.append(lse_block)
    lses = [] if lse is None else [lse]
    return pl.pallas_call(
        kernel,
        grid=(pairs,),
        in_specs=[block] * len(args) + [lse_block] * len(lses) + [fixed(augk), fixed(augq)],
        out_specs=out_specs,
        out_shape=out_shape,
        compiler_params=pltpu.CompilerParams(vmem_limit_bytes=WIDE),
        name="attend" if lse_out else "attend_back",
    )(*args, *lses, augk, augq)


def middle_kernel(
    nt, hid, mixed, cot, gain, w_ref,
    out, gmixed, gres, gain_o, g2,
    wi, wo, wd, gate, up, gp, prod, gg, gu, n2, low, gtot,
):
    n, d = hid.shape
    ff = wd.shape[1]
    el, fl = d // nt, ff // nt
    two, three = 2 * fl, 2 * fl + el
    for t in range(nt):
        at = slice(t * fl, (t + 1) * fl)
        wi[0, :, at] = w_ref[:, t, :, :fl].reshape(d, fl)
        wi[1, :, at] = w_ref[:, t, :, fl:two].reshape(d, fl)
        wo[:, t * el : (t + 1) * el] = w_ref[:, t, :, two:three].reshape(d, el)
        wd[:, at] = w_ref[:, t, :, three:].reshape(d, fl)
    gres[...] = dot(mixed[...], wo[...], NT)

    def norm(at):
        value = hid[at, :].astype(F32) + gres[at, :]
        gres[at, :] = value
        xhat, _ = standard(value)
        n2[at, :] = (xhat * gain[...]).astype(BF)

    rows_loop(n, 64, norm)
    gate[...] = dot(n2[...], wi[0])
    up[...] = dot(n2[...], wi[1])
    gp[...] = dot(cot[...], wd[...])

    def geglu(at):
        for j in range(0, ff, 384):
            to = slice(j, j + 384)
            g, u, p = gate[at, to], up[at, to], gp[at, to]
            cdf = 0.5 + 0.5 * erf(g * math.sqrt(0.5))
            pdf = jnp.exp(-0.5 * g * g) * (1.0 / math.sqrt(2 * math.pi))
            act = g * cdf
            prod[at, to] = (act * u).astype(BF)
            gg[at, to] = (p * u * (cdf + g * pdf)).astype(BF)
            gu[at, to] = (p * act).astype(BF)

    rows_loop(n, 32, geglu)
    out[...] = (gres[...] + dot(prod[...], wd[...], NT)).astype(BF)
    gtot[...] = dot(gg[...], wi[0], NT) + dot(gu[...], wi[1], NT)
    gain_o[...] = jnp.zeros_like(gain_o)

    def back(at):
        xhat, scale = standard(gres[at, :])
        e = gtot[at, :]
        part = e * xhat
        gain_o[...] += jnp.sum(part.reshape(-1, 8, d), axis=0)
        total = cot[at, :].astype(F32) + norm_back(e, xhat, scale, gain[...])
        gres[at, :] = total
        low[at, :] = total.astype(BF)

    rows_loop(n, 64, back)
    gmixed[...] = dot(low[...], wo[...]).astype(BF)
    split = (8, d // 8)
    n2t = n2[...].T
    for t in range(nt):
        at = slice(t * fl, (t + 1) * fl)
        g2[:, t, :, :fl] = dot(n2t, gg[:, at]).astype(BF).reshape(*split, fl)
        g2[:, t, :, fl:two] = dot(n2t, gu[:, at]).astype(BF).reshape(*split, fl)
    lowt = low[...].T
    for t in range(nt):
        at = slice(t * el, (t + 1) * el)
        g2[:, t, :, two:three] = dot(lowt, mixed[:, at]).astype(BF).reshape(*split, el)
    cott = cot[...].T
    for t in range(nt):
        at = slice(t * fl, (t + 1) * fl)
        g2[:, t, :, three:] = dot(cott, prod[:, at]).astype(BF).reshape(*split, fl)


def last_kernel(
    nt, hid, gres, gain, gain_two, wf, n1, cos, sin, gq, gk, gv, ak, av,
    gin, g1,
    raw, gtot, gsum,
):
    n, d = hid.shape
    el = d // nt

    def back(at):
        c, s = cos[at, :], -sin[at, :]
        for j in range(0, d, 128):
            to = slice(j, j + 128)
            raw[at, j : j + 128] = turned(gq[at, to], c, s).astype(BF)
            keys = gk[at, to] + ak[at, to].astype(F32)
            raw[at, d + j : d + j + 128] = turned(keys, c, s).astype(BF)
            raw[at, 2 * d + j : 2 * d + j + 128] = (gv[at, to] + av[at, to].astype(F32)).astype(BF)

    rows_loop(n, 32, back)
    gtot[...] = dot(raw[...], wf[...], NT)
    gsum[...] = jnp.zeros_like(gsum)

    def norm(at):
        xhat, scale = standard(hid[at, :].astype(F32))
        e = gtot[at, :]
        gsum[...] += jnp.sum((e * xhat).reshape(-1, 8, d), axis=0)
        gin[at, :] = (gres[at, :] + norm_back(e, xhat, scale, gain[...])).astype(BF)

    rows_loop(n, 64, norm)
    n1t = n1[...].T
    for t in range(nt):
        for c in range(3):
            cols = raw[:, c * d + t * el : c * d + (t + 1) * el]
            g1[:, t, :, c * el : (c + 1) * el] = dot(n1t, cols).astype(BF).reshape(8, d // 8, el)
    rows = []
    for v in (gsum[...], gain_two[...]):
        total = jnp.sum(v, axis=0, keepdims=True)
        upper = total.astype(BF).astype(F32)
        rows += [upper, total - upper]
    rows.append(jnp.zeros((SPARE - 4, d), F32))
    gains = jnp.concatenate(rows, axis=0).T.astype(BF).reshape(8, d // 8, SPARE)
    for t in range(nt):
        g1[:, t, :, 3 * el :] = gains


def shards(hidden_in, cotangent, segment_ids, w_qkv, w_out, w_in, w_down, norm_gains):
    ndp, nt = lax.axis_size("dp"), lax.axis_size("tensor")
    stride = ndp // 8
    core = lax.axis_index("dp") % 2
    place = lax.axis_index("tensor")
    rows, local_len, d = hidden_in.shape
    half = local_len // 2
    tokens = nt * half
    ff = w_in.shape[2] * nt
    sds = jax.ShapeDtypeStruct
    low_groups = [[h * stride + i for i in range(stride)] for h in range(8)]

    def swap(v):
        return lax.ppermute(v, "dp", [(i, i ^ 1) for i in range(ndp)])

    dl, el, fl = w_qkv.shape[1], w_qkv.shape[2], w_in.shape[2]

    def flat(v):
        return jnp.transpose(v, (1, 0, 2)).reshape(dl, -1)

    def widen(v):
        if stride == 1:
            return v
        return lax.all_gather(v, "dp", axis_index_groups=low_groups, tiled=True)

    def narrow(v):
        if stride == 1:
            return v
        return lax.psum_scatter(v, "dp", axis_index_groups=low_groups, tiled=True)

    gains_t = jnp.pad(norm_gains.T, ((0, 0), (0, SPARE - 2)))
    w1 = widen(jnp.concatenate([flat(w_qkv), gains_t], axis=1))
    w2 = widen(jnp.concatenate([flat(w_in), w_out.T, w_down.T], axis=1))
    split = lambda v: v.reshape(2, 2, half, d)
    all_one, all_two, hid, cot, seg_other = gather_all(
        ndp, nt, w1, w2, split(hidden_in), split(cotangent), segment_ids
    )
    hid, cot = hid.reshape(tokens, d), cot.reshape(tokens, d)
    all_one = all_one.reshape((8, nt) + w1.shape)
    all_two = all_two.reshape((8, nt) + w2.shape)
    gains = all_one[:, 0, :, 3 * el : 3 * el + 2].reshape(d, 2).T.astype(F32)
    gain_one, gain_two = gains[:1], gains[1:]

    mine = place // 2 == core
    row_of = lambda v: lax.dynamic_index_in_dim(v, place % 2, 0, keepdims=False)
    row = jnp.where(mine, row_of(segment_ids), row_of(seg_other))
    by_core = row.reshape(nt, 2, half)
    pick = lambda c: lax.dynamic_index_in_dim(by_core, c, 1, keepdims=False).reshape(tokens)
    seg_q = pick(core)
    seg_k = jnp.concatenate([seg_q, pick(1 - core)])
    spot = jnp.arange(tokens, dtype=jnp.int32)
    spot = spot // half * local_len + core * half + spot % half
    first = jnp.sum((row[None, :] < seg_q[:, None]).astype(jnp.int32), axis=1)
    position = (spot - first).astype(F32)
    lane = jnp.arange(HD // 2, dtype=F32)
    angle = position[:, None] * THETA ** (-2.0 * lane / HD)
    c, s = jnp.cos(angle), jnp.sin(angle)
    cosine = jnp.concatenate([c, c, c, c], axis=1)
    sine = jnp.concatenate([-s, s, -s, s], axis=1)
    ids = jnp.arange(HD, dtype=jnp.int32)
    hot = (seg_k[:, None] == ids) | ((ids >= SEGS) & (ids < SEGS + 3))
    augk = jnp.tile(hot.astype(BF), (1, 2))
    augq = jnp.where((ids[:, None] < SEGS) & (seg_q[None, :] != ids[:, None]), -BIG, 0.0).astype(BF)

    act = sds((tokens, d), BF)
    act32 = sds((tokens, d), F32)
    q, k, v, n1, wf = call(
        functools.partial(project_kernel, nt),
        [act, act, act, act, sds((d, 3 * d), BF)],
        [VM((tokens, d), F32)],
        hid, gain_one, all_one, cosine, sine,
        name="project",
    )
    k2, v2 = swap(k), swap(v)
    mixed, lse = attention(attend_kernel, (q, k, k2, v, v2), None, augk, augq, (BF,), True)
    wide = lambda dtype: VM((tokens, ff), dtype)
    out, gmixed, gres, gain_two_part, g2 = call(
        functools.partial(middle_kernel, nt),
        [act, act, act32, sds((8, d), F32), sds(all_two.shape, BF)],
        [
            VM((2, d, ff), BF), VM((d, d), BF), VM((d, ff), BF),
            wide(F32), wide(F32), wide(F32), wide(BF), wide(BF), wide(BF),
            VM((tokens, d), BF), VM((tokens, d), BF), VM((tokens, d), F32),
        ],
        hid, mixed, cot, gain_two, all_two,
        name="middle",
    )
    second, layer_out = scatter_all(
        ndp, nt, g2.reshape((2, 2, 2, nt) + w2.shape), out.reshape(nt, half, d), 1
    )
    gq, gk, gk2, gv, gv2 = attention(
        attend_back_kernel, (q, k, k2, v, v2, gmixed, mixed), lse, augk, augq, (F32, F32, BF, F32, BF), False
    )
    ak, av = swap(gk2), swap(gv2)
    gin, g1 = call(
        functools.partial(last_kernel, nt),
        [act, sds(all_one.shape, BF)],
        [VM((tokens, 3 * d), BF), VM((tokens, d), F32), VM((8, d), F32)],
        hid, gres, gain_one, gain_two_part, wf, n1, cosine, sine, gq, gk, gv, ak, av,
        name="last",
    )
    one, grad_input = scatter_all(
        ndp, nt, g1.reshape((2, 2, 2, nt) + w1.shape), gin.reshape(nt, half, d), 2
    )
    one, second = narrow(one), narrow(second)
    back = lambda t: t.reshape(rows, local_len, d)

    def stacked(t, n, cols):
        return jnp.transpose(t.reshape(dl, n, cols), (1, 0, 2))

    two, three = 2 * fl, 2 * fl + el
    tail = one[:, 3 * el :]
    grad_gains = jnp.stack([tail[:, 0] + tail[:, 1], tail[:, 2] + tail[:, 3]])
    return (
        back(layer_out),
        back(grad_input),
        stacked(one[:, : 3 * el], 3, el),
        second[:, two:three].T,
        stacked(second[:, :two], 2, fl),
        second[:, three:].T,
        grad_gains,
    )


def solution(mesh):
    placed = (
        P("dp", "tensor", None),
        P("dp", "tensor", None),
        P("dp", None),
        P(None, "dp", "tensor"),
        P("tensor", "dp"),
        P(None, "dp", "tensor"),
        P("tensor", "dp"),
        P(None, "dp"),
    )
    return jax.shard_map(
        shards,
        mesh=mesh,
        in_specs=placed,
        out_specs=(
            P("dp", "tensor", None),
            P("dp", "tensor", None),
            P(None, "dp", "tensor"),
            P("tensor", "dp"),
            P(None, "dp", "tensor"),
            P("tensor", "dp"),
            P(None, "dp"),
        ),
        check_vma=False,
    )
```

```python
import functools
import math

import jax
import jax.numpy as jnp
from jax import lax
from jax.experimental import pallas as pl
from jax.experimental.pallas import tpu as pltpu
from jax.sharding import PartitionSpec as P

HD = 64
EPS = 1e-05
THETA = 160000.0
BIG = 1e30
SEGS = 8
SPARE = 8
TO_EXP2 = math.log2(math.e) / math.sqrt(HD)
MESH = pl.DeviceIdType.MESH
BF, F32 = jnp.bfloat16, jnp.float32
VM = pltpu.VMEM
WIDE = 60 * 1024 * 1024


def dot(a, b, dims=((1,), (0,))):
    return lax.dot_general(a, b, (dims, ((), ())), preferred_element_type=F32)


NT = ((1,), (1,))


def erf(x):
    x = jnp.clip(x, -3.832506856900711, 3.832506856900711)
    s = x * x
    p = 0.00022905065861350646
    for c in (0.0034082910107109506, 0.050955695062380861, 0.18520832239976145, 1.128379143519084):
        p = p * s + c
    q = -1.1791602954361697e-7
    for c in (
        0.000023547966471313185,
        0.0010179625278914885,
        0.014070470171167667,
        0.11098505178285362,
        0.49746925110067538,
        1.0,
    ):
        q = q * s + c
    return x * p / q


class Place:
    def __init__(self, ndp, nt):
        self.nt = nt
        self.stride = ndp // 8
        self.dp, self.z = lax.axis_index("dp"), lax.axis_index("tensor")
        high = self.dp // self.stride
        self.b = (high % 2, (high // 2) % 2, high // 4)
        self.core = self.dp % 2

    def flip(self, bit):
        return (self.dp + (1 - 2 * self.b[bit]) * self.stride * 2**bit, self.z)

    def along(self, step):
        return (self.dp, (self.z + step) % self.nt)

    def pair(self, core, z):
        return (self.dp - self.core + core, z)

    def barrier(self, group):
        others = [self.along(s) for s in range(1, self.nt)]
        others += [self.flip(1), self.flip(2)]
        if group or self.stride == 1:
            others += [self.pair(1 - self.core, self.z)]
        if self.stride > 1:
            others += [self.flip(0)]
        if group:
            others += [self.pair(1 - self.core, (self.z + s) % self.nt) for s in range(1, self.nt)]
        sem = pltpu.get_barrier_semaphore()
        for device in others:
            pl.semaphore_signal(sem, inc=1, device_id=device, device_id_type=MESH)
        pl.semaphore_wait(sem, len(others))


def remote(src, dst, send, recv, device):
    return pltpu.make_async_remote_copy(
        src_ref=src, dst_ref=dst, send_sem=send, recv_sem=recv, device_id=device, device_id_type=MESH
    )


def enter_copies(me, src, dst, send, recv):
    starts, ends = [], []
    half = src.shape[2]
    slot = lambda z: dst.at[pl.ds(pl.multiple_of(z * half, half), half)]
    for row in range(2):
        for core in range(2):
            z = 2 * me.core + row
            k = 2 * row + core
            here = jnp.logical_and(z == me.z, core == me.core)
            copy = remote(src.at[row, core], slot(me.z), send.at[k], recv.at[me.z], me.pair(core, z))
            local = pltpu.make_async_copy(src.at[row, core], slot(me.z), recv.at[me.z])
            starts.append((here, copy, local))
    for z in range(me.nt):
        ends.append(remote(src.at[0, 0], slot(z), send.at[0], recv.at[z], me.pair(1 - me.core, z)))
    return starts, ends


def leave_copies(me, src, dst, send, recv):
    starts, ends = [], []
    for z in range(me.nt):
        here = jnp.logical_and(z == me.z, me.z // 2 == me.core)
        k = 2 * (me.z % 2) + me.core
        to = dst.at[me.z % 2, me.core]
        copy = remote(src.at[z], to, send.at[z], recv.at[k], me.pair(me.z // 2, z))
        local = pltpu.make_async_copy(src.at[z], to, recv.at[k])
        starts.append((here, copy, local))
    for k in range(4):
        ends.append(remote(src.at[0], dst.at[k // 2, k % 2], send.at[0], recv.at[k], me.pair(1 - me.core, me.z)))
    return starts, ends


def start_all(starts):
    for here, copy, local in starts:
        pl.when(here)(local.start)
        pl.when(jnp.logical_not(here))(copy.start)


def wait_sends(starts):
    for here, copy, _ in starts:
        pl.when(jnp.logical_not(here))(copy.wait_send)


class Gather:
    COPIES = 12

    def __init__(self, me, shard, out, send, recv, own):
        self.me, self.shard, self.out, self.own = me, shard, out, own
        b0, b1, b2 = me.b
        nt, h = me.nt, me.nt // 2
        lo, hi, both = pl.ds(0, h), pl.ds(h, h), pl.ds(0, 2)

        def pair(k, at, other, device):
            cp = remote(out.at[at], out.at[at], send.at[k], recv.at[k], device)
            back = remote(out.at[other], out.at[other], send.at[k], recv.at[k], device)
            return cp, back

        n = nt - 1
        self.z = []
        for s in range(1, nt):
            at = (b2, b1, b0, me.z)
            frm = (b2, b1, b0, (me.z + nt - s) % nt)
            cp = remote(shard, out.at[at], send.at[s - 1], recv.at[s - 1], me.along(s))
            back = remote(shard, out.at[frm], send.at[s - 1], recv.at[s - 1], me.along(s))
            self.z.append((cp, back))
        x, y, core = me.flip(1), me.flip(2), me.flip(0)
        o0, o1, o2 = 1 - b0, 1 - b1, 1 - b2
        self.one = [
            pair(n, (b2, b1, b0, lo), (b2, o1, b0, lo), x),
            pair(n + 1, (b2, b1, b0, hi), (o2, b1, b0, hi), y),
        ]
        self.two = [
            pair(n + 2, (b2, both, b0, lo), (o2, both, b0, lo), y),
            pair(n + 3, (both, b1, b0, hi), (both, o1, b0, hi), x),
        ]
        self.core_a = [pair(n + 4, (b2, b1, b0), (b2, b1, o0), core)]
        self.core_b = [
            pair(n + 5, (b2, o1, b0, lo), (b2, o1, o0, lo), core),
            pair(n + 6, (o2, b1, b0, hi), (o2, b1, o0, hi), core),
        ]
        self.core_c = [
            pair(n + 7, (o2, both, b0, lo), (o2, both, o0, lo), core),
            pair(n + 8, (both, o1, b0, hi), (both, o1, o0, hi), core),
        ]

    def start_z(self):
        b0, b1, b2 = self.me.b
        self.mine = pltpu.make_async_copy(self.shard, self.out.at[b2, b1, b0, self.me.z], self.own)
        self.mine.start()
        for cp, _ in self.z:
            cp.start()

    @staticmethod
    def start(copies):
        for cp, _ in copies:
            cp.start()

    @staticmethod
    def landed(copies):
        for _, back in copies:
            back.wait_recv()

    def after_z(self):
        self.mine.wait()
        self.landed(self.z)
        self.start(self.one + self.core_a)

    def after_one(self):
        self.landed(self.one)
        self.start(self.two + self.core_b)

    def after_two(self):
        self.landed(self.two)
        self.start(self.core_c)

    def finish(self):
        for group in (self.core_a, self.core_b, self.core_c):
            self.landed(group)
        for group in (self.z, self.one, self.two, self.core_a, self.core_b, self.core_c):
            for cp, _ in group:
                cp.wait_send()


class Scatter:
    COPIES = 9

    def __init__(self, me, g, out, bufs, send, recv):
        self.me, self.g, self.out = me, g, out
        self.r0, self.s0, self.r1, self.s1, self.r2, self.s2, self.rz = bufs
        b0, b1, b2 = me.b
        o0, o1, o2 = 1 - b0, 1 - b1, 1 - b2
        h, nt = me.nt // 2, me.nt
        both = pl.ds(0, 2)
        x, y, core = me.flip(1), me.flip(2), me.flip(0)
        part = (pl.ds(0, h), pl.ds(h, h))

        def copy(k, src, dst, device):
            return remote(src, dst, send.at[k], recv.at[k], device)

        self.core = [
            copy(i, g.at[both, both, o0, part[i]], self.r0.at[i], core) for i in range(2)
        ]
        self.one = [
            copy(2, self.s0.at[0, both, o1], self.r1.at[0], x),
            copy(3, self.s0.at[1, o2], self.r1.at[1], y),
        ]
        self.two = [
            copy(4, self.s1.at[0, o2], self.r2.at[0], y),
            copy(5, self.s1.at[1, o1], self.r2.at[1], x),
        ]
        self.z = [
            copy(5 + s, self.s2.at[(me.z + s) % nt], self.rz.at[s - 1], me.along(s)) for s in range(1, nt)
        ]

    def begin(self):
        for cp in self.core:
            cp.start()

    def add_core(self, i):
        b0 = self.me.b[0]
        h = self.me.nt // 2
        self.core[i].wait_recv()
        for a in range(2):
            for b in range(2):
                for t in range(h):
                    total = self.g[a, b, b0, i * h + t].astype(F32) + self.r0[i, a, b, t].astype(F32)
                    self.s0[i, a, b, t] = total.astype(BF)
        self.one[i].start()

    def add_one(self, i):
        _, b1, b2 = self.me.b
        self.one[i].wait_recv()
        for a in range(2):
            for t in range(self.me.nt // 2):
                mine = self.s0[0, a, b1, t] if i == 0 else self.s0[1, b2, a, t]
                self.s1[i, a, t] = (mine.astype(F32) + self.r1[i, a, t].astype(F32)).astype(BF)
        self.two[i].start()

    def add_two(self, i):
        _, b1, b2 = self.me.b
        h = self.me.nt // 2
        self.two[i].wait_recv()
        own = b2 if i == 0 else b1
        for t in range(h):
            total = self.s1[i, own, t].astype(F32) + self.r2[i, t].astype(F32)
            self.s2[i * h + t] = total.astype(BF)

    def send_z(self):
        for cp in self.z:
            cp.start()

    def finish(self):
        total = self.s2[self.me.z].astype(F32)
        for s in range(self.me.nt - 1):
            self.z[s].wait_recv()
            total = total + self.rz[s].astype(F32)
        self.out[...] = total
        for cp in self.core + self.one + self.two + self.z:
            cp.wait_send()


def scatter_scratch(nt, r, c):
    h = nt // 2
    dma = pltpu.SemaphoreType.DMA
    return [
        VM((2, 2, 2, h, r, c), BF),
        VM((2, 2, 2, h, r, c), BF),
        VM((2, 2, h, r, c), BF),
        VM((2, 2, h, r, c), BF),
        VM((2, h, r, c), BF),
        VM((nt, r, c), BF),
        VM((nt - 1, r, c), BF),
        dma((6 + nt - 1,)),
        dma((6 + nt - 1,)),
    ]


def scatter_kernel(ndp, nt, g, act, out, act_o, *scratch):
    bufs, (send, recv, sl, rl) = scratch[:7], scratch[7:]
    me = Place(ndp, nt)
    me.barrier(True)
    rs = Scatter(me, g, out, bufs, send, recv)
    rs.begin()
    ls, le = leave_copies(me, act, act_o, sl, rl)
    start_all(ls)
    for i in range(2):
        rs.add_core(i)
    for i in range(2):
        rs.add_one(i)
    for i in range(2):
        rs.add_two(i)
    rs.send_z()
    rs.finish()
    for e in le:
        e.wait_recv()
    wait_sends(ls)


def scatter_all(ndp, nt, g, act, ident):
    r, c = g.shape[4:]
    sds = jax.ShapeDtypeStruct
    half, width = act.shape[1:]
    dma = pltpu.SemaphoreType.DMA
    vm = pl.BlockSpec(memory_space=VM)
    hbm = pl.BlockSpec(memory_space=pl.ANY)
    return pl.pallas_call(
        functools.partial(scatter_kernel, ndp, nt),
        in_specs=[vm, hbm],
        out_specs=[vm, hbm],
        out_shape=[sds((r, c), F32), sds((2, 2, half, width), BF)],
        scratch_shapes=scatter_scratch(nt, r, c) + [dma((4,)), dma((4,))],
        compiler_params=pltpu.CompilerParams(
            collective_id=ident, has_side_effects=True, vmem_limit_bytes=WIDE
        ),
        name=f"scatter_{ident}",
    )(g, act)


def standard(v):
    centred = v - jnp.mean(v, axis=-1, keepdims=True)
    scale = lax.rsqrt(jnp.mean(centred * centred, axis=-1, keepdims=True) + EPS)
    return centred * scale, scale


def norm_back(grad, xhat, scale, gain):
    e = grad * gain
    inner = jnp.mean(e * xhat, axis=-1, keepdims=True)
    return scale * (e - jnp.mean(e, axis=-1, keepdims=True) - xhat * inner)


def rows_loop(total, step, body):
    def run(i, carry):
        body(pl.ds(pl.multiple_of(i * step, step), step))
        return carry

    lax.fori_loop(0, total // step, run, 0)


def turned(v, cosine, sine):
    lane = lax.broadcasted_iota(jnp.int32, v.shape, 1)
    other = jnp.where(lane % HD < HD // 2, pltpu.roll(v, 128 - HD // 2, 1), pltpu.roll(v, HD // 2, 1))
    return v * cosine + other * sine


def call(kernel, outs, scratch, *args, name):
    vm = pl.BlockSpec(memory_space=VM)
    return pl.pallas_call(
        kernel,
        in_specs=[vm] * len(args),
        out_specs=[vm] * len(outs),
        out_shape=outs,
        scratch_shapes=scratch,
        compiler_params=pltpu.CompilerParams(vmem_limit_bytes=WIDE),
        name=name,
    )(*args)


def half_lanes(shape):
    return lax.broadcasted_iota(jnp.int32, shape, 1) < HD


def attend_pair(i, q, k, k2, v, v2, augk, augq, mixed, lse):
    at = pl.ds(pl.multiple_of(i * 2 * HD, 2 * HD), 2 * HD)
    keys = jnp.concatenate([k[:, at], k2[:, at]], axis=0)
    vt = jnp.concatenate([v[:, at], v2[:, at]], axis=0).T
    qt = q[:, at].T
    low = half_lanes(keys.shape)
    ones = jnp.ones((HD, vt.shape[1]), BF)
    outs = []
    for h in range(2):
        if h == 0:
            keys_h = jnp.where(low, keys, augk[...])
            q_h = jnp.concatenate([qt[:HD], augq[...]], axis=0)
            v_h = jnp.concatenate([vt[:HD], ones], axis=0)
        else:
            keys_h = jnp.where(low, augk[...], keys)
            q_h = jnp.concatenate([augq[...], qt[HD:]], axis=0)
            v_h = jnp.concatenate([ones, vt[HD:]], axis=0)
        scores = dot(keys_h, q_h)
        top = jnp.max(scores, axis=0, keepdims=True)
        expo = jnp.exp2((scores - top) * TO_EXP2).astype(BF)
        got = dot(v_h, expo)
        value, total = (got[:HD], got[HD:]) if h == 0 else (got[HD:], got[:HD])
        outs.append(value / total)
        lse[i, h : h + 1, :] = top + jnp.log2(total[:1]) * (1.0 / TO_EXP2)
    mixed[:, at] = jnp.concatenate(outs, axis=0).T.astype(BF)


def column(row):
    return jnp.concatenate([row] * 8, axis=0).T[:, :1]


def masks(me, row, half, freq, cos, sin, augk, augq):
    n = me.nt * half
    part = lambda core: jnp.concatenate(
        [row[:, (2 * z + core) * half : (2 * z + core + 1) * half] for z in range(me.nt)], axis=1
    ).astype(F32)
    even, odd = part(0), part(1)
    seg_q, seg_o = jnp.where(me.core == 0, even, odd), jnp.where(me.core == 0, odd, even)
    whole = jnp.concatenate([seg_q, seg_o], axis=1)
    mine = column(seg_q)
    spot = lax.broadcasted_iota(jnp.int32, (n, 1), 0)
    spot = spot + (spot // half) * half + me.core * half
    first = jnp.zeros((n, 1), F32)
    for s in range(SEGS - 2):
        count = jnp.sum((whole == s).astype(F32), axis=1, keepdims=True)
        first = first + jnp.where(mine > s, count, 0.0)
    angle = (spot.astype(F32) - first) * freq[...]
    cos[...] = jnp.cos(angle)
    sines = jnp.sin(angle)
    lane = lax.broadcasted_iota(jnp.int32, sines.shape, 1)
    sin[...] = jnp.where(lane % HD < HD // 2, -sines, sines)
    for s, seg in enumerate((mine, column(seg_o))):
        ids = lax.broadcasted_iota(jnp.int32, (n, 2 * HD), 1) % HD
        hot = jnp.logical_or(seg == ids.astype(F32), jnp.logical_and(ids >= SEGS, ids < SEGS + 3))
        augk[s * n : (s + 1) * n, :] = jnp.where(hot, 1.0, 0.0).astype(BF)
    ids = lax.broadcasted_iota(jnp.int32, (HD, n), 0)
    off = jnp.logical_and(ids < SEGS, seg_q != ids.astype(F32))
    augq[...] = jnp.where(off, -BIG, 0.0).astype(BF)


def front_kernel(
    ndp, nt,
    w_qkv, w_out, w_in, w_down, gains_in, hid_in, cot_in, seg, freq,
    hid, cot, all_two, q, k, v, k2, v2, n1, wf, mixed, lse, cos, sin, augk, augq, gains,
    w1, w2, all_one, seg_o, raw, s1, r1, s2, r2, own, se, re, sc, rc, ss,
):
    n, d = hid.shape
    el, fl = w_qkv.shape[2], w_in.shape[2]
    r = w_qkv.shape[1]
    half = n // nt
    me = Place(ndp, nt)
    me.barrier(True)
    first = Gather(me, w1, all_one, s1, r1, own.at[0])
    second = Gather(me, w2, all_two, s2, r2, own.at[1])
    hs, he = enter_copies(me, hid_in, hid, se, re)
    cs, ce = enter_copies(me, cot_in, cot, sc, rc)
    buddy = me.pair(1 - me.core, me.z)
    swap = remote(seg, seg_o, ss.at[0], ss.at[3], buddy)
    swap.start()
    for c in range(3):
        w1[:, c * el : (c + 1) * el] = w_qkv[c]
    cols = jnp.concatenate([gains_in[...].astype(F32), jnp.zeros((SPARE - 2, r), F32)], axis=0)
    w1[:, 3 * el :] = cols.T.astype(BF)
    first.start_z()
    start_all(hs)
    two, three = 2 * fl, 2 * fl + el
    w2[:, :fl] = w_in[0]
    w2[:, fl:two] = w_in[1]
    w2[:, two:three] = w_out[...].astype(F32).T.astype(BF)
    w2[:, three:] = w_down[...].astype(F32).T.astype(BF)
    first.after_z()
    second.start_z()
    swap.wait()
    here = me.z // 2 == me.core
    index = me.z % 2
    both = jnp.where(here, seg[...], seg_o[...])
    row = jnp.where(index == 0, both[:1], both[1:2])
    masks(me, row, half, freq, cos, sin, augk, augq)
    first.after_one()
    for e in he:
        e.wait_recv()

    def spread(at):
        raw[at, :] = standard(hid[at, :].astype(F32))[0]

    rows_loop(n, 64, spread)
    first.after_two()
    first.finish()
    top = all_one[:, :, :, 0, :, 3 * el :].reshape(d, SPARE).astype(F32).T
    gains[...] = top
    gain = top[:1]

    def norm(at):
        n1[at, :] = (raw[at, :] * gain).astype(BF)

    rows_loop(n, 64, norm)
    for t in range(nt):
        for c in range(3):
            block = all_one[:, :, :, t, :, c * el : (c + 1) * el]
            wf[:, c * d + t * el : c * d + (t + 1) * el] = block.reshape(d, el)
    swaps = [remote(k, k2, ss.at[1], ss.at[4], buddy), remote(v, v2, ss.at[2], ss.at[5], buddy)]
    for c, out in ((1, k), (2, v), (0, q)):
        raw[...] = dot(n1[...], wf[:, c * d : (c + 1) * d])

        def finish(at, c=c, out=out):
            for j in range(0, d, 128):
                value = raw[at, j : j + 128]
                if c < 2:
                    value = turned(value, cos[at, :], sin[at, :])
                out[at, j : j + 128] = value.astype(BF)

        rows_loop(n, 64, finish)
        if c:
            swaps[c - 1].start()
    second.after_z()
    start_all(cs)
    for s in swaps:
        s.wait()
    pairs = d // (2 * HD)

    def attend(begin, end):
        def step(i, carry):
            attend_pair(i, q, k, k2, v, v2, augk, augq, mixed, lse)
            return carry

        lax.fori_loop(begin, end, step, 0)

    attend(0, pairs // 2)
    second.after_one()
    attend(pairs // 2, pairs)
    second.after_two()
    for e in ce:
        e.wait_recv()
    second.finish()
    wait_sends(hs)
    wait_sends(cs)


def front(ndp, nt, w_qkv, w_out, w_in, w_down, gains, hid, cot, seg):
    half, d = hid.shape[2:]
    n = nt * half
    r, el, fl = w_qkv.shape[1], w_qkv.shape[2], w_in.shape[2]
    c1, c2 = 3 * el + SPARE, 2 * fl + el + fl
    freq = jnp.tile(THETA ** (-2.0 * jnp.arange(HD // 2, dtype=F32) / HD), 4)[None]
    sds = jax.ShapeDtypeStruct
    dma = pltpu.SemaphoreType.DMA
    copies = Gather.COPIES
    vm, hbm = pl.BlockSpec(memory_space=VM), pl.BlockSpec(memory_space=pl.ANY)
    act = sds((n, d), BF)
    return pl.pallas_call(
        functools.partial(front_kernel, ndp, nt),
        in_specs=[vm] * 5 + [hbm] * 2 + [vm] * 2,
        out_specs=[vm, hbm, hbm] + [vm] * 14,
        out_shape=[act, act, sds((2, 2, 2, nt, r, c2), BF)]
        + [act] * 6
        + [sds((d, 3 * d), BF), act, sds((d // (2 * HD), 2, n), F32)]
        + [sds((n, 2 * HD), F32)] * 2
        + [sds((2 * n, 2 * HD), BF), sds((HD, n), BF), sds((SPARE, d), F32)],
        scratch_shapes=[
            VM((r, c1), BF),
            VM((r, c2), BF),
            VM((2, 2, 2, nt, r, c1), BF),
            VM(seg.shape, seg.dtype),
            VM((n, d), F32),
        ]
        + [dma((copies,))] * 4
        + [dma((2,))]
        + [dma((4,))] * 4
        + [dma((6,))],
        compiler_params=pltpu.CompilerParams(
            collective_id=0, has_side_effects=True, vmem_limit_bytes=WIDE
        ),
        name="front",
    )(w_qkv, w_out, w_in, w_down, gains, hid, cot, seg, freq)


def split_rows(value, n, rows):
    parts = []
    for _ in range(n):
        part = value.astype(BF).astype(F32)
        parts.append(part)
        value = value - part
    parts.append(jnp.zeros((rows - n, value.shape[1]), F32))
    return jnp.concatenate(parts, axis=0).astype(BF)


def attend_back_kernel(q, k, k2, v, v2, g, mixed, lse, augk, augq, gq, gk, gk2, gv, gv2):
    rows = q.shape[0]
    gt, qt, mt = g[...].T, q[...].T, mixed[...].T
    grads, query = g[...], q[...]
    prod = gt.astype(F32) * mt.astype(F32)
    tall = (2, rows)
    gq_parts = []
    sides = [(k, v, gk, gv), (k2, v2, gk2, gv2)]
    low = half_lanes((rows, 2 * HD))
    one = jnp.ones((rows, 2 * HD), BF)
    held = {}
    for h in range(2):
        mine = slice(h * HD, (h + 1) * HD)
        inner = jnp.sum(prod[mine], axis=0, keepdims=True)
        neg = split_rows(-lse[0, h : h + 1, :], 3, 2 * SEGS - SEGS)
        extra_q = jnp.concatenate([augq[:SEGS], neg, augq[2 * SEGS :]], axis=0)
        extra_g = jnp.concatenate([split_rows(-inner, 2, 8), jnp.zeros((HD - 8, rows), BF)], axis=0)
        order = (lambda a, b: jnp.concatenate([a, b], axis=0)) if h == 0 else (lambda a, b: jnp.concatenate([b, a], axis=0))
        q_h, g_h = order(qt[mine], extra_q), order(gt[mine], extra_g)
        gq_h = None
        for s, (kr, vr, _, _) in enumerate(sides):
            aug = augk[s * rows : (s + 1) * rows, :]
            keys, values = kr[...], vr[...]
            pick = (lambda a, b: jnp.where(low, a, b)) if h == 0 else (lambda a, b: jnp.where(low, b, a))
            probs = jnp.exp2(dot(pick(keys, aug), q_h) * TO_EXP2)
            grad_p = dot(pick(values, one), g_h)
            held[h, s, "v"] = dot(probs.astype(BF), grads)
            ds = (probs * grad_p).astype(BF)
            held[h, s, "k"] = dot(ds, query)
            part = dot(keys.T[mine], ds)
            gq_h = part if gq_h is None else gq_h + part
        gq_parts.append(gq_h)
    scale = 1.0 / math.sqrt(HD)
    gq[...] = jnp.concatenate(gq_parts, axis=0).T * scale
    for s, (_, _, gkr, gvr) in enumerate(sides):
        gkr[...] = (jnp.where(low, held[0, s, "k"], held[1, s, "k"]) * scale).astype(gkr.dtype)
        gvr[...] = jnp.where(low, held[0, s, "v"], held[1, s, "v"]).astype(gvr.dtype)


def attention(kernel, args, lse, augk, augq, outs, lse_out):
    rows, d = args[0].shape
    pairs = d // (2 * HD)
    sds = jax.ShapeDtypeStruct
    block = pl.BlockSpec((rows, 2 * HD), lambda i: (0, i))
    lse_block = pl.BlockSpec((1, 2, rows), lambda i: (i, 0, 0))
    fixed = lambda a: pl.BlockSpec(a.shape, lambda i: (0, 0))
    out_shape = [sds((rows, d), dtype) for dtype in outs]
    out_specs = [block] * len(outs)
    if lse_out:
        out_shape.append(sds((pairs, 2, rows), F32))
        out_specs.append(lse_block)
    lses = [] if lse is None else [lse]
    return pl.pallas_call(
        kernel,
        grid=(pairs,),
        in_specs=[block] * len(args) + [lse_block] * len(lses) + [fixed(augk), fixed(augq)],
        out_specs=out_specs,
        out_shape=out_shape,
        compiler_params=pltpu.CompilerParams(vmem_limit_bytes=WIDE),
        name="attend_back",
    )(*args, *lses, augk, augq)


def middle_kernel(
    nt, hid, mixed, cot, gain, w_ref,
    out, gmixed, gres, gain_o, g2,
    wi, wo, wd, gate, up, gp, prod, gg, gu, n2, low, gtot,
):
    n, d = hid.shape
    ff = wd.shape[1]
    el, fl = d // nt, ff // nt
    two, three = 2 * fl, 2 * fl + el
    for t in range(nt):
        at = slice(t * fl, (t + 1) * fl)
        wi[0, :, at] = w_ref[:, t, :, :fl].reshape(d, fl)
        wi[1, :, at] = w_ref[:, t, :, fl:two].reshape(d, fl)
        wo[:, t * el : (t + 1) * el] = w_ref[:, t, :, two:three].reshape(d, el)
        wd[:, at] = w_ref[:, t, :, three:].reshape(d, fl)
    gres[...] = dot(mixed[...], wo[...], NT)

    def norm(at):
        value = hid[at, :].astype(F32) + gres[at, :]
        gres[at, :] = value
        xhat, _ = standard(value)
        n2[at, :] = (xhat * gain[...]).astype(BF)

    rows_loop(n, 64, norm)
    gate[...] = dot(n2[...], wi[0])
    up[...] = dot(n2[...], wi[1])
    gp[...] = dot(cot[...], wd[...])

    def geglu(at):
        for j in range(0, ff, 384):
            to = slice(j, j + 384)
            g, u, p = gate[at, to], up[at, to], gp[at, to]
            cdf = 0.5 + 0.5 * erf(g * math.sqrt(0.5))
            pdf = jnp.exp(-0.5 * g * g) * (1.0 / math.sqrt(2 * math.pi))
            act = g * cdf
            prod[at, to] = (act * u).astype(BF)
            gg[at, to] = (p * u * (cdf + g * pdf)).astype(BF)
            gu[at, to] = (p * act).astype(BF)

    rows_loop(n, 32, geglu)
    out[...] = (gres[...] + dot(prod[...], wd[...], NT)).astype(BF)
    gtot[...] = dot(gg[...], wi[0], NT) + dot(gu[...], wi[1], NT)
    gain_o[...] = jnp.zeros_like(gain_o)

    def back(at):
        xhat, scale = standard(gres[at, :])
        e = gtot[at, :]
        part = e * xhat
        gain_o[...] += jnp.sum(part.reshape(-1, 8, d), axis=0)
        total = cot[at, :].astype(F32) + norm_back(e, xhat, scale, gain[...])
        gres[at, :] = total
        low[at, :] = total.astype(BF)

    rows_loop(n, 64, back)
    gmixed[...] = dot(low[...], wo[...]).astype(BF)
    split = (8, d // 8)
    n2t = n2[...].T
    for t in range(nt):
        at = slice(t * fl, (t + 1) * fl)
        g2[:, t, :, :fl] = dot(n2t, gg[:, at]).astype(BF).reshape(*split, fl)
        g2[:, t, :, fl:two] = dot(n2t, gu[:, at]).astype(BF).reshape(*split, fl)
    lowt = low[...].T
    for t in range(nt):
        at = slice(t * el, (t + 1) * el)
        g2[:, t, :, two:three] = dot(lowt, mixed[:, at]).astype(BF).reshape(*split, el)
    cott = cot[...].T
    for t in range(nt):
        at = slice(t * fl, (t + 1) * fl)
        g2[:, t, :, three:] = dot(cott, prod[:, at]).astype(BF).reshape(*split, fl)


def last_kernel(
    nt, hid, gres, gain, gain_two, wf, n1, cos, sin, gq, gk, gv, ak, av,
    gin, g1,
    raw, gtot, gsum,
):
    n, d = hid.shape
    el = d // nt

    def back(at):
        c, s = cos[at, :], -sin[at, :]
        for j in range(0, d, 128):
            to = slice(j, j + 128)
            raw[at, j : j + 128] = turned(gq[at, to], c, s).astype(BF)
            keys = gk[at, to] + ak[at, to].astype(F32)
            raw[at, d + j : d + j + 128] = turned(keys, c, s).astype(BF)
            raw[at, 2 * d + j : 2 * d + j + 128] = (gv[at, to] + av[at, to].astype(F32)).astype(BF)

    rows_loop(n, 32, back)
    gtot[...] = dot(raw[...], wf[...], NT)
    gsum[...] = jnp.zeros_like(gsum)

    def norm(at):
        xhat, scale = standard(hid[at, :].astype(F32))
        e = gtot[at, :]
        gsum[...] += jnp.sum((e * xhat).reshape(-1, 8, d), axis=0)
        gin[at, :] = (gres[at, :] + norm_back(e, xhat, scale, gain[...])).astype(BF)

    rows_loop(n, 64, norm)
    n1t = n1[...].T
    for t in range(nt):
        for c in range(3):
            cols = raw[:, c * d + t * el : c * d + (t + 1) * el]
            g1[:, t, :, c * el : (c + 1) * el] = dot(n1t, cols).astype(BF).reshape(8, d // 8, el)
    rows = []
    for v in (gsum[...], gain_two[...]):
        total = jnp.sum(v, axis=0, keepdims=True)
        upper = total.astype(BF).astype(F32)
        rows += [upper, total - upper]
    rows.append(jnp.zeros((SPARE - 4, d), F32))
    gains = jnp.concatenate(rows, axis=0).T.astype(BF).reshape(8, d // 8, SPARE)
    for t in range(nt):
        g1[:, t, :, 3 * el :] = gains


def shards(hidden_in, cotangent, segment_ids, w_qkv, w_out, w_in, w_down, norm_gains):
    ndp, nt = lax.axis_size("dp"), lax.axis_size("tensor")
    stride = ndp // 8
    rows, local_len, d = hidden_in.shape
    half = local_len // 2
    tokens = nt * half
    ff = w_in.shape[2] * nt
    sds = jax.ShapeDtypeStruct
    low_groups = [[h * stride + i for i in range(stride)] for h in range(8)]

    def swap(v):
        return lax.ppermute(v, "dp", [(i, i ^ 1) for i in range(ndp)])

    dl, el, fl = w_qkv.shape[1], w_qkv.shape[2], w_in.shape[2]

    def widen(v, axis):
        if stride == 1:
            return v
        return lax.all_gather(v, "dp", axis_index_groups=low_groups, axis=axis, tiled=True)

    def narrow(v):
        if stride == 1:
            return v
        return lax.psum_scatter(v, "dp", axis_index_groups=low_groups, tiled=True)

    split = lambda v: v.reshape(2, 2, half, d)
    (
        hid, cot, all_two, q, k, v, k2, v2, n1, wf, mixed, lse, cosine, sine, augk, augq, gains,
    ) = front(
        ndp, nt,
        widen(w_qkv, 1), widen(w_out, 1), widen(w_in, 1), widen(w_down, 1), widen(norm_gains, 1),
        split(hidden_in), split(cotangent), segment_ids,
    )
    gain_one, gain_two = gains[:1], gains[1:2]
    r2, c2 = all_two.shape[4:]
    all_two = all_two.reshape(8, nt, r2, c2)
    c1 = 3 * el + SPARE
    act = sds((tokens, d), BF)
    act32 = sds((tokens, d), F32)
    wide = lambda dtype: VM((tokens, ff), dtype)
    out, gmixed, gres, gain_two_part, g2 = call(
        functools.partial(middle_kernel, nt),
        [act, act, act32, sds((8, d), F32), sds(all_two.shape, BF)],
        [
            VM((2, d, ff), BF), VM((d, d), BF), VM((d, ff), BF),
            wide(F32), wide(F32), wide(F32), wide(BF), wide(BF), wide(BF),
            VM((tokens, d), BF), VM((tokens, d), BF), VM((tokens, d), F32),
        ],
        hid, mixed, cot, gain_two, all_two,
        name="middle",
    )
    second, layer_out = scatter_all(
        ndp, nt, g2.reshape(2, 2, 2, nt, r2, c2), out.reshape(nt, half, d), 1
    )
    gq, gk, gk2, gv, gv2 = attention(
        attend_back_kernel, (q, k, k2, v, v2, gmixed, mixed), lse, augk, augq, (F32, F32, BF, F32, BF), False
    )
    ak, av = swap(gk2), swap(gv2)
    gin, g1 = call(
        functools.partial(last_kernel, nt),
        [act, sds((8, nt, r2, c1), BF)],
        [VM((tokens, 3 * d), BF), VM((tokens, d), F32), VM((8, d), F32)],
        hid, gres, gain_one, gain_two_part, wf, n1, cosine, sine, gq, gk, gv, ak, av,
        name="last",
    )
    one, grad_input = scatter_all(
        ndp, nt, g1.reshape(2, 2, 2, nt, r2, c1), gin.reshape(nt, half, d), 2
    )
    one, second = narrow(one), narrow(second)
    back = lambda t: t.reshape(rows, local_len, d)

    def stacked(t, n, cols):
        return jnp.transpose(t.reshape(dl, n, cols), (1, 0, 2))

    two, three = 2 * fl, 2 * fl + el
    tail = one[:, 3 * el :]
    grad_gains = jnp.stack([tail[:, 0] + tail[:, 1], tail[:, 2] + tail[:, 3]])
    return (
        back(layer_out),
        back(grad_input),
        stacked(one[:, : 3 * el], 3, el),
        second[:, two:three].T,
        stacked(second[:, :two], 2, fl),
        second[:, three:].T,
        grad_gains,
    )


def solution(mesh):
    placed = (
        P("dp", "tensor", None),
        P("dp", "tensor", None),
        P("dp", None),
        P(None, "dp", "tensor"),
        P("tensor", "dp"),
        P(None, "dp", "tensor"),
        P("tensor", "dp"),
        P(None, "dp"),
    )
    return jax.shard_map(
        shards,
        mesh=mesh,
        in_specs=placed,
        out_specs=(
            P("dp", "tensor", None),
            P("dp", "tensor", None),
            P(None, "dp", "tensor"),
            P("tensor", "dp"),
            P(None, "dp", "tensor"),
            P("tensor", "dp"),
            P(None, "dp"),
        ),
        check_vma=False,
    )
```

```python
import functools
import math

import jax
import jax.numpy as jnp
from jax import lax
from jax.experimental import pallas as pl
from jax.experimental.pallas import tpu as pltpu
from jax.sharding import PartitionSpec as P

HD = 64
EPS = 1e-05
THETA = 160000.0
BIG = 1e30
SEGS = 8
SPARE = 8
TO_EXP2 = math.log2(math.e) / math.sqrt(HD)
MESH = pl.DeviceIdType.MESH
BF, F32 = jnp.bfloat16, jnp.float32
VM = pltpu.VMEM
WIDE = 60 * 1024 * 1024


def dot(a, b, dims=((1,), (0,))):
    return lax.dot_general(a, b, (dims, ((), ())), preferred_element_type=F32)


NT = ((1,), (1,))


def erf(x):
    x = jnp.clip(x, -3.832506856900711, 3.832506856900711)
    s = x * x
    p = 0.00022905065861350646
    for c in (0.0034082910107109506, 0.050955695062380861, 0.18520832239976145, 1.128379143519084):
        p = p * s + c
    q = -1.1791602954361697e-7
    for c in (
        0.000023547966471313185,
        0.0010179625278914885,
        0.014070470171167667,
        0.11098505178285362,
        0.49746925110067538,
        1.0,
    ):
        q = q * s + c
    return x * p / q


class Place:
    def __init__(self, ndp, nt):
        self.nt = nt
        self.stride = ndp // 8
        self.dp, self.z = lax.axis_index("dp"), lax.axis_index("tensor")
        high = self.dp // self.stride
        self.b = (high % 2, (high // 2) % 2, high // 4)
        self.core = self.dp % 2

    def flip(self, bit):
        return (self.dp + (1 - 2 * self.b[bit]) * self.stride * 2**bit, self.z)

    def along(self, step):
        return (self.dp, (self.z + step) % self.nt)

    def pair(self, core, z):
        return (self.dp - self.core + core, z)

    def barrier(self, group):
        others = [self.along(s) for s in range(1, self.nt)]
        others += [self.flip(1), self.flip(2)]
        if group or self.stride == 1:
            others += [self.pair(1 - self.core, self.z)]
        if self.stride > 1:
            others += [self.flip(0)]
        if group:
            others += [self.pair(1 - self.core, (self.z + s) % self.nt) for s in range(1, self.nt)]
        sem = pltpu.get_barrier_semaphore()
        for device in others:
            pl.semaphore_signal(sem, inc=1, device_id=device, device_id_type=MESH)
        pl.semaphore_wait(sem, len(others))


def remote(src, dst, send, recv, device):
    return pltpu.make_async_remote_copy(
        src_ref=src, dst_ref=dst, send_sem=send, recv_sem=recv, device_id=device, device_id_type=MESH
    )


def enter_copies(me, src, dst, send, recv):
    starts, ends = [], []
    half = src.shape[2]
    slot = lambda z: dst.at[pl.ds(pl.multiple_of(z * half, half), half)]
    for row in range(2):
        for core in range(2):
            z = 2 * me.core + row
            k = 2 * row + core
            here = jnp.logical_and(z == me.z, core == me.core)
            copy = remote(src.at[row, core], slot(me.z), send.at[k], recv.at[me.z], me.pair(core, z))
            local = pltpu.make_async_copy(src.at[row, core], slot(me.z), recv.at[me.z])
            starts.append((here, copy, local))
    for z in range(me.nt):
        ends.append(remote(src.at[0, 0], slot(z), send.at[0], recv.at[z], me.pair(1 - me.core, z)))
    return starts, ends


def leave_copies(me, src, dst, send, recv):
    starts, ends = [], []
    half = dst.shape[2]
    for z in range(me.nt):
        here = jnp.logical_and(z == me.z, me.z // 2 == me.core)
        k = 2 * (me.z % 2) + me.core
        to = dst.at[me.z % 2, me.core]
        copy = remote(src.at[z * half : (z + 1) * half], to, send.at[z], recv.at[k], me.pair(me.z // 2, z))
        local = pltpu.make_async_copy(src.at[z * half : (z + 1) * half], to, recv.at[k])
        starts.append((here, copy, local))
    for k in range(4):
        ends.append(remote(src.at[:half], dst.at[k // 2, k % 2], send.at[0], recv.at[k], me.pair(1 - me.core, me.z)))
    return starts, ends


def start_all(starts):
    for here, copy, local in starts:
        pl.when(here)(local.start)
        pl.when(jnp.logical_not(here))(copy.start)


def wait_sends(starts):
    for here, copy, _ in starts:
        pl.when(jnp.logical_not(here))(copy.wait_send)


class Gather:
    COPIES = 12

    def __init__(self, me, shard, out, send, recv, own):
        self.me, self.shard, self.out, self.own = me, shard, out, own
        b0, b1, b2 = me.b
        nt, h = me.nt, me.nt // 2
        lo, hi, both = pl.ds(0, h), pl.ds(h, h), pl.ds(0, 2)

        def pair(k, at, other, device):
            cp = remote(out.at[at], out.at[at], send.at[k], recv.at[k], device)
            back = remote(out.at[other], out.at[other], send.at[k], recv.at[k], device)
            return cp, back

        n = nt - 1
        self.z = []
        for s in range(1, nt):
            at = (b2, b1, b0, me.z)
            frm = (b2, b1, b0, (me.z + nt - s) % nt)
            cp = remote(shard, out.at[at], send.at[s - 1], recv.at[s - 1], me.along(s))
            back = remote(shard, out.at[frm], send.at[s - 1], recv.at[s - 1], me.along(s))
            self.z.append((cp, back))
        x, y, core = me.flip(1), me.flip(2), me.flip(0)
        o0, o1, o2 = 1 - b0, 1 - b1, 1 - b2
        self.one = [
            pair(n, (b2, b1, b0, lo), (b2, o1, b0, lo), x),
            pair(n + 1, (b2, b1, b0, hi), (o2, b1, b0, hi), y),
        ]
        self.two = [
            pair(n + 2, (b2, both, b0, lo), (o2, both, b0, lo), y),
            pair(n + 3, (both, b1, b0, hi), (both, o1, b0, hi), x),
        ]
        self.core_a = [pair(n + 4, (b2, b1, b0), (b2, b1, o0), core)]
        self.core_b = [
            pair(n + 5, (b2, o1, b0, lo), (b2, o1, o0, lo), core),
            pair(n + 6, (o2, b1, b0, hi), (o2, b1, o0, hi), core),
        ]
        self.core_c = [
            pair(n + 7, (o2, both, b0, lo), (o2, both, o0, lo), core),
            pair(n + 8, (both, o1, b0, hi), (both, o1, o0, hi), core),
        ]

    def start_z(self):
        b0, b1, b2 = self.me.b
        self.mine = pltpu.make_async_copy(self.shard, self.out.at[b2, b1, b0, self.me.z], self.own)
        self.mine.start()
        for cp, _ in self.z:
            cp.start()

    @staticmethod
    def start(copies):
        for cp, _ in copies:
            cp.start()

    @staticmethod
    def landed(copies):
        for _, back in copies:
            back.wait_recv()

    def after_z(self):
        self.mine.wait()
        self.landed(self.z)
        self.start(self.one + self.core_a)

    def after_one(self):
        self.landed(self.one)
        self.start(self.two + self.core_b)

    def after_two(self):
        self.landed(self.two)
        self.start(self.core_c)

    def finish(self):
        for group in (self.core_a, self.core_b, self.core_c):
            self.landed(group)
        for group in (self.z, self.one, self.two, self.core_a, self.core_b, self.core_c):
            for cp, _ in group:
                cp.wait_send()


class Scatter:
    def __init__(self, me, g, bufs, send, recv):
        self.me, self.g = me, g
        self.r0, self.r1, self.r2, self.rz = bufs
        b0, b1, b2 = me.b
        o0, o1, o2 = 1 - b0, 1 - b1, 1 - b2
        h, nt = me.nt // 2, me.nt
        both = pl.ds(0, 2)
        x, y, core = me.flip(1), me.flip(2), me.flip(0)
        lo, hi = part = (pl.ds(0, h), pl.ds(h, h))

        def copy(k, src, dst, device):
            return remote(src, dst, send.at[k], recv.at[k], device)

        self.core = [
            copy(i, g.at[both, both, o0, part[i]], self.r0.at[i], core) for i in range(2)
        ]
        self.one = [
            copy(2, g.at[both, o1, b0, lo], self.r1.at[0], x),
            copy(3, g.at[o2, both, b0, hi], self.r1.at[1], y),
        ]
        self.two = [
            copy(4, g.at[o2, b1, b0, lo], self.r2.at[0], y),
            copy(5, g.at[b2, o1, b0, hi], self.r2.at[1], x),
        ]
        self.z = [
            copy(5 + s, g.at[b2, b1, b0, (me.z + s) % nt], self.rz.at[s - 1], me.along(s))
            for s in range(1, nt)
        ]

    def add(self, at, got):
        self.g[at] = (self.g[at].astype(F32) + got.astype(F32)).astype(BF)

    def add_core(self, i):
        h = self.me.nt // 2
        self.core[i].wait_recv()
        for a in range(2):
            for b in range(2):
                for t in range(h):
                    self.add((a, b, self.me.b[0], i * h + t), self.r0[i, a, b, t])
        self.one[i].start()

    def add_one(self, i):
        b0, b1, b2 = self.me.b
        h = self.me.nt // 2
        self.one[i].wait_recv()
        for a in range(2):
            for t in range(h):
                at = (a, b1, b0, t) if i == 0 else (b2, a, b0, h + t)
                self.add(at, self.r1[i, a, t])
        self.two[i].start()

    def add_two(self, i):
        b0, b1, b2 = self.me.b
        h = self.me.nt // 2
        self.two[i].wait_recv()
        for t in range(h):
            self.add((b2, b1, b0, i * h + t), self.r2[i, t])

    def send_z(self):
        for cp in self.z:
            cp.start()

    def total(self):
        b0, b1, b2 = self.me.b
        total = self.g[b2, b1, b0, self.me.z].astype(F32)
        for s in range(self.me.nt - 1):
            self.z[s].wait_recv()
            total = total + self.rz[s].astype(F32)
        return total

    def finish(self):
        for cp in self.core + self.one + self.two + self.z:
            cp.wait_send()


def scatter_scratch(nt, r, c):
    h = nt // 2
    dma = pltpu.SemaphoreType.DMA
    return [
        VM((2, 2, 2, nt, r, c), BF),
        VM((2, 2, 2, h, r, c), BF),
        VM((2, 2, h, r, c), BF),
        VM((2, h, r, c), BF),
        VM((nt - 1, r, c), BF),
        dma((6 + nt - 1,)),
        dma((6 + nt - 1,)),
    ]


def standard(v):
    centred = v - jnp.mean(v, axis=-1, keepdims=True)
    scale = lax.rsqrt(jnp.mean(centred * centred, axis=-1, keepdims=True) + EPS)
    return centred * scale, scale


def norm_back(grad, xhat, scale, gain):
    e = grad * gain
    inner = jnp.mean(e * xhat, axis=-1, keepdims=True)
    return scale * (e - jnp.mean(e, axis=-1, keepdims=True) - xhat * inner)


def rows_loop(total, step, body):
    def run(i, carry):
        body(pl.ds(pl.multiple_of(i * step, step), step))
        return carry

    lax.fori_loop(0, total // step, run, 0)


def turned(v, cosine, sine):
    lane = lax.broadcasted_iota(jnp.int32, v.shape, 1)
    other = jnp.where(lane % HD < HD // 2, pltpu.roll(v, 128 - HD // 2, 1), pltpu.roll(v, HD // 2, 1))
    return v * cosine + other * sine


def half_lanes(shape):
    return lax.broadcasted_iota(jnp.int32, shape, 1) < HD


def attend_pair(i, q, k, k2, v, v2, augk, augq, mixed, lse):
    at = pl.ds(pl.multiple_of(i * 2 * HD, 2 * HD), 2 * HD)
    keys = jnp.concatenate([k[:, at], k2[:, at]], axis=0)
    vt = jnp.concatenate([v[:, at], v2[:, at]], axis=0).T
    qt = q[:, at].T
    low = half_lanes(keys.shape)
    ones = jnp.ones((HD, vt.shape[1]), BF)
    outs = []
    for h in range(2):
        if h == 0:
            keys_h = jnp.where(low, keys, augk[...])
            q_h = jnp.concatenate([qt[:HD], augq[...]], axis=0)
            v_h = jnp.concatenate([vt[:HD], ones], axis=0)
        else:
            keys_h = jnp.where(low, augk[...], keys)
            q_h = jnp.concatenate([augq[...], qt[HD:]], axis=0)
            v_h = jnp.concatenate([ones, vt[HD:]], axis=0)
        scores = dot(keys_h, q_h)
        top = jnp.max(scores, axis=0, keepdims=True)
        expo = jnp.exp2((scores - top) * TO_EXP2).astype(BF)
        got = dot(v_h, expo)
        value, total = (got[:HD], got[HD:]) if h == 0 else (got[HD:], got[:HD])
        outs.append(value / total)
        lse[i, h : h + 1, :] = top + jnp.log2(total[:1]) * (1.0 / TO_EXP2)
    mixed[:, at] = jnp.concatenate(outs, axis=0).T.astype(BF)


def column(row):
    return jnp.concatenate([row] * 8, axis=0).T[:, :1]


def masks(me, row, half, freq, cos, sin, augk, augq):
    n = me.nt * half
    part = lambda core: jnp.concatenate(
        [row[:, (2 * z + core) * half : (2 * z + core + 1) * half] for z in range(me.nt)], axis=1
    ).astype(F32)
    even, odd = part(0), part(1)
    seg_q, seg_o = jnp.where(me.core == 0, even, odd), jnp.where(me.core == 0, odd, even)
    whole = jnp.concatenate([seg_q, seg_o], axis=1)
    mine = column(seg_q)
    spot = lax.broadcasted_iota(jnp.int32, (n, 1), 0)
    spot = spot + (spot // half) * half + me.core * half
    first = jnp.zeros((n, 1), F32)
    for s in range(SEGS - 2):
        count = jnp.sum((whole == s).astype(F32), axis=1, keepdims=True)
        first = first + jnp.where(mine > s, count, 0.0)
    angle = (spot.astype(F32) - first) * freq[...]
    cos[...] = jnp.cos(angle)
    sines = jnp.sin(angle)
    lane = lax.broadcasted_iota(jnp.int32, sines.shape, 1)
    sin[...] = jnp.where(lane % HD < HD // 2, -sines, sines)
    for s, seg in enumerate((mine, column(seg_o))):
        ids = lax.broadcasted_iota(jnp.int32, (n, 2 * HD), 1) % HD
        hot = jnp.logical_or(seg == ids.astype(F32), jnp.logical_and(ids >= SEGS, ids < SEGS + 3))
        augk[s * n : (s + 1) * n, :] = jnp.where(hot, 1.0, 0.0).astype(BF)
    ids = lax.broadcasted_iota(jnp.int32, (HD, n), 0)
    off = jnp.logical_and(ids < SEGS, seg_q != ids.astype(F32))
    augq[...] = jnp.where(off, -BIG, 0.0).astype(BF)


def front_kernel(
    ndp, nt,
    w_qkv, w_out, w_in, w_down, gains_in, hid_in, cot_in, seg, freq,
    hid, cot, all_two, q, k, v, k2, v2, n1, wf, mixed, lse, cos, sin, augk, augq, gains,
    w1, w2, all_one, seg_o, raw, s1, r1, s2, r2, own, se, re, sc, rc, ss,
):
    n, d = hid.shape
    el, fl = w_qkv.shape[2], w_in.shape[2]
    r = w_qkv.shape[1]
    half = n // nt
    me = Place(ndp, nt)
    me.barrier(True)
    first = Gather(me, w1, all_one, s1, r1, own.at[0])
    second = Gather(me, w2, all_two, s2, r2, own.at[1])
    hs, he = enter_copies(me, hid_in, hid, se, re)
    cs, ce = enter_copies(me, cot_in, cot, sc, rc)
    buddy = me.pair(1 - me.core, me.z)
    swap = remote(seg, seg_o, ss.at[0], ss.at[3], buddy)
    swap.start()
    for c in range(3):
        w1[:, c * el : (c + 1) * el] = w_qkv[c]
    cols = jnp.concatenate([gains_in[...].astype(F32), jnp.zeros((SPARE - 2, r), F32)], axis=0)
    w1[:, 3 * el :] = cols.T.astype(BF)
    first.start_z()
    start_all(hs)
    two, three = 2 * fl, 2 * fl + el
    w2[:, :fl] = w_in[0]
    w2[:, fl:two] = w_in[1]
    w2[:, two:three] = w_out[...].astype(F32).T.astype(BF)
    w2[:, three:] = w_down[...].astype(F32).T.astype(BF)
    first.after_z()
    second.start_z()
    swap.wait()
    here = me.z // 2 == me.core
    index = me.z % 2
    both = jnp.where(here, seg[...], seg_o[...])
    row = jnp.where(index == 0, both[:1], both[1:2])
    masks(me, row, half, freq, cos, sin, augk, augq)
    first.after_one()
    for e in he:
        e.wait_recv()

    def spread(at):
        raw[at, :] = standard(hid[at, :].astype(F32))[0]

    rows_loop(n, 64, spread)
    first.after_two()
    first.finish()
    top = all_one[:, :, :, 0, :, 3 * el :].reshape(d, SPARE).astype(F32).T
    gains[...] = top
    gain = top[:1]

    def norm(at):
        n1[at, :] = (raw[at, :] * gain).astype(BF)

    rows_loop(n, 64, norm)
    for t in range(nt):
        for c in range(3):
            block = all_one[:, :, :, t, :, c * el : (c + 1) * el]
            wf[:, c * d + t * el : c * d + (t + 1) * el] = block.reshape(d, el)
    swaps = [remote(k, k2, ss.at[1], ss.at[4], buddy), remote(v, v2, ss.at[2], ss.at[5], buddy)]
    for c, out in ((1, k), (2, v), (0, q)):
        raw[...] = dot(n1[...], wf[:, c * d : (c + 1) * d])

        def finish(at, c=c, out=out):
            for j in range(0, d, 128):
                value = raw[at, j : j + 128]
                if c < 2:
                    value = turned(value, cos[at, :], sin[at, :])
                out[at, j : j + 128] = value.astype(BF)

        rows_loop(n, 64, finish)
        if c:
            swaps[c - 1].start()
    second.after_z()
    start_all(cs)
    for s in swaps:
        s.wait()
    pairs = d // (2 * HD)

    def attend(begin, end):
        def step(i, carry):
            attend_pair(i, q, k, k2, v, v2, augk, augq, mixed, lse)
            return carry

        lax.fori_loop(begin, end, step, 0)

    attend(0, pairs // 2)
    second.after_one()
    attend(pairs // 2, pairs)
    second.after_two()
    for e in ce:
        e.wait_recv()
    second.finish()
    wait_sends(hs)
    wait_sends(cs)


def front(ndp, nt, w_qkv, w_out, w_in, w_down, gains, hid, cot, seg):
    half, d = hid.shape[2:]
    n = nt * half
    r, el, fl = w_qkv.shape[1], w_qkv.shape[2], w_in.shape[2]
    c1, c2 = 3 * el + SPARE, 2 * fl + el + fl
    freq = jnp.tile(THETA ** (-2.0 * jnp.arange(HD // 2, dtype=F32) / HD), 4)[None]
    sds = jax.ShapeDtypeStruct
    dma = pltpu.SemaphoreType.DMA
    copies = Gather.COPIES
    vm, hbm = pl.BlockSpec(memory_space=VM), pl.BlockSpec(memory_space=pl.ANY)
    act = sds((n, d), BF)
    return pl.pallas_call(
        functools.partial(front_kernel, ndp, nt),
        in_specs=[vm] * 5 + [hbm] * 2 + [vm] * 2,
        out_specs=[vm, hbm, hbm] + [vm] * 14,
        out_shape=[act, act, sds((2, 2, 2, nt, r, c2), BF)]
        + [act] * 6
        + [sds((d, 3 * d), BF), act, sds((d // (2 * HD), 2, n), F32)]
        + [sds((n, 2 * HD), F32)] * 2
        + [sds((2 * n, 2 * HD), BF), sds((HD, n), BF), sds((SPARE, d), F32)],
        scratch_shapes=[
            VM((r, c1), BF),
            VM((r, c2), BF),
            VM((2, 2, 2, nt, r, c1), BF),
            VM(seg.shape, seg.dtype),
            VM((n, d), F32),
        ]
        + [dma((copies,))] * 4
        + [dma((2,))]
        + [dma((4,))] * 4
        + [dma((6,))],
        compiler_params=pltpu.CompilerParams(
            collective_id=0, has_side_effects=True, vmem_limit_bytes=WIDE
        ),
        name="front",
    )(w_qkv, w_out, w_in, w_down, gains, hid, cot, seg, freq)


def split_rows(value, n, rows):
    parts = []
    for _ in range(n):
        part = value.astype(BF).astype(F32)
        parts.append(part)
        value = value - part
    parts.append(jnp.zeros((rows - n, value.shape[1]), F32))
    return jnp.concatenate(parts, axis=0).astype(BF)


def attend_back_pair(i, q, k, k2, v, v2, g, mixed, lse, augk, augq, gq, gk, gk2, gv, gv2):
    at = pl.ds(pl.multiple_of(i * 2 * HD, 2 * HD), 2 * HD)
    rows = q.shape[0]
    grads, query = g[:, at], q[:, at]
    gt, qt = grads.T, query.T
    prod = gt.astype(F32) * mixed[:, at].T.astype(F32)
    gq_parts = []
    sides = [(k, v, gk, gv), (k2, v2, gk2, gv2)]
    low = half_lanes((rows, 2 * HD))
    one = jnp.ones((rows, 2 * HD), BF)
    held = {}
    for h in range(2):
        mine = slice(h * HD, (h + 1) * HD)

        def swapped(a, b, h=h):
            return (a, b) if h == 0 else (b, a)

        inner = jnp.sum(prod[mine], axis=0, keepdims=True)
        neg = split_rows(-lse[i, h : h + 1, :], 3, SEGS)
        extra_q = jnp.concatenate([augq[:SEGS], neg, augq[2 * SEGS :]], axis=0)
        extra_g = jnp.concatenate([split_rows(-inner, 2, 8), jnp.zeros((HD - 8, rows), BF)], axis=0)
        q_h = jnp.concatenate(swapped(qt[mine], extra_q), axis=0)
        g_h = jnp.concatenate(swapped(gt[mine], extra_g), axis=0)
        gq_h = None
        for s, (kr, vr, _, _) in enumerate(sides):
            aug = augk[s * rows : (s + 1) * rows, :]
            keys, values = kr[:, at], vr[:, at]
            probs = jnp.exp2(dot(jnp.where(low, *swapped(keys, aug)), q_h) * TO_EXP2)
            grad_p = dot(jnp.where(low, *swapped(values, one)), g_h)
            held[h, s, "v"] = dot(probs.astype(BF), grads)
            ds = (probs * grad_p).astype(BF)
            held[h, s, "k"] = dot(ds, query)
            part = dot(keys.T[mine], ds)
            gq_h = part if gq_h is None else gq_h + part
        gq_parts.append(gq_h)
    scale = 1.0 / math.sqrt(HD)
    gq[:, at] = jnp.concatenate(gq_parts, axis=0).T * scale
    for s, (_, _, gkr, gvr) in enumerate(sides):
        gkr[:, at] = (jnp.where(low, held[0, s, "k"], held[1, s, "k"]) * scale).astype(gkr.dtype)
        gvr[:, at] = jnp.where(low, held[0, s, "v"], held[1, s, "v"]).astype(gvr.dtype)


def back_kernel(
    ndp, nt,
    hid, cot, all_two, q, k, v, k2, v2, n1, wf, mixed, lse, cos, sin, augk, augq, gains,
    out_o, gin_o, grad_qkv, grad_out, grad_in, grad_down, grad_gains,
    w3, wo, wd, gate, up, gp, prod, gu, n2, low, gres, gtot, gmixed, out, ak, av, gsum, local, ss, so, ro, si, ri, *rest,
):
    n, d = hid.shape
    ff = wd.shape[1]
    el, fl = d // nt, ff // nt
    two, three = 2 * fl, 2 * fl + el
    split = (2, 2, 2, d // 8)
    g2, g1 = rest[0], rest[7]
    gin, gk2, gv2 = gmixed, low, n2
    me = Place(ndp, nt)
    load = pltpu.make_async_copy(all_two, g2, local.at[0])
    load.start()
    me.barrier(True)
    rs2 = Scatter(me, g2, rest[1:5], *rest[5:7])
    rs1 = Scatter(me, g1, rest[8:12], *rest[12:14])
    lo_s, lo_e = leave_copies(me, out, out_o, so, ro)
    gi_s, gi_e = leave_copies(me, gin, gin_o, si, ri)
    gain_one, gain_two = gains[0:1, :], gains[1:2, :]
    load.wait()
    for t in range(nt):
        w3[:, t * fl : (t + 1) * fl] = g2[:, :, :, t, :, :fl].reshape(d, fl)
        w3[:, ff + t * fl : ff + (t + 1) * fl] = g2[:, :, :, t, :, fl:two].reshape(d, fl)
        wo[:, t * el : (t + 1) * el] = g2[:, :, :, t, :, two:three].reshape(d, el)
        wd[:, t * fl : (t + 1) * fl] = g2[:, :, :, t, :, three:].reshape(d, fl)
    gres[...] = dot(mixed[...], wo[...], NT)

    def norm(at):
        value = hid[at, :].astype(F32) + gres[at, :]
        gres[at, :] = value
        n2[at, :] = (standard(value)[0] * gain_two).astype(BF)

    rows_loop(n, 64, norm)
    gate[...] = dot(n2[...], w3[:, :ff])
    up[...] = dot(n2[...], w3[:, ff:])
    gp[...] = dot(cot[...], wd[...])

    def geglu(at):
        for j in range(0, ff, 384):
            to = slice(j, j + 384)
            g, u, p = gate[at, to], up[at, to], gp[at, to]
            cdf = 0.5 + 0.5 * erf(g * math.sqrt(0.5))
            pdf = jnp.exp(-0.5 * g * g) * (1.0 / math.sqrt(2 * math.pi))
            act = g * cdf
            prod[at, to] = (act * u).astype(BF)
            gu[at, to] = (p * u * (cdf + g * pdf)).astype(BF)
            gu[at, ff + j : ff + j + 384] = (p * act).astype(BF)

    rows_loop(n, 32, geglu)
    out[...] = (gres[...] + dot(prod[...], wd[...], NT)).astype(BF)
    start_all(lo_s)
    gtot[...] = dot(gu[...], w3[...], NT)
    load_wf = pltpu.make_async_copy(wf, w3, local.at[1])
    load_wf.start()
    gsum[...] = jnp.zeros_like(gsum)

    def back_two(at):
        xhat, scale = standard(gres[at, :])
        e = gtot[at, :]
        gsum[0] += jnp.sum((e * xhat).reshape(-1, 8, d), axis=0)
        total = cot[at, :].astype(F32) + norm_back(e, xhat, scale, gain_two)
        gres[at, :] = total
        low[at, :] = total.astype(BF)

    rows_loop(n, 64, back_two)
    n2t, lowt, cott = n2[...].T, low[...].T, cot[...].T
    for t in range(nt):
        at, to = slice(t * fl, (t + 1) * fl), slice(t * el, (t + 1) * el)
        g2[:, :, :, t, :, :fl] = dot(n2t, gu[:, at]).astype(BF).reshape(*split, fl)
        g2[:, :, :, t, :, fl:two] = dot(n2t, gu[:, ff + t * fl : ff + (t + 1) * fl]).astype(BF).reshape(*split, fl)
        g2[:, :, :, t, :, two:three] = dot(lowt, mixed[:, to]).astype(BF).reshape(*split, el)
        g2[:, :, :, t, :, three:] = dot(cott, prod[:, at]).astype(BF).reshape(*split, fl)
        if t == nt // 2 - 1:
            rs2.core[0].start()
    rs2.core[1].start()
    gmixed[...] = dot(low[...], wo[...]).astype(BF)
    rs2.add_core(0)
    rs2.add_core(1)
    gq, gk, gv = gate, up, gp

    def step(i, carry):
        attend_back_pair(i, q, k, k2, v, v2, gmixed, mixed, lse, augk, augq, gq, gk, gk2, gv, gv2)
        return carry

    lax.fori_loop(0, d // (2 * HD), step, 0)
    buddy = me.pair(1 - me.core, me.z)
    swaps = [remote(gk2, ak, ss.at[0], ss.at[2], buddy), remote(gv2, av, ss.at[1], ss.at[3], buddy)]
    for s in swaps:
        s.start()
    rs2.add_one(0)
    rs2.add_one(1)
    for s in swaps:
        s.wait()
    raw = gu

    def back_rope(at):
        c, s = cos[at, :], -sin[at, :]
        for j in range(0, d, 128):
            to = slice(j, j + 128)
            raw[at, j : j + 128] = turned(gq[at, to], c, s).astype(BF)
            keys = gk[at, to] + ak[at, to].astype(F32)
            raw[at, d + j : d + j + 128] = turned(keys, c, s).astype(BF)
            raw[at, 2 * d + j : 2 * d + j + 128] = (gv[at, to] + av[at, to].astype(F32)).astype(BF)

    rows_loop(n, 32, back_rope)
    load_wf.wait()
    gtot[...] = dot(raw[...], w3[...], NT)
    rs2.add_two(0)
    rs2.add_two(1)
    rs2.send_z()

    def back_one(at):
        xhat, scale = standard(hid[at, :].astype(F32))
        e = gtot[at, :]
        gsum[1] += jnp.sum((e * xhat).reshape(-1, 8, d), axis=0)
        gin[at, :] = (gres[at, :] + norm_back(e, xhat, scale, gain_one)).astype(BF)

    rows_loop(n, 64, back_one)
    rows = []
    for v_ in (gsum[1], gsum[0]):
        total = jnp.sum(v_, axis=0, keepdims=True)
        upper = total.astype(BF).astype(F32)
        rows += [upper, total - upper]
    rows.append(jnp.zeros((SPARE - 4, d), F32))
    gain_cols = jnp.concatenate(rows, axis=0).T.astype(BF).reshape(*split, SPARE)
    n1t = n1[...].T
    for t in range(nt):
        for c in range(3):
            cols = raw[:, c * d + t * el : c * d + (t + 1) * el]
            g1[:, :, :, t, :, c * el : (c + 1) * el] = dot(n1t, cols).astype(BF).reshape(*split, el)
        g1[:, :, :, t, :, 3 * el :] = gain_cols
        if t == nt // 2 - 1:
            rs1.core[0].start()
    rs1.core[1].start()
    start_all(gi_s)
    rs1.add_core(0)
    rs1.add_core(1)
    rs1.add_one(0)
    rs1.add_one(1)
    total = rs2.total()
    grad_in[0] = total[:, :fl]
    grad_in[1] = total[:, fl:two]
    grad_out[...] = total[:, two:three].T
    grad_down[...] = total[:, three:].T
    rs1.add_two(0)
    rs1.add_two(1)
    rs1.send_z()
    total = rs1.total()
    for c in range(3):
        grad_qkv[c] = total[:, c * el : (c + 1) * el]
    tail = total[:, 3 * el :].T
    grad_gains[...] = jnp.concatenate([tail[0:1] + tail[1:2], tail[2:3] + tail[3:4]], axis=0)
    for e in lo_e + gi_e:
        e.wait_recv()
    rs2.finish()
    rs1.finish()
    wait_sends(lo_s)
    wait_sends(gi_s)


def backward(ndp, nt, half, arrays):
    hid, all_two = arrays[0], arrays[2]
    n, d = hid.shape
    r, c2 = all_two.shape[4:]
    el = d // nt
    fl = (c2 - el) // 3
    ff = fl * nt
    sds = jax.ShapeDtypeStruct
    dma = pltpu.SemaphoreType.DMA
    vm, hbm = pl.BlockSpec(memory_space=VM), pl.BlockSpec(memory_space=pl.ANY)
    specs = [vm] * len(arrays)
    specs[2] = specs[9] = hbm
    wide, act = VM((n, ff), F32), VM((n, d), BF)
    return pl.pallas_call(
        functools.partial(back_kernel, ndp, nt),
        in_specs=specs,
        out_specs=[hbm, hbm] + [vm] * 5,
        out_shape=[sds((2, 2, half, d), BF)] * 2
        + [
            sds((3, r, el), F32),
            sds((el, r), F32),
            sds((2, r, fl), F32),
            sds((fl, r), F32),
            sds((2, r), F32),
        ],
        scratch_shapes=[VM((d, 2 * ff), BF), VM((d, d), BF), VM((d, ff), BF)]
        + [wide] * 3
        + [VM((n, ff), BF), VM((n, 2 * ff), BF), act, act, VM((n, d), F32), VM((n, d), F32)]
        + [act] * 4
        + [VM((2, 8, d), F32), dma((2,)), dma((4,))]
        + [dma((4,))] * 4
        + scatter_scratch(nt, r, c2)
        + scatter_scratch(nt, r, 3 * el + SPARE),
        compiler_params=pltpu.CompilerParams(
            collective_id=1, has_side_effects=True, vmem_limit_bytes=WIDE
        ),
        name="backward",
    )(*arrays)


def shards(hidden_in, cotangent, segment_ids, w_qkv, w_out, w_in, w_down, norm_gains):
    ndp, nt = lax.axis_size("dp"), lax.axis_size("tensor")
    stride = ndp // 8
    rows, local_len, d = hidden_in.shape
    half = local_len // 2
    low_groups = [[h * stride + i for i in range(stride)] for h in range(8)]

    def widen(v, axis):
        if stride == 1:
            return v
        return lax.all_gather(v, "dp", axis_index_groups=low_groups, axis=axis, tiled=True)

    def narrow(v, axis):
        if stride == 1:
            return v
        return lax.psum_scatter(
            v, "dp", scatter_dimension=axis, axis_index_groups=low_groups, tiled=True
        )

    split = lambda v: v.reshape(2, 2, half, d)
    arrays = front(
        ndp, nt,
        widen(w_qkv, 1), widen(w_out, 1), widen(w_in, 1), widen(w_down, 1), widen(norm_gains, 1),
        split(hidden_in), split(cotangent), segment_ids,
    )
    layer_out, grad_input, grad_qkv, grad_out, grad_in, grad_down, grad_gains = backward(
        ndp, nt, half, arrays
    )
    back = lambda t: t.reshape(rows, local_len, d)
    return (
        back(layer_out),
        back(grad_input),
        narrow(grad_qkv, 1),
        narrow(grad_out, 1),
        narrow(grad_in, 1),
        narrow(grad_down, 1),
        narrow(grad_gains, 1),
    )


def solution(mesh):
    placed = (
        P("dp", "tensor", None),
        P("dp", "tensor", None),
        P("dp", None),
        P(None, "dp", "tensor"),
        P("tensor", "dp"),
        P(None, "dp", "tensor"),
        P("tensor", "dp"),
        P(None, "dp"),
    )
    return jax.shard_map(
        shards,
        mesh=mesh,
        in_specs=placed,
        out_specs=(
            P("dp", "tensor", None),
            P("dp", "tensor", None),
            P(None, "dp", "tensor"),
            P("tensor", "dp"),
            P(None, "dp", "tensor"),
            P("tensor", "dp"),
            P(None, "dp"),
        ),
        check_vma=False,
    )
```

```python
import functools
import math

import jax
import jax.numpy as jnp
from jax import lax
from jax.experimental import pallas as pl
from jax.experimental.pallas import tpu as pltpu
from jax.sharding import PartitionSpec as P

HD = 64
EPS = 1e-05
THETA = 160000.0
BIG = 1e30
SEGS = 8
SPARE = 8
TO_EXP2 = math.log2(math.e) / math.sqrt(HD)
MESH = pl.DeviceIdType.MESH
BF, F32 = jnp.bfloat16, jnp.float32
VM = pltpu.VMEM
WIDE = 60 * 1024 * 1024


def dot(a, b, dims=((1,), (0,))):
    return lax.dot_general(a, b, (dims, ((), ())), preferred_element_type=F32)


NT = ((1,), (1,))


def erf(x):
    x = jnp.clip(x, -3.832506856900711, 3.832506856900711)
    s = x * x
    p = 0.00022905065861350646
    for c in (0.0034082910107109506, 0.050955695062380861, 0.18520832239976145, 1.128379143519084):
        p = p * s + c
    q = -1.1791602954361697e-7
    for c in (
        0.000023547966471313185,
        0.0010179625278914885,
        0.014070470171167667,
        0.11098505178285362,
        0.49746925110067538,
        1.0,
    ):
        q = q * s + c
    return x * p / q


class Place:
    def __init__(self, ndp, nt):
        self.nt = nt
        self.stride = ndp // 8
        self.dp, self.z = lax.axis_index("dp"), lax.axis_index("tensor")
        high = self.dp // self.stride
        self.b = (high % 2, (high // 2) % 2, high // 4)
        self.core = self.dp % 2

    def flip(self, bit):
        return (self.dp + (1 - 2 * self.b[bit]) * self.stride * 2**bit, self.z)

    def along(self, step):
        return (self.dp, (self.z + step) % self.nt)

    def pair(self, core, z):
        return (self.dp - self.core + core, z)

    def barrier(self, group):
        others = [self.along(s) for s in range(1, self.nt)]
        others += [self.flip(1), self.flip(2)]
        if group or self.stride == 1:
            others += [self.pair(1 - self.core, self.z)]
        if self.stride > 1:
            others += [self.flip(0)]
        if group:
            others += [self.pair(1 - self.core, (self.z + s) % self.nt) for s in range(1, self.nt)]
        sem = pltpu.get_barrier_semaphore()
        for device in others:
            pl.semaphore_signal(sem, inc=1, device_id=device, device_id_type=MESH)
        pl.semaphore_wait(sem, len(others))


def remote(src, dst, send, recv, device):
    return pltpu.make_async_remote_copy(
        src_ref=src, dst_ref=dst, send_sem=send, recv_sem=recv, device_id=device, device_id_type=MESH
    )


def enter_copies(me, src, dst, send, recv):
    starts, ends = [], []
    half = src.shape[2]
    slot = lambda z: dst.at[pl.ds(pl.multiple_of(z * half, half), half)]
    for row in range(2):
        for core in range(2):
            z = 2 * me.core + row
            k = 2 * row + core
            here = jnp.logical_and(z == me.z, core == me.core)
            copy = remote(src.at[row, core], slot(me.z), send.at[k], recv.at[me.z], me.pair(core, z))
            local = pltpu.make_async_copy(src.at[row, core], slot(me.z), recv.at[me.z])
            starts.append((here, copy, local))
    for z in range(me.nt):
        ends.append(remote(src.at[0, 0], slot(z), send.at[0], recv.at[z], me.pair(1 - me.core, z)))
    return starts, ends


def leave_copies(me, src, dst, send, recv):
    starts, ends = [], []
    half = dst.shape[2]
    for z in range(me.nt):
        here = jnp.logical_and(z == me.z, me.z // 2 == me.core)
        k = 2 * (me.z % 2) + me.core
        to = dst.at[me.z % 2, me.core]
        copy = remote(src.at[z * half : (z + 1) * half], to, send.at[z], recv.at[k], me.pair(me.z // 2, z))
        local = pltpu.make_async_copy(src.at[z * half : (z + 1) * half], to, recv.at[k])
        starts.append((here, copy, local))
    for k in range(4):
        ends.append(remote(src.at[:half], dst.at[k // 2, k % 2], send.at[0], recv.at[k], me.pair(1 - me.core, me.z)))
    return starts, ends


def start_all(starts):
    for here, copy, local in starts:
        pl.when(here)(local.start)
        pl.when(jnp.logical_not(here))(copy.start)


def wait_sends(starts):
    for here, copy, _ in starts:
        pl.when(jnp.logical_not(here))(copy.wait_send)


class Gather:
    def __init__(self, me, shard, out, send, recv, own):
        self.me, self.shard, self.out = me, shard, out
        b0, b1, b2 = me.b
        nt = me.nt
        both = pl.ds(0, 2)
        x, y, core = me.flip(1), me.flip(2), me.flip(0)
        o0, o1, o2 = 1 - b0, 1 - b1, 1 - b2
        self.mine = pltpu.make_async_copy(shard, out.at[b2, b1, b0, me.z], own)
        self.z, self.one, self.two, self.core = [], [], [], []
        for s in range(nt):
            t = (me.z + nt - s) % nt

            def pair(k, at, other, device, s=s, t=t):
                sems = send.at[s, k], recv.at[s, k]
                cp = remote(out.at[(*at, t)], out.at[(*at, t)], *sems, device)
                return cp, remote(out.at[(*other, t)], out.at[(*other, t)], *sems, device)

            if s:
                sems = send.at[s, 0], recv.at[s, 0]
                to, frm = out.at[b2, b1, b0, me.z], out.at[b2, b1, b0, t]
                self.z.append((remote(shard, to, *sems, me.along(s)), remote(shard, frm, *sems, me.along(s))))
            else:
                self.z.append(None)
            if s % 2 == 0:
                self.one.append(pair(1, (b2, b1, b0), (b2, o1, b0), x))
                self.two.append(pair(2, (b2, both, b0), (o2, both, b0), y))
                got_one, got_two = (b2, o1), (o2, both)
            else:
                self.one.append(pair(1, (b2, b1, b0), (o2, b1, b0), y))
                self.two.append(pair(2, (both, b1, b0), (both, o1, b0), x))
                got_one, got_two = (o2, b1), (both, o1)
            self.core.append(
                [
                    pair(3, (b2, b1, b0), (b2, b1, o0), core),
                    pair(4, (*got_one, b0), (*got_one, o0), core),
                    pair(5, (*got_two, b0), (*got_two, o0), core),
                ]
            )

    def start_z(self):
        self.mine.start()
        for cp, _ in self.z[1:]:
            cp.start()

    def after_z(self, s):
        if s:
            self.z[s][1].wait_recv()
        else:
            self.mine.wait()
        self.one[s][0].start()
        self.core[s][0][0].start()

    def after_one(self, s):
        self.one[s][1].wait_recv()
        self.two[s][0].start()
        self.core[s][1][0].start()

    def after_two(self, s):
        self.two[s][1].wait_recv()
        self.core[s][2][0].start()

    def finish(self):
        for group in self.core:
            for _, back in group:
                back.wait_recv()
        for cp, _ in self.z[1:] + self.one + self.two + sum(self.core, []):
            cp.wait_send()


class Scatter:
    def __init__(self, me, g, bufs, send, recv):
        self.me, self.g = me, g
        self.r0, self.r1, self.r2, self.rz = bufs
        b0, b1, b2 = me.b
        o0, o1, o2 = 1 - b0, 1 - b1, 1 - b2
        nt = me.nt
        both = pl.ds(0, 2)
        x, y, core = me.flip(1), me.flip(2), me.flip(0)
        self.core, self.one, self.two, self.z, self.back = [], [], [], [], []
        for t in range(nt):
            sems = [(send.at[t, k], recv.at[t, k]) for k in range(3)]
            one, two = (g.at[both, o1, b0, t], g.at[o2, b1, b0, t]), (x, y)
            if t % 2:
                one, two = (g.at[o2, both, b0, t], g.at[b2, o1, b0, t]), (y, x)
            self.core.append(remote(g.at[both, both, o0, t], self.r0.at[t], *sems[0], core))
            self.one.append(remote(one[0], self.r1.at[t], *sems[1], two[0]))
            self.two.append(remote(one[1], self.r2.at[t], *sems[2], two[1]))
            slot = (t - me.z + nt - 1) % nt
            slot = jnp.minimum(slot, nt - 2)
            self.z.append(
                remote(g.at[b2, b1, b0, t], self.rz.at[slot], send.at[t, 3], recv.at[slot, 3], (me.dp, t))
            )
        for s in range(nt - 1):
            self.back.append(
                remote(g.at[b2, b1, b0, 0], self.rz.at[s], send.at[s, 3], recv.at[s, 3], me.along(1))
            )

    def add(self, at, got):
        self.g[at] = (self.g[at].astype(F32) + got.astype(F32)).astype(BF)

    def add_core(self, t):
        self.core[t].wait_recv()
        for a in range(2):
            for b in range(2):
                self.add((a, b, self.me.b[0], t), self.r0[t, a, b])
        self.one[t].start()

    def add_one(self, t):
        b0, b1, b2 = self.me.b
        self.one[t].wait_recv()
        for a in range(2):
            self.add((b2, a, b0, t) if t % 2 else (a, b1, b0, t), self.r1[t, a])
        self.two[t].start()

    def add_two(self, t):
        b0, b1, b2 = self.me.b
        self.two[t].wait_recv()
        self.add((b2, b1, b0, t), self.r2[t])
        pl.when(self.me.z != t)(self.z[t].start)

    def total(self):
        b0, b1, b2 = self.me.b
        total = self.g[b2, b1, b0, self.me.z].astype(F32)
        for s in range(self.me.nt - 1):
            self.back[s].wait_recv()
            total = total + self.rz[s].astype(F32)
        return total

    def finish(self):
        for cp in self.core + self.one + self.two:
            cp.wait_send()
        for t, cp in enumerate(self.z):
            pl.when(self.me.z != t)(cp.wait_send)


def scatter_scratch(nt, r, c):
    dma = pltpu.SemaphoreType.DMA
    return [
        VM((2, 2, 2, nt, r, c), BF),
        VM((nt, 2, 2, r, c), BF),
        VM((nt, 2, r, c), BF),
        VM((nt, r, c), BF),
        VM((nt - 1, r, c), BF),
        dma((nt, 4)),
        dma((nt, 4)),
    ]


def standard(v):
    centred = v - jnp.mean(v, axis=-1, keepdims=True)
    scale = lax.rsqrt(jnp.mean(centred * centred, axis=-1, keepdims=True) + EPS)
    return centred * scale, scale


def norm_back(grad, xhat, scale, gain):
    e = grad * gain
    inner = jnp.mean(e * xhat, axis=-1, keepdims=True)
    return scale * (e - jnp.mean(e, axis=-1, keepdims=True) - xhat * inner)


def rows_loop(total, step, body):
    def run(i, carry):
        body(pl.ds(pl.multiple_of(i * step, step), step))
        return carry

    lax.fori_loop(0, total // step, run, 0)


def turned(v, cosine, sine):
    lane = lax.broadcasted_iota(jnp.int32, v.shape, 1)
    other = jnp.where(lane % HD < HD // 2, pltpu.roll(v, 128 - HD // 2, 1), pltpu.roll(v, HD // 2, 1))
    return v * cosine + other * sine


def half_lanes(shape):
    return lax.broadcasted_iota(jnp.int32, shape, 1) < HD


def attend_pair(i, q, k, k2, v, v2, augk, augq, mixed, lse):
    at = pl.ds(pl.multiple_of(i * 2 * HD, 2 * HD), 2 * HD)
    keys = jnp.concatenate([k[:, at], k2[:, at]], axis=0)
    vt = jnp.concatenate([v[:, at], v2[:, at]], axis=0).T
    qt = q[:, at].T
    low = half_lanes(keys.shape)
    ones = jnp.ones((HD, vt.shape[1]), BF)
    outs = []
    for h in range(2):
        if h == 0:
            keys_h = jnp.where(low, keys, augk[...])
            q_h = jnp.concatenate([qt[:HD], augq[...]], axis=0)
            v_h = jnp.concatenate([vt[:HD], ones], axis=0)
        else:
            keys_h = jnp.where(low, augk[...], keys)
            q_h = jnp.concatenate([augq[...], qt[HD:]], axis=0)
            v_h = jnp.concatenate([ones, vt[HD:]], axis=0)
        scores = dot(keys_h, q_h)
        top = jnp.max(scores, axis=0, keepdims=True)
        expo = jnp.exp2((scores - top) * TO_EXP2).astype(BF)
        got = dot(v_h, expo)
        value, total = (got[:HD], got[HD:]) if h == 0 else (got[HD:], got[:HD])
        outs.append(value / total)
        lse[i, h : h + 1, :] = top + jnp.log2(total[:1]) * (1.0 / TO_EXP2)
    mixed[:, at] = jnp.concatenate(outs, axis=0).T.astype(BF)


def column(row):
    return jnp.concatenate([row] * 8, axis=0).T[:, :1]


def masks(me, row, half, freq, cos, sin, augk, augq):
    n = me.nt * half
    part = lambda core: jnp.concatenate(
        [row[:, (2 * z + core) * half : (2 * z + core + 1) * half] for z in range(me.nt)], axis=1
    ).astype(F32)
    even, odd = part(0), part(1)
    seg_q, seg_o = jnp.where(me.core == 0, even, odd), jnp.where(me.core == 0, odd, even)
    whole = jnp.concatenate([seg_q, seg_o], axis=1)
    mine = column(seg_q)
    spot = lax.broadcasted_iota(jnp.int32, (n, 1), 0)
    spot = spot + (spot // half) * half + me.core * half
    first = jnp.zeros((n, 1), F32)
    for s in range(SEGS - 2):
        count = jnp.sum((whole == s).astype(F32), axis=1, keepdims=True)
        first = first + jnp.where(mine > s, count, 0.0)
    angle = (spot.astype(F32) - first) * freq[...]
    cos[...] = jnp.cos(angle)
    sines = jnp.sin(angle)
    lane = lax.broadcasted_iota(jnp.int32, sines.shape, 1)
    sin[...] = jnp.where(lane % HD < HD // 2, -sines, sines)
    for s, seg in enumerate((mine, column(seg_o))):
        ids = lax.broadcasted_iota(jnp.int32, (n, 2 * HD), 1) % HD
        hot = jnp.logical_or(seg == ids.astype(F32), jnp.logical_and(ids >= SEGS, ids < SEGS + 3))
        augk[s * n : (s + 1) * n, :] = jnp.where(hot, 1.0, 0.0).astype(BF)
    ids = lax.broadcasted_iota(jnp.int32, (HD, n), 0)
    off = jnp.logical_and(ids < SEGS, seg_q != ids.astype(F32))
    augq[...] = jnp.where(off, -BIG, 0.0).astype(BF)


def front_kernel(
    ndp, nt,
    w_qkv, w_out, w_in, w_down, gains_in, hid_in, cot_in, seg, freq,
    hid, cot, all_two, q, k, v, k2, v2, n1, wf, mixed, lse, cos, sin, augk, augq, gains,
    w1, w2, all_one, seg_o, raw, s1, r1, s2, r2, own, se, re, sc, rc, ss,
):
    n, d = hid.shape
    el, fl = w_qkv.shape[2], w_in.shape[2]
    r = w_qkv.shape[1]
    half = n // nt
    me = Place(ndp, nt)
    me.barrier(True)
    first = Gather(me, w1, all_one, s1, r1, own.at[0])
    second = Gather(me, w2, all_two, s2, r2, own.at[1])
    hs, he = enter_copies(me, hid_in, hid, se, re)
    cs, ce = enter_copies(me, cot_in, cot, sc, rc)
    buddy = me.pair(1 - me.core, me.z)
    swap = remote(seg, seg_o, ss.at[0], ss.at[3], buddy)
    swap.start()
    for c in range(3):
        w1[:, c * el : (c + 1) * el] = w_qkv[c]
    cols = jnp.concatenate([gains_in[...].astype(F32), jnp.zeros((SPARE - 2, r), F32)], axis=0)
    w1[:, 3 * el :] = cols.T.astype(BF)
    first.start_z()
    start_all(hs)
    two, three = 2 * fl, 2 * fl + el
    w2[:, :fl] = w_in[0]
    w2[:, fl:two] = w_in[1]
    w2[:, two:three] = w_out[...].astype(F32).T.astype(BF)
    w2[:, three:] = w_down[...].astype(F32).T.astype(BF)
    blocks = range(nt)
    for s in blocks:
        first.after_z(s)
    swap.wait()
    here = me.z // 2 == me.core
    index = me.z % 2
    both = jnp.where(here, seg[...], seg_o[...])
    row = jnp.where(index == 0, both[:1], both[1:2])
    masks(me, row, half, freq, cos, sin, augk, augq)
    for s in blocks:
        first.after_one(s)
    for e in he:
        e.wait_recv()
    second.start_z()

    def spread(at):
        raw[at, :] = standard(hid[at, :].astype(F32))[0]

    rows_loop(n, 64, spread)
    for s in blocks:
        first.after_two(s)
    first.finish()
    second.after_z(0)
    top = all_one[:, :, :, 0, :, 3 * el :].reshape(d, SPARE).astype(F32).T
    gains[...] = top
    gain = top[:1]

    def norm(at):
        n1[at, :] = (raw[at, :] * gain).astype(BF)

    rows_loop(n, 64, norm)
    for t in range(nt):
        for c in range(3):
            block = all_one[:, :, :, t, :, c * el : (c + 1) * el]
            wf[:, c * d + t * el : c * d + (t + 1) * el] = block.reshape(d, el)
    swaps = [remote(k, k2, ss.at[1], ss.at[4], buddy), remote(v, v2, ss.at[2], ss.at[5], buddy)]
    for c, out in ((1, k), (2, v), (0, q)):
        raw[...] = dot(n1[...], wf[:, c * d : (c + 1) * d])

        def finish(at, c=c, out=out):
            for j in range(0, d, 128):
                value = raw[at, j : j + 128]
                if c < 2:
                    value = turned(value, cos[at, :], sin[at, :])
                out[at, j : j + 128] = value.astype(BF)

        rows_loop(n, 64, finish)
        if c:
            swaps[c - 1].start()
            second.after_z(c)
    for s in swaps:
        s.wait()
    for s in range(3, nt):
        second.after_z(s)
    start_all(cs)
    pairs = d // (2 * HD)

    def attend(begin, end):
        def step(i, carry):
            attend_pair(i, q, k, k2, v, v2, augk, augq, mixed, lse)
            return carry

        lax.fori_loop(begin, end, step, 0)

    attend(0, pairs // 6)
    second.after_one(0)
    second.after_one(1)
    attend(pairs // 6, pairs // 2)
    for s in range(2, nt):
        second.after_one(s)
    attend(pairs // 2, pairs * 2 // 3)
    second.after_two(0)
    attend(pairs * 2 // 3, pairs)
    for s in range(1, nt):
        second.after_two(s)
    for e in ce:
        e.wait_recv()
    second.finish()
    wait_sends(hs)
    wait_sends(cs)


def front(ndp, nt, w_qkv, w_out, w_in, w_down, gains, hid, cot, seg):
    half, d = hid.shape[2:]
    n = nt * half
    r, el, fl = w_qkv.shape[1], w_qkv.shape[2], w_in.shape[2]
    c1, c2 = 3 * el + SPARE, 2 * fl + el + fl
    freq = jnp.tile(THETA ** (-2.0 * jnp.arange(HD // 2, dtype=F32) / HD), 4)[None]
    sds = jax.ShapeDtypeStruct
    dma = pltpu.SemaphoreType.DMA
    vm, hbm = pl.BlockSpec(memory_space=VM), pl.BlockSpec(memory_space=pl.ANY)
    act = sds((n, d), BF)
    return pl.pallas_call(
        functools.partial(front_kernel, ndp, nt),
        in_specs=[vm] * 5 + [hbm] * 2 + [vm] * 2,
        out_specs=[vm, hbm, hbm] + [vm] * 14,
        out_shape=[act, act, sds((2, 2, 2, nt, r, c2), BF)]
        + [act] * 6
        + [sds((d, 3 * d), BF), act, sds((d // (2 * HD), 2, n), F32)]
        + [sds((n, 2 * HD), F32)] * 2
        + [sds((2 * n, 2 * HD), BF), sds((HD, n), BF), sds((SPARE, d), F32)],
        scratch_shapes=[
            VM((r, c1), BF),
            VM((r, c2), BF),
            VM((2, 2, 2, nt, r, c1), BF),
            VM(seg.shape, seg.dtype),
            VM((n, d), F32),
        ]
        + [dma((nt, 6))] * 4
        + [dma((2,))]
        + [dma((4,))] * 4
        + [dma((6,))],
        compiler_params=pltpu.CompilerParams(
            collective_id=0, has_side_effects=True, vmem_limit_bytes=WIDE
        ),
        name="front",
    )(w_qkv, w_out, w_in, w_down, gains, hid, cot, seg, freq)


def split_rows(value, n, rows):
    parts = []
    for _ in range(n):
        part = value.astype(BF).astype(F32)
        parts.append(part)
        value = value - part
    parts.append(jnp.zeros((rows - n, value.shape[1]), F32))
    return jnp.concatenate(parts, axis=0).astype(BF)


def attend_back_pair(i, q, k, k2, v, v2, g, mixed, lse, augk, augq, gq, gk, gk2, gv, gv2):
    at = pl.ds(pl.multiple_of(i * 2 * HD, 2 * HD), 2 * HD)
    rows = q.shape[0]
    grads, query = g[:, at], q[:, at]
    gt, qt = grads.T, query.T
    prod = gt.astype(F32) * mixed[:, at].T.astype(F32)
    gq_parts = []
    sides = [(k, v, gk, gv), (k2, v2, gk2, gv2)]
    low = half_lanes((rows, 2 * HD))
    one = jnp.ones((rows, 2 * HD), BF)
    held = {}
    for h in range(2):
        mine = slice(h * HD, (h + 1) * HD)

        def swapped(a, b, h=h):
            return (a, b) if h == 0 else (b, a)

        inner = jnp.sum(prod[mine], axis=0, keepdims=True)
        neg = split_rows(-lse[i, h : h + 1, :], 3, SEGS)
        extra_q = jnp.concatenate([augq[:SEGS], neg, augq[2 * SEGS :]], axis=0)
        extra_g = jnp.concatenate([split_rows(-inner, 2, 8), jnp.zeros((HD - 8, rows), BF)], axis=0)
        q_h = jnp.concatenate(swapped(qt[mine], extra_q), axis=0)
        g_h = jnp.concatenate(swapped(gt[mine], extra_g), axis=0)
        gq_h = None
        for s, (kr, vr, _, _) in enumerate(sides):
            aug = augk[s * rows : (s + 1) * rows, :]
            keys, values = kr[:, at], vr[:, at]
            probs = jnp.exp2(dot(jnp.where(low, *swapped(keys, aug)), q_h) * TO_EXP2)
            grad_p = dot(jnp.where(low, *swapped(values, one)), g_h)
            held[h, s, "v"] = dot(probs.astype(BF), grads)
            ds = (probs * grad_p).astype(BF)
            held[h, s, "k"] = dot(ds, query)
            part = dot(keys.T[mine], ds)
            gq_h = part if gq_h is None else gq_h + part
        gq_parts.append(gq_h)
    scale = 1.0 / math.sqrt(HD)
    gq[:, at] = jnp.concatenate(gq_parts, axis=0).T * scale
    for s, (_, _, gkr, gvr) in enumerate(sides):
        gkr[:, at] = (jnp.where(low, held[0, s, "k"], held[1, s, "k"]) * scale).astype(gkr.dtype)
        gvr[:, at] = jnp.where(low, held[0, s, "v"], held[1, s, "v"]).astype(gvr.dtype)


def back_kernel(
    ndp, nt,
    hid, cot, all_two, q, k, v, k2, v2, n1, wf, mixed, lse, cos, sin, augk, augq, gains,
    out_o, gin_o, grad_qkv, grad_out, grad_in, grad_down, grad_gains,
    w3, wo, wd, gate, up, gp, prod, gu, n2, low, gres, gtot, gmixed, out, ak, av, gsum, local, ss, so, ro, si, ri, *rest,
):
    n, d = hid.shape
    ff = wd.shape[1]
    el, fl = d // nt, ff // nt
    two, three = 2 * fl, 2 * fl + el
    split = (2, 2, 2, d // 8)
    g2, g1 = rest[0], rest[7]
    gin, gk2, gv2 = gmixed, low, n2
    me = Place(ndp, nt)
    load = pltpu.make_async_copy(all_two, g2, local.at[0])
    load.start()
    me.barrier(True)
    rs2 = Scatter(me, g2, rest[1:5], *rest[5:7])
    rs1 = Scatter(me, g1, rest[8:12], *rest[12:14])
    lo_s, lo_e = leave_copies(me, out, out_o, so, ro)
    gi_s, gi_e = leave_copies(me, gin, gin_o, si, ri)
    gain_one, gain_two = gains[0:1, :], gains[1:2, :]
    load.wait()
    for t in range(nt):
        w3[:, t * fl : (t + 1) * fl] = g2[:, :, :, t, :, :fl].reshape(d, fl)
        w3[:, ff + t * fl : ff + (t + 1) * fl] = g2[:, :, :, t, :, fl:two].reshape(d, fl)
        wo[:, t * el : (t + 1) * el] = g2[:, :, :, t, :, two:three].reshape(d, el)
        wd[:, t * fl : (t + 1) * fl] = g2[:, :, :, t, :, three:].reshape(d, fl)
    gres[...] = dot(mixed[...], wo[...], NT)

    def norm(at):
        value = hid[at, :].astype(F32) + gres[at, :]
        gres[at, :] = value
        n2[at, :] = (standard(value)[0] * gain_two).astype(BF)

    rows_loop(n, 64, norm)
    gate[...] = dot(n2[...], w3[:, :ff])
    up[...] = dot(n2[...], w3[:, ff:])
    gp[...] = dot(cot[...], wd[...])

    def geglu(at):
        for j in range(0, ff, 384):
            to = slice(j, j + 384)
            g, u, p = gate[at, to], up[at, to], gp[at, to]
            cdf = 0.5 + 0.5 * erf(g * math.sqrt(0.5))
            pdf = jnp.exp(-0.5 * g * g) * (1.0 / math.sqrt(2 * math.pi))
            act = g * cdf
            prod[at, to] = (act * u).astype(BF)
            gu[at, to] = (p * u * (cdf + g * pdf)).astype(BF)
            gu[at, ff + j : ff + j + 384] = (p * act).astype(BF)

    rows_loop(n, 32, geglu)
    out[...] = (gres[...] + dot(prod[...], wd[...], NT)).astype(BF)
    start_all(lo_s)
    gtot[...] = dot(gu[...], w3[...], NT)
    load_wf = pltpu.make_async_copy(wf, w3, local.at[1])
    load_wf.start()
    gsum[...] = jnp.zeros_like(gsum)

    def back_two(at):
        xhat, scale = standard(gres[at, :])
        e = gtot[at, :]
        gsum[0] += jnp.sum((e * xhat).reshape(-1, 8, d), axis=0)
        total = cot[at, :].astype(F32) + norm_back(e, xhat, scale, gain_two)
        gres[at, :] = total
        low[at, :] = total.astype(BF)

    rows_loop(n, 64, back_two)
    n2t, lowt, cott = n2[...].T, low[...].T, cot[...].T
    for t in range(nt):
        at, to = slice(t * fl, (t + 1) * fl), slice(t * el, (t + 1) * el)
        g2[:, :, :, t, :, :fl] = dot(n2t, gu[:, at]).astype(BF).reshape(*split, fl)
        g2[:, :, :, t, :, fl:two] = dot(n2t, gu[:, ff + t * fl : ff + (t + 1) * fl]).astype(BF).reshape(*split, fl)
        g2[:, :, :, t, :, two:three] = dot(lowt, mixed[:, to]).astype(BF).reshape(*split, el)
        g2[:, :, :, t, :, three:] = dot(cott, prod[:, at]).astype(BF).reshape(*split, fl)
        rs2.core[t].start()
    gmixed[...] = dot(low[...], wo[...]).astype(BF)
    rs2.add_core(0)
    rs2.add_core(1)
    blocks, pairs = range(nt), d // (2 * HD)
    gq, gk, gv = gate, up, gp

    def step(i, carry):
        attend_back_pair(i, q, k, k2, v, v2, gmixed, mixed, lse, augk, augq, gq, gk, gk2, gv, gv2)
        return carry

    lax.fori_loop(0, pairs // 6, step, 0)
    for t in range(2, nt):
        rs2.add_core(t)
    lax.fori_loop(pairs // 6, pairs * 2 // 3, step, 0)
    rs2.add_one(0)
    rs2.add_one(1)
    lax.fori_loop(pairs * 2 // 3, pairs, step, 0)
    buddy = me.pair(1 - me.core, me.z)
    swaps = [remote(gk2, ak, ss.at[0], ss.at[2], buddy), remote(gv2, av, ss.at[1], ss.at[3], buddy)]
    for s in swaps:
        s.start()
    for t in range(2, nt):
        rs2.add_one(t)
    for s in swaps:
        s.wait()
    raw = gu

    def back_rope(at):
        c, s = cos[at, :], -sin[at, :]
        for j in range(0, d, 128):
            to = slice(j, j + 128)
            raw[at, j : j + 128] = turned(gq[at, to], c, s).astype(BF)
            keys = gk[at, to] + ak[at, to].astype(F32)
            raw[at, d + j : d + j + 128] = turned(keys, c, s).astype(BF)
            raw[at, 2 * d + j : 2 * d + j + 128] = (gv[at, to] + av[at, to].astype(F32)).astype(BF)

    rows_loop(n, 32, back_rope)
    rs2.add_two(0)
    rs2.add_two(1)
    load_wf.wait()
    gtot[...] = dot(raw[...], w3[...], NT)

    def back_one(at):
        xhat, scale = standard(hid[at, :].astype(F32))
        e = gtot[at, :]
        gsum[1] += jnp.sum((e * xhat).reshape(-1, 8, d), axis=0)
        gin[at, :] = (gres[at, :] + norm_back(e, xhat, scale, gain_one)).astype(BF)

    rows_loop(n, 64, back_one)
    rows = []
    for v_ in (gsum[1], gsum[0]):
        total = jnp.sum(v_, axis=0, keepdims=True)
        upper = total.astype(BF).astype(F32)
        rows += [upper, total - upper]
    rows.append(jnp.zeros((SPARE - 4, d), F32))
    gain_cols = jnp.concatenate(rows, axis=0).T.astype(BF).reshape(*split, SPARE)
    n1t = n1[...].T
    for t in range(nt):
        for c in range(3):
            cols = raw[:, c * d + t * el : c * d + (t + 1) * el]
            g1[:, :, :, t, :, c * el : (c + 1) * el] = dot(n1t, cols).astype(BF).reshape(*split, el)
        g1[:, :, :, t, :, 3 * el :] = gain_cols
        rs1.core[t].start()
    for t in range(2, nt):
        rs2.add_two(t)
    start_all(gi_s)
    for t in blocks:
        rs1.add_core(t)
    for t in blocks:
        rs1.add_one(t)
    total = rs2.total()
    grad_in[0] = total[:, :fl]
    grad_in[1] = total[:, fl:two]
    grad_out[...] = total[:, two:three].T
    grad_down[...] = total[:, three:].T
    for t in blocks:
        rs1.add_two(t)
    total = rs1.total()
    for c in range(3):
        grad_qkv[c] = total[:, c * el : (c + 1) * el]
    tail = total[:, 3 * el :].T
    grad_gains[...] = jnp.concatenate([tail[0:1] + tail[1:2], tail[2:3] + tail[3:4]], axis=0)
    for e in lo_e + gi_e:
        e.wait_recv()
    rs2.finish()
    rs1.finish()
    wait_sends(lo_s)
    wait_sends(gi_s)


def backward(ndp, nt, half, arrays):
    hid, all_two = arrays[0], arrays[2]
    n, d = hid.shape
    r, c2 = all_two.shape[4:]
    el = d // nt
    fl = (c2 - el) // 3
    ff = fl * nt
    sds = jax.ShapeDtypeStruct
    dma = pltpu.SemaphoreType.DMA
    vm, hbm = pl.BlockSpec(memory_space=VM), pl.BlockSpec(memory_space=pl.ANY)
    specs = [vm] * len(arrays)
    specs[2] = specs[9] = hbm
    wide, act = VM((n, ff), F32), VM((n, d), BF)
    return pl.pallas_call(
        functools.partial(back_kernel, ndp, nt),
        in_specs=specs,
        out_specs=[hbm, hbm] + [vm] * 5,
        out_shape=[sds((2, 2, half, d), BF)] * 2
        + [
            sds((3, r, el), F32),
            sds((el, r), F32),
            sds((2, r, fl), F32),
            sds((fl, r), F32),
            sds((2, r), F32),
        ],
        scratch_shapes=[VM((d, 2 * ff), BF), VM((d, d), BF), VM((d, ff), BF)]
        + [wide] * 3
        + [VM((n, ff), BF), VM((n, 2 * ff), BF), act, act, VM((n, d), F32), VM((n, d), F32)]
        + [act] * 4
        + [VM((2, 8, d), F32), dma((2,)), dma((4,))]
        + [dma((4,))] * 4
        + scatter_scratch(nt, r, c2)
        + scatter_scratch(nt, r, 3 * el + SPARE),
        compiler_params=pltpu.CompilerParams(
            collective_id=1, has_side_effects=True, vmem_limit_bytes=WIDE
        ),
        name="backward",
    )(*arrays)


def finish_kernel(*refs):
    count = len(refs) // 2
    sems = refs[-1]
    copies = [pltpu.make_async_copy(refs[i], refs[count + i], sems.at[i]) for i in range(count)]
    for copy in copies:
        copy.start()
    for copy in copies:
        copy.wait()


def finish(arrays):
    hbm = pl.BlockSpec(memory_space=pl.ANY)
    count = len(arrays)
    return pl.pallas_call(
        finish_kernel,
        in_specs=[hbm] * count,
        out_specs=[hbm] * count,
        out_shape=[jax.ShapeDtypeStruct(a.shape, a.dtype) for a in arrays],
        scratch_shapes=[pltpu.SemaphoreType.DMA((count,))],
        name="finish",
    )(*arrays)


def shards(hidden_in, cotangent, segment_ids, w_qkv, w_out, w_in, w_down, norm_gains):
    ndp, nt = lax.axis_size("dp"), lax.axis_size("tensor")
    stride = ndp // 8
    rows, local_len, d = hidden_in.shape
    half = local_len // 2
    low_groups = [[h * stride + i for i in range(stride)] for h in range(8)]

    def widen(v, axis):
        if stride == 1:
            return v
        return lax.all_gather(v, "dp", axis_index_groups=low_groups, axis=axis, tiled=True)

    def narrow(v, axis):
        if stride == 1:
            return v
        return lax.psum_scatter(
            v, "dp", scatter_dimension=axis, axis_index_groups=low_groups, tiled=True
        )

    split = lambda v: v.reshape(2, 2, half, d)
    arrays = front(
        ndp, nt,
        widen(w_qkv, 1), widen(w_out, 1), widen(w_in, 1), widen(w_down, 1), widen(norm_gains, 1),
        split(hidden_in), split(cotangent), segment_ids,
    )
    layer_out, grad_input, grad_qkv, grad_out, grad_in, grad_down, grad_gains = finish(
        backward(ndp, nt, half, arrays)
    )
    back = lambda t: t.reshape(rows, local_len, d)
    return (
        back(layer_out),
        back(grad_input),
        narrow(grad_qkv, 1),
        narrow(grad_out, 1),
        narrow(grad_in, 1),
        narrow(grad_down, 1),
        narrow(grad_gains, 1),
    )


def solution(mesh):
    placed = (
        P("dp", "tensor", None),
        P("dp", "tensor", None),
        P("dp", None),
        P(None, "dp", "tensor"),
        P("tensor", "dp"),
        P(None, "dp", "tensor"),
        P("tensor", "dp"),
        P(None, "dp"),
    )
    return jax.shard_map(
        shards,
        mesh=mesh,
        in_specs=placed,
        out_specs=(
            P("dp", "tensor", None),
            P("dp", "tensor", None),
            P(None, "dp", "tensor"),
            P("tensor", "dp"),
            P(None, "dp", "tensor"),
            P("tensor", "dp"),
            P(None, "dp"),
        ),
        check_vma=False,
    )
```

```python
import functools
import math

import jax
import jax.numpy as jnp
from jax import lax
from jax.experimental import pallas as pl
from jax.experimental.pallas import tpu as pltpu
from jax.sharding import PartitionSpec as P

HD = 64
EPS = 1e-05
THETA = 160000.0
BIG = 1e30
SEGS = 8
SPARE = 8
TO_EXP2 = math.log2(math.e) / math.sqrt(HD)
MESH = pl.DeviceIdType.MESH
BF, F32 = jnp.bfloat16, jnp.float32
VM = pltpu.VMEM
WIDE = 60 * 1024 * 1024


def dot(a, b, dims=((1,), (0,))):
    return lax.dot_general(a, b, (dims, ((), ())), preferred_element_type=F32)


NT = ((1,), (1,))


def padded(n):
    return -(-n // 128) * 128


def erf(x):
    x = jnp.clip(x, -3.832506856900711, 3.832506856900711)
    s = x * x
    p = 0.00022905065861350646
    for c in (0.0034082910107109506, 0.050955695062380861, 0.18520832239976145, 1.128379143519084):
        p = p * s + c
    q = -1.1791602954361697e-7
    for c in (
        0.000023547966471313185,
        0.0010179625278914885,
        0.014070470171167667,
        0.11098505178285362,
        0.49746925110067538,
        1.0,
    ):
        q = q * s + c
    return x * p / q


class Place:
    def __init__(self, ndp, nt):
        self.nt = nt
        self.stride = ndp // 8
        self.dp, self.z = lax.axis_index("dp"), lax.axis_index("tensor")
        high = self.dp // self.stride
        self.b = (high % 2, (high // 2) % 2, high // 4)
        self.core = self.dp % 2

    def flip(self, bit):
        return (self.dp + (1 - 2 * self.b[bit]) * self.stride * 2**bit, self.z)

    def along(self, step):
        return (self.dp, (self.z + step) % self.nt)

    def pair(self, core, z):
        return (self.dp - self.core + core, z)

    def barrier(self, group):
        others = [self.along(s) for s in range(1, self.nt)]
        others += [self.flip(1), self.flip(2)]
        if group or self.stride == 1:
            others += [self.pair(1 - self.core, self.z)]
        if self.stride > 1:
            others += [self.flip(0)]
        if group:
            others += [self.pair(1 - self.core, (self.z + s) % self.nt) for s in range(1, self.nt)]
        sem = pltpu.get_barrier_semaphore()
        for device in others:
            pl.semaphore_signal(sem, inc=1, device_id=device, device_id_type=MESH)
        pl.semaphore_wait(sem, len(others))


def remote(src, dst, send, recv, device):
    return pltpu.make_async_remote_copy(
        src_ref=src, dst_ref=dst, send_sem=send, recv_sem=recv, device_id=device, device_id_type=MESH
    )


def enter_copies(me, src, dst, send, recv):
    starts, ends = [], []
    half = src.shape[2]
    slot = lambda z: dst.at[pl.ds(pl.multiple_of(z * half, half), half)]
    for row in range(2):
        for core in range(2):
            z = 2 * me.core + row
            k = 2 * row + core
            here = jnp.logical_and(z == me.z, core == me.core)
            copy = remote(src.at[row, core], slot(me.z), send.at[k], recv.at[me.z], me.pair(core, z))
            local = pltpu.make_async_copy(src.at[row, core], slot(me.z), recv.at[me.z])
            starts.append((here, copy, local))
    for z in range(me.nt):
        ends.append(remote(src.at[0, 0], slot(z), send.at[0], recv.at[z], me.pair(1 - me.core, z)))
    return starts, ends


def leave_copies(me, src, dst, send, recv):
    starts, ends = [], []
    half = dst.shape[2]
    for z in range(me.nt):
        here = jnp.logical_and(z == me.z, me.z // 2 == me.core)
        k = 2 * (me.z % 2) + me.core
        to = dst.at[me.z % 2, me.core]
        copy = remote(src.at[z * half : (z + 1) * half], to, send.at[z], recv.at[k], me.pair(me.z // 2, z))
        local = pltpu.make_async_copy(src.at[z * half : (z + 1) * half], to, recv.at[k])
        starts.append((here, copy, local))
    for k in range(4):
        ends.append(remote(src.at[:half], dst.at[k // 2, k % 2], send.at[0], recv.at[k], me.pair(1 - me.core, me.z)))
    return starts, ends


def start_all(starts):
    for here, copy, local in starts:
        pl.when(here)(local.start)
        pl.when(jnp.logical_not(here))(copy.start)


def wait_sends(starts):
    for here, copy, _ in starts:
        pl.when(jnp.logical_not(here))(copy.wait_send)


class Gather:
    def __init__(self, me, shard, out, send, recv, own):
        self.me, self.shard, self.out = me, shard, out
        b0, b1, b2 = me.b
        nt = me.nt
        both = pl.ds(0, 2)
        x, y, core = me.flip(1), me.flip(2), me.flip(0)
        o0, o1, o2 = 1 - b0, 1 - b1, 1 - b2
        self.mine = pltpu.make_async_copy(shard, out.at[b2, b1, b0, me.z], own)
        self.z, self.one, self.two, self.core = [], [], [], []
        for s in range(nt):
            t = (me.z + nt - s) % nt

            def pair(k, at, other, device, s=s, t=t):
                sems = send.at[s, k], recv.at[s, k]
                cp = remote(out.at[(*at, t)], out.at[(*at, t)], *sems, device)
                return cp, remote(out.at[(*other, t)], out.at[(*other, t)], *sems, device)

            if s:
                sems = send.at[s, 0], recv.at[s, 0]
                to, frm = out.at[b2, b1, b0, me.z], out.at[b2, b1, b0, t]
                self.z.append((remote(shard, to, *sems, me.along(s)), remote(shard, frm, *sems, me.along(s))))
            else:
                self.z.append(None)
            if s % 2 == 0:
                self.one.append(pair(1, (b2, b1, b0), (b2, o1, b0), x))
                self.two.append(pair(2, (b2, both, b0), (o2, both, b0), y))
                got_one, got_two = (b2, o1), (o2, both)
            else:
                self.one.append(pair(1, (b2, b1, b0), (o2, b1, b0), y))
                self.two.append(pair(2, (both, b1, b0), (both, o1, b0), x))
                got_one, got_two = (o2, b1), (both, o1)
            self.core.append(
                [
                    pair(3, (b2, b1, b0), (b2, b1, o0), core),
                    pair(4, (*got_one, b0), (*got_one, o0), core),
                    pair(5, (*got_two, b0), (*got_two, o0), core),
                ]
            )

    def start_z(self):
        self.mine.start()
        for cp, _ in self.z[1:]:
            cp.start()

    def after_z(self, s):
        if s:
            self.z[s][1].wait_recv()
        else:
            self.mine.wait()
        self.one[s][0].start()
        self.core[s][0][0].start()

    def after_one(self, s):
        self.one[s][1].wait_recv()
        self.two[s][0].start()
        self.core[s][1][0].start()

    def after_two(self, s):
        self.two[s][1].wait_recv()
        self.core[s][2][0].start()

    def finish(self):
        for group in self.core:
            for _, back in group:
                back.wait_recv()
        for cp, _ in self.z[1:] + self.one + self.two + sum(self.core, []):
            cp.wait_send()


class Scatter:
    def __init__(self, me, g, bufs, send, recv):
        self.me, self.g = me, g
        self.r0, self.r1, self.r2, self.rz = bufs
        b0, b1, b2 = me.b
        o0, o1, o2 = 1 - b0, 1 - b1, 1 - b2
        nt = me.nt
        both = pl.ds(0, 2)
        x, y, core = me.flip(1), me.flip(2), me.flip(0)
        self.core, self.one, self.two, self.z, self.back = [], [], [], [], []
        for t in range(nt):
            sems = [(send.at[t, k], recv.at[t, k]) for k in range(3)]
            one, two = (g.at[both, o1, b0, t], g.at[o2, b1, b0, t]), (x, y)
            if t % 2:
                one, two = (g.at[o2, both, b0, t], g.at[b2, o1, b0, t]), (y, x)
            self.core.append(remote(g.at[both, both, o0, t], self.r0.at[t], *sems[0], core))
            self.one.append(remote(one[0], self.r1.at[t], *sems[1], two[0]))
            self.two.append(remote(one[1], self.r2.at[t], *sems[2], two[1]))
            slot = (t - me.z + nt - 1) % nt
            slot = jnp.minimum(slot, nt - 2)
            self.z.append(
                remote(g.at[b2, b1, b0, t], self.rz.at[slot], send.at[t, 3], recv.at[slot, 3], (me.dp, t))
            )
        for s in range(nt - 1):
            self.back.append(
                remote(g.at[b2, b1, b0, 0], self.rz.at[s], send.at[s, 3], recv.at[s, 3], me.along(1))
            )

    def add(self, at, got):
        self.g[at] = (self.g[at].astype(F32) + got.astype(F32)).astype(BF)

    def add_core(self, t):
        self.core[t].wait_recv()
        for a in range(2):
            for b in range(2):
                self.add((a, b, self.me.b[0], t), self.r0[t, a, b])
        self.one[t].start()

    def add_one(self, t):
        b0, b1, b2 = self.me.b
        self.one[t].wait_recv()
        for a in range(2):
            self.add((b2, a, b0, t) if t % 2 else (a, b1, b0, t), self.r1[t, a])
        self.two[t].start()

    def add_two(self, t):
        b0, b1, b2 = self.me.b
        self.two[t].wait_recv()
        self.add((b2, b1, b0, t), self.r2[t])
        pl.when(self.me.z != t)(self.z[t].start)

    def total(self):
        b0, b1, b2 = self.me.b
        total = self.g[b2, b1, b0, self.me.z].astype(F32)
        for s in range(self.me.nt - 1):
            self.back[s].wait_recv()
            total = total + self.rz[s].astype(F32)
        return total

    def finish(self):
        for cp in self.core + self.one + self.two:
            cp.wait_send()
        for t, cp in enumerate(self.z):
            pl.when(self.me.z != t)(cp.wait_send)


def scatter_scratch(nt, r, c):
    dma = pltpu.SemaphoreType.DMA
    return [
        VM((2, 2, 2, nt, r, c), BF),
        VM((nt, 2, 2, r, c), BF),
        VM((nt, 2, r, c), BF),
        VM((nt, r, c), BF),
        VM((nt - 1, r, c), BF),
        dma((nt, 4)),
        dma((nt, 4)),
    ]


def standard(v):
    centred = v - jnp.mean(v, axis=-1, keepdims=True)
    scale = lax.rsqrt(jnp.mean(centred * centred, axis=-1, keepdims=True) + EPS)
    return centred * scale, scale


def norm_back(grad, xhat, scale, gain):
    e = grad * gain
    inner = jnp.mean(e * xhat, axis=-1, keepdims=True)
    return scale * (e - jnp.mean(e, axis=-1, keepdims=True) - xhat * inner)


def rows_loop(total, step, body):
    def run(i, carry):
        body(pl.ds(pl.multiple_of(i * step, step), step))
        return carry

    lax.fori_loop(0, total // step, run, 0)


def turned(v, cosine, sine):
    lane = lax.broadcasted_iota(jnp.int32, v.shape, 1)
    other = jnp.where(lane % HD < HD // 2, pltpu.roll(v, 128 - HD // 2, 1), pltpu.roll(v, HD // 2, 1))
    return v * cosine + other * sine


def half_lanes(shape):
    return lax.broadcasted_iota(jnp.int32, shape, 1) < HD


def attend_pair(i, q, k, k2, v, v2, augk, augq, mixed, lse):
    at = pl.ds(pl.multiple_of(i * 2 * HD, 2 * HD), 2 * HD)
    keys = jnp.concatenate([k[:, at], k2[:, at]], axis=0)
    vt = jnp.concatenate([v[:, at], v2[:, at]], axis=0).T
    qt = q[:, at].T
    low = half_lanes(keys.shape)
    ones = jnp.ones((HD, vt.shape[1]), BF)
    outs = []
    for h in range(2):
        if h == 0:
            keys_h = jnp.where(low, keys, augk[...])
            q_h = jnp.concatenate([qt[:HD], augq[...]], axis=0)
            v_h = jnp.concatenate([vt[:HD], ones], axis=0)
        else:
            keys_h = jnp.where(low, augk[...], keys)
            q_h = jnp.concatenate([augq[...], qt[HD:]], axis=0)
            v_h = jnp.concatenate([ones, vt[HD:]], axis=0)
        scores = dot(keys_h, q_h)
        top = jnp.max(scores, axis=0, keepdims=True)
        expo = jnp.exp2((scores - top) * TO_EXP2).astype(BF)
        got = dot(v_h, expo)
        value, total = (got[:HD], got[HD:]) if h == 0 else (got[HD:], got[:HD])
        outs.append(value / total)
        lse[i, h : h + 1, :] = top + jnp.log2(total[:1]) * (1.0 / TO_EXP2)
    mixed[:, at] = jnp.concatenate(outs, axis=0).T.astype(BF)


def column(row):
    return jnp.concatenate([row] * 8, axis=0).T[:, :1]


def masks(me, row, half, freq, cos, sin, augk, augq):
    n = me.nt * half
    part = lambda core: jnp.concatenate(
        [row[:, (2 * z + core) * half : (2 * z + core + 1) * half] for z in range(me.nt)], axis=1
    ).astype(F32)
    even, odd = part(0), part(1)
    seg_q, seg_o = jnp.where(me.core == 0, even, odd), jnp.where(me.core == 0, odd, even)
    whole = jnp.concatenate([seg_q, seg_o], axis=1)
    mine = column(seg_q)
    spot = lax.broadcasted_iota(jnp.int32, (n, 1), 0)
    spot = spot + (spot // half) * half + me.core * half
    first = jnp.zeros((n, 1), F32)
    for s in range(SEGS - 2):
        count = jnp.sum((whole == s).astype(F32), axis=1, keepdims=True)
        first = first + jnp.where(mine > s, count, 0.0)
    angle = (spot.astype(F32) - first) * freq[...]
    cos[...] = jnp.cos(angle)
    sines = jnp.sin(angle)
    lane = lax.broadcasted_iota(jnp.int32, sines.shape, 1)
    sin[...] = jnp.where(lane % HD < HD // 2, -sines, sines)
    for s, seg in enumerate((mine, column(seg_o))):
        ids = lax.broadcasted_iota(jnp.int32, (n, 2 * HD), 1) % HD
        hot = jnp.logical_or(seg == ids.astype(F32), jnp.logical_and(ids >= SEGS, ids < SEGS + 3))
        augk[s * n : (s + 1) * n, :] = jnp.where(hot, 1.0, 0.0).astype(BF)
    ids = lax.broadcasted_iota(jnp.int32, (HD, n), 0)
    off = jnp.logical_and(ids < SEGS, seg_q != ids.astype(F32))
    augq[...] = jnp.where(off, -BIG, 0.0).astype(BF)


def front_kernel(
    ndp, nt,
    w_qkv, w_out, w_in, w_down, gains_in, hid_in, cot_in, seg, freq,
    hid, cot, all_two, q, k, v, k2, v2, n1, wf, mixed, lse, cos, sin, augk, augq, gains,
    w1, w2, all_one, seg_o, raw, s1, r1, s2, r2, own, se, re, sc, rc, ss,
):
    n, d = hid.shape
    el, fl = w_qkv.shape[2], w_in.shape[2]
    r = w_qkv.shape[1]
    half = n // nt
    me = Place(ndp, nt)
    me.barrier(True)
    first = Gather(me, w1, all_one, s1, r1, own.at[0])
    second = Gather(me, w2, all_two, s2, r2, own.at[1])
    hs, he = enter_copies(me, hid_in, hid, se, re)
    cs, ce = enter_copies(me, cot_in, cot, sc, rc)
    buddy = me.pair(1 - me.core, me.z)
    swap = remote(seg, seg_o, ss.at[0], ss.at[3], buddy)
    swap.start()
    for c in range(3):
        w1[:, c * el : (c + 1) * el] = w_qkv[c]
    spare = w1.shape[1] - 3 * el
    cols = jnp.concatenate([gains_in[...].astype(F32), jnp.zeros((spare - 2, r), F32)], axis=0)
    w1[:, 3 * el :] = cols.T.astype(BF)
    first.start_z()
    start_all(hs)
    w2[...] = jnp.zeros_like(w2)
    w2[:, :fl] = w_in[0]
    w2[:, fl : 2 * fl] = w_in[1]
    w2[:, 2 * fl : 3 * fl] = w_down[...].astype(F32).T.astype(BF)
    w2[:, padded(3 * fl) : padded(3 * fl) + el] = w_out[...].astype(F32).T.astype(BF)
    blocks = range(nt)
    for s in blocks:
        first.after_z(s)
    swap.wait()
    here = me.z // 2 == me.core
    index = me.z % 2
    both = jnp.where(here, seg[...], seg_o[...])
    row = jnp.where(index == 0, both[:1], both[1:2])
    masks(me, row, half, freq, cos, sin, augk, augq)
    for s in blocks:
        first.after_one(s)
    for e in he:
        e.wait_recv()
    second.start_z()

    def spread(at):
        raw[at, :] = standard(hid[at, :].astype(F32))[0]

    rows_loop(n, 64, spread)
    for s in blocks:
        first.after_two(s)
    first.finish()
    second.after_z(0)
    top = all_one[:, :, :, 0, :, 3 * el : 3 * el + SPARE].reshape(d, SPARE).astype(F32).T
    gains[...] = top
    gain = top[:1]

    def norm(at):
        n1[at, :] = (raw[at, :] * gain).astype(BF)

    rows_loop(n, 64, norm)
    for t in range(nt):
        for c in range(3):
            block = all_one[:, :, :, t, :, c * el : (c + 1) * el]
            wf[:, c * d + t * el : c * d + (t + 1) * el] = block.reshape(d, el)
    swaps = [remote(k, k2, ss.at[1], ss.at[4], buddy), remote(v, v2, ss.at[2], ss.at[5], buddy)]
    for c, out in ((1, k), (2, v), (0, q)):
        raw[...] = dot(n1[...], wf[:, c * d : (c + 1) * d])

        def finish(at, c=c, out=out):
            for j in range(0, d, 128):
                value = raw[at, j : j + 128]
                if c < 2:
                    value = turned(value, cos[at, :], sin[at, :])
                out[at, j : j + 128] = value.astype(BF)

        rows_loop(n, 64, finish)
        if c:
            swaps[c - 1].start()
            second.after_z(c)
    for s in swaps:
        s.wait()
    for s in range(3, nt):
        second.after_z(s)
    start_all(cs)
    pairs = d // (2 * HD)

    def attend(begin, end):
        def step(i, carry):
            attend_pair(i, q, k, k2, v, v2, augk, augq, mixed, lse)
            return carry

        lax.fori_loop(begin, end, step, 0)

    attend(0, pairs // 6)
    second.after_one(0)
    second.after_one(1)
    attend(pairs // 6, pairs // 2)
    for s in range(2, nt):
        second.after_one(s)
    attend(pairs // 2, pairs * 2 // 3)
    second.after_two(0)
    attend(pairs * 2 // 3, pairs)
    for s in range(1, nt):
        second.after_two(s)
    for e in ce:
        e.wait_recv()
    second.finish()
    wait_sends(hs)
    wait_sends(cs)


def front(ndp, nt, w_qkv, w_out, w_in, w_down, gains, hid, cot, seg):
    half, d = hid.shape[2:]
    n = nt * half
    r, el, fl = w_qkv.shape[1], w_qkv.shape[2], w_in.shape[2]
    c1, c2 = padded(3 * el + SPARE), padded(3 * fl) + padded(el)
    freq = jnp.tile(THETA ** (-2.0 * jnp.arange(HD // 2, dtype=F32) / HD), 4)[None]
    sds = jax.ShapeDtypeStruct
    dma = pltpu.SemaphoreType.DMA
    vm, hbm = pl.BlockSpec(memory_space=VM), pl.BlockSpec(memory_space=pl.ANY)
    act = sds((n, d), BF)
    return pl.pallas_call(
        functools.partial(front_kernel, ndp, nt),
        in_specs=[vm] * 5 + [hbm] * 2 + [vm] * 2,
        out_specs=[vm, hbm, hbm] + [vm] * 14,
        out_shape=[act, act, sds((2, 2, 2, nt, r, c2), BF)]
        + [act] * 6
        + [sds((d, 3 * d), BF), act, sds((d // (2 * HD), 2, n), F32)]
        + [sds((n, 2 * HD), F32)] * 2
        + [sds((2 * n, 2 * HD), BF), sds((HD, n), BF), sds((SPARE, d), F32)],
        scratch_shapes=[
            VM((r, c1), BF),
            VM((r, c2), BF),
            VM((2, 2, 2, nt, r, c1), BF),
            VM(seg.shape, seg.dtype),
            VM((n, d), F32),
        ]
        + [dma((nt, 6))] * 4
        + [dma((2,))]
        + [dma((4,))] * 4
        + [dma((6,))],
        compiler_params=pltpu.CompilerParams(
            collective_id=0, has_side_effects=True, vmem_limit_bytes=WIDE
        ),
        name="front",
    )(w_qkv, w_out, w_in, w_down, gains, hid, cot, seg, freq)


def split_rows(value, n, rows):
    parts = []
    for _ in range(n):
        part = value.astype(BF).astype(F32)
        parts.append(part)
        value = value - part
    parts.append(jnp.zeros((rows - n, value.shape[1]), F32))
    return jnp.concatenate(parts, axis=0).astype(BF)


def attend_back_pair(i, q, k, k2, v, v2, g, mixed, lse, augk, augq, gq, gk, gk2, gv, gv2):
    at = pl.ds(pl.multiple_of(i * 2 * HD, 2 * HD), 2 * HD)
    rows = q.shape[0]
    grads, query = g[:, at], q[:, at]
    gt, qt = grads.T, query.T
    prod = gt.astype(F32) * mixed[:, at].T.astype(F32)
    gq_parts = []
    sides = [(k, v, gk, gv), (k2, v2, gk2, gv2)]
    low = half_lanes((rows, 2 * HD))
    one = jnp.ones((rows, 2 * HD), BF)
    held = {}
    for h in range(2):
        mine = slice(h * HD, (h + 1) * HD)

        def swapped(a, b, h=h):
            return (a, b) if h == 0 else (b, a)

        inner = jnp.sum(prod[mine], axis=0, keepdims=True)
        neg = split_rows(-lse[i, h : h + 1, :], 3, SEGS)
        extra_q = jnp.concatenate([augq[:SEGS], neg, augq[2 * SEGS :]], axis=0)
        extra_g = jnp.concatenate([split_rows(-inner, 2, 8), jnp.zeros((HD - 8, rows), BF)], axis=0)
        q_h = jnp.concatenate(swapped(qt[mine], extra_q), axis=0)
        g_h = jnp.concatenate(swapped(gt[mine], extra_g), axis=0)
        gq_h = None
        for s, (kr, vr, _, _) in enumerate(sides):
            aug = augk[s * rows : (s + 1) * rows, :]
            keys, values = kr[:, at], vr[:, at]
            probs = jnp.exp2(dot(jnp.where(low, *swapped(keys, aug)), q_h) * TO_EXP2)
            grad_p = dot(jnp.where(low, *swapped(values, one)), g_h)
            held[h, s, "v"] = dot(probs.astype(BF), grads)
            ds = (probs * grad_p).astype(BF)
            held[h, s, "k"] = dot(ds, query)
            part = dot(keys.T[mine], ds)
            gq_h = part if gq_h is None else gq_h + part
        gq_parts.append(gq_h)
    scale = 1.0 / math.sqrt(HD)
    gq[:, at] = jnp.concatenate(gq_parts, axis=0).T * scale
    for s, (_, _, gkr, gvr) in enumerate(sides):
        gkr[:, at] = (jnp.where(low, held[0, s, "k"], held[1, s, "k"]) * scale).astype(gkr.dtype)
        gvr[:, at] = jnp.where(low, held[0, s, "v"], held[1, s, "v"]).astype(gvr.dtype)


def back_kernel(
    ndp, nt,
    hid, cot, all_two, q, k, v, k2, v2, n1, wf, mixed, lse, cos, sin, augk, augq, gains,
    out_o, gin_o, grad_qkv, grad_out, grad_in, grad_down, grad_gains,
    w3, wo, wd, gate, up, gp, prod, gu, n2, low, gres, gtot, gmixed, out, ak, av, gsum, rgain,
    local, ss, so, ro, si, ri, sg, rg, *rest,
):
    n, d = hid.shape
    ff = wd.shape[1]
    el, fl = d // nt, ff // nt
    split = (2, 2, 2, d // 8)
    g2, g3, g1 = rest[0], rest[7], rest[14]
    gin, gk2, gv2 = gmixed, low, n2
    me = Place(ndp, nt)
    b0, b1, b2 = me.b
    ca, cb = g2.shape[5], g3.shape[5]
    loads = [
        pltpu.make_async_copy(all_two.at[:, :, :, :, :, pl.ds(0, ca)], g2, local.at[0]),
        pltpu.make_async_copy(all_two.at[:, :, :, :, :, pl.ds(ca, cb)], g3, local.at[1]),
    ]
    for load in loads:
        load.start()
    me.barrier(True)
    rs2 = Scatter(me, g2, rest[1:5], *rest[5:7])
    rs3 = Scatter(me, g3, rest[8:12], *rest[12:14])
    rs1 = Scatter(me, g1, rest[15:19], *rest[19:21])
    lo_s, lo_e = leave_copies(me, out, out_o, so, ro)
    gi_s, gi_e = leave_copies(me, gin, gin_o, si, ri)
    gain_one, gain_two = gains[0:1, :], gains[1:2, :]
    for load in loads:
        load.wait()
    blocks, pairs = range(nt), d // (2 * HD)
    for t in blocks:
        at = slice(t * fl, (t + 1) * fl)
        wo[:, t * el : (t + 1) * el] = g3[:, :, :, t, :, :el].reshape(d, el)
        w3[:, at] = g2[:, :, :, t, :, :fl].reshape(d, fl)
        w3[:, ff + t * fl : ff + (t + 1) * fl] = g2[:, :, :, t, :, fl : 2 * fl].reshape(d, fl)
        wd[:, at] = g2[:, :, :, t, :, 2 * fl : 3 * fl].reshape(d, fl)
    gres[...] = dot(mixed[...], wo[...], NT)

    def norm(at):
        value = hid[at, :].astype(F32) + gres[at, :]
        gres[at, :] = value
        n2[at, :] = (standard(value)[0] * gain_two).astype(BF)

    rows_loop(n, 64, norm)
    gate[...] = dot(n2[...], w3[:, :ff])
    up[...] = dot(n2[...], w3[:, ff:])
    gp[...] = dot(cot[...], wd[...])

    def geglu(at):
        for j in range(0, ff, 384):
            to = slice(j, j + 384)
            g, u, p = gate[at, to], up[at, to], gp[at, to]
            cdf = 0.5 + 0.5 * erf(g * math.sqrt(0.5))
            pdf = jnp.exp(-0.5 * g * g) * (1.0 / math.sqrt(2 * math.pi))
            act = g * cdf
            prod[at, to] = (act * u).astype(BF)
            gu[at, to] = (p * u * (cdf + g * pdf)).astype(BF)
            gu[at, ff + j : ff + j + 384] = (p * act).astype(BF)

    rows_loop(n, 32, geglu)
    n2t, cott = n2[...].T, cot[...].T
    for t in blocks:
        at = slice(t * fl, (t + 1) * fl)
        also = slice(ff + t * fl, ff + (t + 1) * fl)
        g2[:, :, :, t, :, :fl] = dot(n2t, gu[:, at]).astype(BF).reshape(*split, fl)
        g2[:, :, :, t, :, fl : 2 * fl] = dot(n2t, gu[:, also]).astype(BF).reshape(*split, fl)
        g2[:, :, :, t, :, 2 * fl : 3 * fl] = dot(cott, prod[:, at]).astype(BF).reshape(*split, fl)
        rs2.core[t].start()
    out[...] = (gres[...] + dot(prod[...], wd[...], NT)).astype(BF)
    start_all(lo_s)
    rs2.add_core(0)
    rs2.add_core(1)
    gtot[...] = dot(gu[...], w3[...], NT)
    load_wf = pltpu.make_async_copy(wf, w3, local.at[2])
    load_wf.start()
    gsum[...] = jnp.zeros_like(gsum)
    for t in range(2, nt):
        rs2.add_core(t)

    def back_two(at):
        xhat, scale = standard(gres[at, :])
        e = gtot[at, :]
        gsum[0] += jnp.sum((e * xhat).reshape(-1, 8, d), axis=0)
        total = cot[at, :].astype(F32) + norm_back(e, xhat, scale, gain_two)
        gres[at, :] = total
        low[at, :] = total.astype(BF)

    rows_loop(n, 64, back_two)
    lowt = low[...].T
    for t in blocks:
        to = slice(t * el, (t + 1) * el)
        g3[:, :, :, t, :, :el] = dot(lowt, mixed[:, to]).astype(BF).reshape(*split, el)
        rs3.core[t].start()
    gmixed[...] = dot(low[...], wo[...]).astype(BF)
    rs2.add_one(0)
    rs2.add_one(1)
    gq, gk, gv = gate, up, gp

    def attend(begin, end):
        def step(i, carry):
            attend_back_pair(i, q, k, k2, v, v2, gmixed, mixed, lse, augk, augq, gq, gk, gk2, gv, gv2)
            return carry

        lax.fori_loop(begin, end, step, 0)

    buddy = me.pair(1 - me.core, me.z)
    swaps = []
    for i in range(2):
        at = pl.ds(i * d // 2, d // 2)
        for j, (src, dst) in enumerate(((gk2, ak), (gv2, av))):
            m = 2 * i + j
            swaps.append(remote(src.at[:, at], dst.at[:, at], ss.at[m], ss.at[4 + m], buddy))
    raw = gu

    def back_rope(half):
        def body(at):
            c, s = cos[at, :], -sin[at, :]
            for j in range(half * d // 2, (half + 1) * d // 2, 128):
                to = slice(j, j + 128)
                raw[at, j : j + 128] = turned(gq[at, to], c, s).astype(BF)
                keys = gk[at, to] + ak[at, to].astype(F32)
                raw[at, d + j : d + j + 128] = turned(keys, c, s).astype(BF)
                raw[at, 2 * d + j : 2 * d + j + 128] = (gv[at, to] + av[at, to].astype(F32)).astype(BF)

        rows_loop(n, 32, body)

    def grads_one(n1t, t):
        for c in range(3):
            cols = raw[:, c * d + t * el : c * d + (t + 1) * el]
            g1[:, :, :, t, :, c * el : (c + 1) * el] = dot(n1t, cols).astype(BF).reshape(*split, el)

    attend(0, pairs // 6)
    for t in blocks:
        rs3.add_core(t)
    attend(pairs // 6, pairs // 2)
    for swap in swaps[:2]:
        swap.start()
    for t in range(2, nt):
        rs2.add_one(t)
    attend(pairs // 2, pairs * 2 // 3)
    for swap in swaps[:2]:
        swap.wait()
    back_rope(0)
    n1t = n1[...].T
    for t in range(nt // 2):
        grads_one(n1t, t)
        rs1.core[t].start()
    rs2.add_two(0)
    rs2.add_two(1)
    for t in blocks:
        rs3.add_one(t)
    attend(pairs * 2 // 3, pairs)
    for swap in swaps[2:]:
        swap.start()
    for t in range(nt // 2):
        rs1.add_core(t)
    for t in range(2, nt):
        rs2.add_two(t)
    for swap in swaps[2:]:
        swap.wait()
    back_rope(1)
    n1t = n1[...].T
    for t in range(nt // 2, nt - 1):
        grads_one(n1t, t)
        rs1.core[t].start()
    load_wf.wait()
    gtot[...] = dot(raw[...], w3[...], NT)
    for t in blocks:
        rs3.add_two(t)
    for t in range(nt // 2):
        rs1.add_one(t)

    def back_one(at):
        xhat, scale = standard(hid[at, :].astype(F32))
        e = gtot[at, :]
        gsum[1] += jnp.sum((e * xhat).reshape(-1, 8, d), axis=0)
        gin[at, :] = (gres[at, :] + norm_back(e, xhat, scale, gain_one)).astype(BF)

    rows_loop(n, 64, back_one)
    start_all(gi_s)
    rows = []
    for v_ in (gsum[1], gsum[0]):
        total = jnp.sum(v_, axis=0, keepdims=True)
        upper = total.astype(BF).astype(F32)
        rows += [upper, total - upper]
    rows.append(jnp.zeros((SPARE - 4, d), F32))
    gain_cols = jnp.concatenate(rows, axis=0).T.astype(BF).reshape(*split, SPARE)
    last = nt - 1
    grads_one(n1t, last)
    g1[:, :, :, last, :, 3 * el : 3 * el + SPARE] = gain_cols
    rs1.core[last].start()
    for t in range(nt // 2, nt):
        rs1.add_core(t)
    for t in range(nt // 2):
        rs1.add_two(t)
    for t in range(nt // 2, nt):
        rs1.add_one(t)
    total = rs3.total()
    grad_out[...] = total[:, :el].T
    total = rs2.total()
    grad_in[0] = total[:, :fl]
    grad_in[1] = total[:, fl : 2 * fl]
    grad_down[...] = total[:, 2 * fl : 3 * fl].T
    for t in range(nt // 2, nt):
        rs1.add_two(t)
    first = 3 * el // 128 * 128
    tile = (b2, b1, b0, last, slice(None), pl.ds(first, 128))
    gain_copies = [
        remote(g1.at[tile], rgain.at[s - 1], sg.at[s - 1], rg.at[s - 1], me.along(s)) for s in range(1, nt)
    ]
    for cp in gain_copies:
        cp.start()
    total = rs1.total()
    for c in range(3):
        grad_qkv[c] = total[:, c * el : (c + 1) * el]
    tail = g1[b2, b1, b0, last, :, first : first + 128].astype(F32)
    for s, cp in enumerate(gain_copies):
        cp.wait()
        tail = tail + rgain[s].astype(F32)
    tail = tail.T[3 * el - first : 3 * el - first + 8]
    grad_gains[...] = jnp.concatenate([tail[0:1] + tail[1:2], tail[2:3] + tail[3:4]], axis=0)
    for e in lo_e + gi_e:
        e.wait_recv()
    rs2.finish()
    rs3.finish()
    rs1.finish()
    wait_sends(lo_s)
    wait_sends(gi_s)


def backward(ndp, nt, half, fl, arrays):
    n, d = arrays[0].shape
    r = d // 8
    el, ff = d // nt, fl * nt
    c1 = padded(3 * el + SPARE)
    sds = jax.ShapeDtypeStruct
    dma = pltpu.SemaphoreType.DMA
    vm, hbm = pl.BlockSpec(memory_space=VM), pl.BlockSpec(memory_space=pl.ANY)
    specs = [vm] * len(arrays)
    specs[2] = specs[9] = hbm
    wide, act = VM((n, ff), F32), VM((n, d), BF)
    return pl.pallas_call(
        functools.partial(back_kernel, ndp, nt),
        in_specs=specs,
        out_specs=[hbm, hbm] + [vm] * 5,
        out_shape=[sds((2, 2, half, d), BF)] * 2
        + [
            sds((3, r, el), F32),
            sds((el, r), F32),
            sds((2, r, fl), F32),
            sds((fl, r), F32),
            sds((2, r), F32),
        ],
        scratch_shapes=[VM((d, 2 * ff), BF), VM((d, d), BF), VM((d, ff), BF)]
        + [wide] * 3
        + [VM((n, ff), BF), VM((n, 2 * ff), BF), act, act, VM((n, d), F32), VM((n, d), F32)]
        + [act] * 4
        + [VM((2, 8, d), F32), VM((nt - 1, r, 128), BF), dma((3,)), dma((8,))]
        + [dma((4,))] * 4
        + [dma((nt - 1,))] * 2
        + scatter_scratch(nt, r, padded(3 * fl))
        + scatter_scratch(nt, r, padded(el))
        + scatter_scratch(nt, r, c1),
        compiler_params=pltpu.CompilerParams(
            collective_id=1, has_side_effects=True, vmem_limit_bytes=WIDE
        ),
        name="backward",
    )(*arrays)


def finish_kernel(count, *refs):
    arrays, outs, held, (sems, more) = refs[:count], refs[count : 2 * count], refs[2 * count : 3 * count], refs[3 * count :]
    ins = [pltpu.make_async_copy(a, h, sems.at[i]) for i, (a, h) in enumerate(zip(arrays, held))]
    ends = [pltpu.make_async_copy(h, o, more.at[i]) for i, (h, o) in enumerate(zip(held, outs))]
    for copy in ins:
        copy.start()
    for copy, end in zip(ins, ends):
        copy.wait()
        end.start()
    for end in ends:
        end.wait()


def finish(arrays):
    hbm = pl.BlockSpec(memory_space=pl.ANY)
    count = len(arrays)
    return pl.pallas_call(
        functools.partial(finish_kernel, count),
        in_specs=[hbm] * count,
        out_specs=[hbm] * count,
        out_shape=[jax.ShapeDtypeStruct(a.shape, a.dtype) for a in arrays],
        scratch_shapes=[VM(a.shape, a.dtype) for a in arrays] + [pltpu.SemaphoreType.DMA((count,))] * 2,
        compiler_params=pltpu.CompilerParams(vmem_limit_bytes=WIDE // 4),
        name="finish",
    )(*arrays)


def shards(hidden_in, cotangent, segment_ids, w_qkv, w_out, w_in, w_down, norm_gains):
    ndp, nt = lax.axis_size("dp"), lax.axis_size("tensor")
    stride = ndp // 8
    rows, local_len, d = hidden_in.shape
    half = local_len // 2
    low_groups = [[h * stride + i for i in range(stride)] for h in range(8)]

    def widen(v, axis):
        if stride == 1:
            return v
        return lax.all_gather(v, "dp", axis_index_groups=low_groups, axis=axis, tiled=True)

    def narrow(v, axis):
        if stride == 1:
            return v
        return lax.psum_scatter(
            v, "dp", scatter_dimension=axis, axis_index_groups=low_groups, tiled=True
        )

    split = lambda v: v.reshape(2, 2, half, d)
    arrays = front(
        ndp, nt,
        widen(w_qkv, 1), widen(w_out, 1), widen(w_in, 1), widen(w_down, 1), widen(norm_gains, 1),
        split(hidden_in), split(cotangent), segment_ids,
    )
    layer_out, grad_input, grad_qkv, grad_out, grad_in, grad_down, grad_gains = finish(
        backward(ndp, nt, half, w_in.shape[2], arrays)
    )
    back = lambda t: t.reshape(rows, local_len, d)
    return (
        back(layer_out),
        back(grad_input),
        narrow(grad_qkv, 1),
        narrow(grad_out, 1),
        narrow(grad_in, 1),
        narrow(grad_down, 1),
        narrow(grad_gains, 1),
    )


def solution(mesh):
    placed = (
        P("dp", "tensor", None),
        P("dp", "tensor", None),
        P("dp", None),
        P(None, "dp", "tensor"),
        P("tensor", "dp"),
        P(None, "dp", "tensor"),
        P("tensor", "dp"),
        P(None, "dp"),
    )
    return jax.shard_map(
        shards,
        mesh=mesh,
        in_specs=placed,
        out_specs=(
            P("dp", "tensor", None),
            P("dp", "tensor", None),
            P(None, "dp", "tensor"),
            P("tensor", "dp"),
            P(None, "dp", "tensor"),
            P("tensor", "dp"),
            P(None, "dp"),
        ),
        check_vma=False,
    )
```

```python
import functools
import math

import jax
import jax.numpy as jnp
from jax import lax
from jax.experimental import pallas as pl
from jax.experimental.pallas import tpu as pltpu
from jax.sharding import PartitionSpec as P

HD = 64
EPS = 1e-05
THETA = 160000.0
BIG = 1e30
SEGS = 8
SPARE = 8
TO_EXP2 = math.log2(math.e) / math.sqrt(HD)
MESH = pl.DeviceIdType.MESH
BF, F32 = jnp.bfloat16, jnp.float32
VM = pltpu.VMEM
WIDE = 60 * 1024 * 1024


def dot(a, b, dims=((1,), (0,))):
    return lax.dot_general(a, b, (dims, ((), ())), preferred_element_type=F32)


NT = ((1,), (1,))


def padded(n):
    return -(-n // 128) * 128


def erf(x):
    x = jnp.clip(x, -3.832506856900711, 3.832506856900711)
    s = x * x
    p = 0.00022905065861350646
    for c in (0.0034082910107109506, 0.050955695062380861, 0.18520832239976145, 1.128379143519084):
        p = p * s + c
    q = -1.1791602954361697e-7
    for c in (
        0.000023547966471313185,
        0.0010179625278914885,
        0.014070470171167667,
        0.11098505178285362,
        0.49746925110067538,
        1.0,
    ):
        q = q * s + c
    return x * p / q


class Place:
    def __init__(self, ndp, nt):
        self.nt = nt
        self.stride = ndp // 8
        self.dp, self.z = lax.axis_index("dp"), lax.axis_index("tensor")
        high = self.dp // self.stride
        self.b = (high % 2, (high // 2) % 2, high // 4)
        self.core = self.dp % 2

    def flip(self, bit):
        return (self.dp + (1 - 2 * self.b[bit]) * self.stride * 2**bit, self.z)

    def along(self, step):
        return (self.dp, (self.z + step) % self.nt)

    def pair(self, core, z):
        return (self.dp - self.core + core, z)

    def barrier(self, group):
        others = [self.along(s) for s in range(1, self.nt)]
        others += [self.flip(1), self.flip(2)]
        if group or self.stride == 1:
            others += [self.pair(1 - self.core, self.z)]
        if self.stride > 1:
            others += [self.flip(0)]
        if group:
            others += [self.pair(1 - self.core, (self.z + s) % self.nt) for s in range(1, self.nt)]
        sem = pltpu.get_barrier_semaphore()
        for device in others:
            pl.semaphore_signal(sem, inc=1, device_id=device, device_id_type=MESH)
        pl.semaphore_wait(sem, len(others))


def remote(src, dst, send, recv, device):
    return pltpu.make_async_remote_copy(
        src_ref=src, dst_ref=dst, send_sem=send, recv_sem=recv, device_id=device, device_id_type=MESH
    )


def enter_copies(me, src, dst, send, recv):
    starts, ends = [], []
    half = src.shape[2]
    slot = lambda z: dst.at[pl.ds(pl.multiple_of(z * half, half), half)]
    for row in range(2):
        for core in range(2):
            z = 2 * me.core + row
            k = 2 * row + core
            here = jnp.logical_and(z == me.z, core == me.core)
            copy = remote(src.at[row, core], slot(me.z), send.at[k], recv.at[me.z], me.pair(core, z))
            local = pltpu.make_async_copy(src.at[row, core], slot(me.z), recv.at[me.z])
            starts.append((here, copy, local))
    for z in range(me.nt):
        ends.append(remote(src.at[0, 0], slot(z), send.at[0], recv.at[z], me.pair(1 - me.core, z)))
    return starts, ends


def leave_copies(me, src, dst, send, recv):
    starts, ends = [], []
    half = dst.shape[2]
    for z in range(me.nt):
        here = jnp.logical_and(z == me.z, me.z // 2 == me.core)
        k = 2 * (me.z % 2) + me.core
        to = dst.at[me.z % 2, me.core]
        copy = remote(src.at[z * half : (z + 1) * half], to, send.at[z], recv.at[k], me.pair(me.z // 2, z))
        local = pltpu.make_async_copy(src.at[z * half : (z + 1) * half], to, recv.at[k])
        starts.append((here, copy, local))
    for k in range(4):
        ends.append(remote(src.at[:half], dst.at[k // 2, k % 2], send.at[0], recv.at[k], me.pair(1 - me.core, me.z)))
    return starts, ends


def start_all(starts):
    for here, copy, local in starts:
        pl.when(here)(local.start)
        pl.when(jnp.logical_not(here))(copy.start)


def wait_sends(starts):
    for here, copy, _ in starts:
        pl.when(jnp.logical_not(here))(copy.wait_send)


class Gather:
    def __init__(self, me, shard, out, send, recv, own):
        self.me, self.shard, self.out = me, shard, out
        b0, b1, b2 = me.b
        nt = me.nt
        both = pl.ds(0, 2)
        x, y, core = me.flip(1), me.flip(2), me.flip(0)
        o0, o1, o2 = 1 - b0, 1 - b1, 1 - b2
        self.mine = pltpu.make_async_copy(shard, out.at[b2, b1, b0, me.z], own)
        self.z, self.one, self.two, self.core = [], [], [], []
        for s in range(nt):
            t = (me.z + nt - s) % nt

            def pair(k, at, other, device, s=s, t=t):
                sems = send.at[s, k], recv.at[s, k]
                cp = remote(out.at[(*at, t)], out.at[(*at, t)], *sems, device)
                return cp, remote(out.at[(*other, t)], out.at[(*other, t)], *sems, device)

            if s:
                sems = send.at[s, 0], recv.at[s, 0]
                to, frm = out.at[b2, b1, b0, me.z], out.at[b2, b1, b0, t]
                self.z.append((remote(shard, to, *sems, me.along(s)), remote(shard, frm, *sems, me.along(s))))
            else:
                self.z.append(None)
            if s % 2 == 0:
                self.one.append(pair(1, (b2, b1, b0), (b2, o1, b0), x))
                self.two.append(pair(2, (b2, both, b0), (o2, both, b0), y))
                got_one, got_two = (b2, o1), (o2, both)
            else:
                self.one.append(pair(1, (b2, b1, b0), (o2, b1, b0), y))
                self.two.append(pair(2, (both, b1, b0), (both, o1, b0), x))
                got_one, got_two = (o2, b1), (both, o1)
            self.core.append(
                [
                    pair(3, (b2, b1, b0), (b2, b1, o0), core),
                    pair(4, (*got_one, b0), (*got_one, o0), core),
                    pair(5, (*got_two, b0), (*got_two, o0), core),
                ]
            )

    def start_z(self):
        self.mine.start()
        for cp, _ in self.z[1:]:
            cp.start()

    def after_z(self, s):
        if s:
            self.z[s][1].wait_recv()
        else:
            self.mine.wait()
        self.one[s][0].start()
        self.core[s][0][0].start()

    def after_one(self, s):
        self.one[s][1].wait_recv()
        self.two[s][0].start()
        self.core[s][1][0].start()

    def after_two(self, s):
        self.two[s][1].wait_recv()
        self.core[s][2][0].start()

    def finish(self):
        for group in self.core:
            for _, back in group:
                back.wait_recv()
        for cp, _ in self.z[1:] + self.one + self.two + sum(self.core, []):
            cp.wait_send()


class Scatter:
    def __init__(self, me, g, bufs, send, recv):
        self.me, self.g = me, g
        self.r0, self.r1, self.r2, self.rz = bufs
        b0, b1, b2 = me.b
        o0, o1, o2 = 1 - b0, 1 - b1, 1 - b2
        nt = me.nt
        both = pl.ds(0, 2)
        x, y, core = me.flip(1), me.flip(2), me.flip(0)
        self.core, self.one, self.two, self.z, self.back = [], [], [], [], []
        for t in range(nt):
            sems = [(send.at[t, k], recv.at[t, k]) for k in range(3)]
            one, two = (g.at[both, o1, b0, t], g.at[o2, b1, b0, t]), (x, y)
            if t % 2:
                one, two = (g.at[o2, both, b0, t], g.at[b2, o1, b0, t]), (y, x)
            self.core.append(remote(g.at[both, both, o0, t], self.r0.at[t], *sems[0], core))
            self.one.append(remote(one[0], self.r1.at[t], *sems[1], two[0]))
            self.two.append(remote(one[1], self.r2.at[t], *sems[2], two[1]))
            slot = (t - me.z + nt - 1) % nt
            slot = jnp.minimum(slot, nt - 2)
            self.z.append(
                remote(g.at[b2, b1, b0, t], self.rz.at[slot], send.at[t, 3], recv.at[slot, 3], (me.dp, t))
            )
        for s in range(nt - 1):
            self.back.append(
                remote(g.at[b2, b1, b0, 0], self.rz.at[s], send.at[s, 3], recv.at[s, 3], me.along(1))
            )

    def add(self, count, at, buf, got):
        tiles = self.g.shape[4] // 32

        def body(i, carry):
            rows = pl.ds(pl.multiple_of(i % tiles * 32, 32), 32)
            here, there = (*at(i // tiles), rows), (*got(i // tiles), rows)
            self.g[here] = (self.g[here].astype(F32) + buf[there].astype(F32)).astype(BF)
            return carry

        lax.fori_loop(0, count * tiles, body, 0)

    def add_core(self, t):
        b0 = self.me.b[0]
        self.core[t].wait_recv()
        self.add(4, lambda i: (i // 2, i % 2, b0, t), self.r0, lambda i: (t, i // 2, i % 2))
        self.one[t].start()

    def add_one(self, t):
        b0, b1, b2 = self.me.b
        self.one[t].wait_recv()
        self.add(2, lambda i: (b2, i, b0, t) if t % 2 else (i, b1, b0, t), self.r1, lambda i: (t, i))
        self.two[t].start()

    def add_two(self, t):
        b0, b1, b2 = self.me.b
        self.two[t].wait_recv()
        self.add(1, lambda i: (b2, b1, b0, t), self.r2, lambda i: (t,))
        pl.when(self.me.z != t)(self.z[t].start)

    def total(self):
        b0, b1, b2 = self.me.b
        total = self.g[b2, b1, b0, self.me.z].astype(F32)
        for s in range(self.me.nt - 1):
            self.back[s].wait_recv()
            total = total + self.rz[s].astype(F32)
        return total

    def finish(self):
        for cp in self.core + self.one + self.two:
            cp.wait_send()
        for t, cp in enumerate(self.z):
            pl.when(self.me.z != t)(cp.wait_send)


def scatter_scratch(nt, r, c):
    dma = pltpu.SemaphoreType.DMA
    return [
        VM((2, 2, 2, nt, r, c), BF),
        VM((nt, 2, 2, r, c), BF),
        VM((nt, 2, r, c), BF),
        VM((nt, r, c), BF),
        VM((nt - 1, r, c), BF),
        dma((nt, 4)),
        dma((nt, 4)),
    ]


def standard(v):
    centred = v - jnp.mean(v, axis=-1, keepdims=True)
    scale = lax.rsqrt(jnp.mean(centred * centred, axis=-1, keepdims=True) + EPS)
    return centred * scale, scale


def norm_back(grad, xhat, scale, gain):
    e = grad * gain
    inner = jnp.mean(e * xhat, axis=-1, keepdims=True)
    return scale * (e - jnp.mean(e, axis=-1, keepdims=True) - xhat * inner)


def rows_loop(total, step, body):
    def run(i, carry):
        body(pl.ds(pl.multiple_of(i * step, step), step))
        return carry

    lax.fori_loop(0, total // step, run, 0)


def turned(v, cosine, sine):
    lane = lax.broadcasted_iota(jnp.int32, v.shape, 1)
    other = jnp.where(lane % HD < HD // 2, pltpu.roll(v, 128 - HD // 2, 1), pltpu.roll(v, HD // 2, 1))
    return v * cosine + other * sine


def half_lanes(shape):
    return lax.broadcasted_iota(jnp.int32, shape, 1) < HD


def attend_pair(i, q, k, k2, v, v2, augk, augq, mixed, lse):
    at = pl.ds(pl.multiple_of(i * 2 * HD, 2 * HD), 2 * HD)
    keys = jnp.concatenate([k[:, at], k2[:, at]], axis=0)
    vt = jnp.concatenate([v[:, at], v2[:, at]], axis=0).T
    qt = q[:, at].T
    low = half_lanes(keys.shape)
    ones = jnp.ones((HD, vt.shape[1]), BF)
    outs = []
    for h in range(2):
        if h == 0:
            keys_h = jnp.where(low, keys, augk[...])
            q_h = jnp.concatenate([qt[:HD], augq[...]], axis=0)
            v_h = jnp.concatenate([vt[:HD], ones], axis=0)
        else:
            keys_h = jnp.where(low, augk[...], keys)
            q_h = jnp.concatenate([augq[...], qt[HD:]], axis=0)
            v_h = jnp.concatenate([ones, vt[HD:]], axis=0)
        scores = dot(keys_h, q_h)
        top = jnp.max(scores, axis=0, keepdims=True)
        expo = jnp.exp2((scores - top) * TO_EXP2).astype(BF)
        got = dot(v_h, expo)
        value, total = (got[:HD], got[HD:]) if h == 0 else (got[HD:], got[:HD])
        outs.append(value / total)
        lse[i, h : h + 1, :] = top + jnp.log2(total[:1]) * (1.0 / TO_EXP2)
    mixed[:, at] = jnp.concatenate(outs, axis=0).T.astype(BF)


def column(row):
    return jnp.concatenate([row] * 8, axis=0).T[:, :1]


def masks(me, row, half, freq, cos, sin, augk, augq):
    n = me.nt * half
    part = lambda core: jnp.concatenate(
        [row[:, (2 * z + core) * half : (2 * z + core + 1) * half] for z in range(me.nt)], axis=1
    ).astype(F32)
    even, odd = part(0), part(1)
    seg_q, seg_o = jnp.where(me.core == 0, even, odd), jnp.where(me.core == 0, odd, even)
    whole = jnp.concatenate([seg_q, seg_o], axis=1)
    mine = column(seg_q)
    spot = lax.broadcasted_iota(jnp.int32, (n, 1), 0)
    spot = spot + (spot // half) * half + me.core * half
    first = jnp.zeros((n, 1), F32)
    for s in range(SEGS - 2):
        count = jnp.sum((whole == s).astype(F32), axis=1, keepdims=True)
        first = first + jnp.where(mine > s, count, 0.0)
    angle = (spot.astype(F32) - first) * freq[...]
    cos[...] = jnp.cos(angle)
    sines = jnp.sin(angle)
    lane = lax.broadcasted_iota(jnp.int32, sines.shape, 1)
    sin[...] = jnp.where(lane % HD < HD // 2, -sines, sines)
    for s, seg in enumerate((mine, column(seg_o))):
        ids = lax.broadcasted_iota(jnp.int32, (n, 2 * HD), 1) % HD
        hot = jnp.logical_or(seg == ids.astype(F32), jnp.logical_and(ids >= SEGS, ids < SEGS + 3))
        augk[s * n : (s + 1) * n, :] = jnp.where(hot, 1.0, 0.0).astype(BF)
    ids = lax.broadcasted_iota(jnp.int32, (HD, n), 0)
    off = jnp.logical_and(ids < SEGS, seg_q != ids.astype(F32))
    augq[...] = jnp.where(off, -BIG, 0.0).astype(BF)


def front_kernel(
    ndp, nt,
    w_qkv, w_out, w_in, w_down, gains_in, hid_in, cot_in, seg, freq,
    hid, cot, all_two, q, k, v, k2, v2, n1, wf, mixed, lse, cos, sin, augk, augq, gains,
    w1, w2, all_one, seg_o, raw, s1, r1, s2, r2, own, se, re, sc, rc, ss,
):
    n, d = hid.shape
    el, fl = w_qkv.shape[2], w_in.shape[2]
    r = w_qkv.shape[1]
    half = n // nt
    me = Place(ndp, nt)
    me.barrier(True)
    first = Gather(me, w1, all_one, s1, r1, own.at[0])
    second = Gather(me, w2, all_two, s2, r2, own.at[1])
    hs, he = enter_copies(me, hid_in, hid, se, re)
    cs, ce = enter_copies(me, cot_in, cot, sc, rc)
    buddy = me.pair(1 - me.core, me.z)
    swap = remote(seg, seg_o, ss.at[0], ss.at[3], buddy)
    swap.start()
    for c in range(3):
        w1[:, c * el : (c + 1) * el] = w_qkv[c]
    spare = w1.shape[1] - 3 * el
    cols = jnp.concatenate([gains_in[...].astype(F32), jnp.zeros((spare - 2, r), F32)], axis=0)
    w1[:, 3 * el :] = cols.T.astype(BF)
    first.start_z()
    start_all(hs)
    w2[...] = jnp.zeros_like(w2)
    w2[:, :fl] = w_in[0]
    w2[:, fl : 2 * fl] = w_in[1]
    w2[:, 2 * fl : 3 * fl] = w_down[...].astype(F32).T.astype(BF)
    w2[:, padded(3 * fl) : padded(3 * fl) + el] = w_out[...].astype(F32).T.astype(BF)
    blocks = range(nt)
    for s in blocks:
        first.after_z(s)
    swap.wait()
    here = me.z // 2 == me.core
    index = me.z % 2
    both = jnp.where(here, seg[...], seg_o[...])
    row = jnp.where(index == 0, both[:1], both[1:2])
    masks(me, row, half, freq, cos, sin, augk, augq)
    for s in blocks:
        first.after_one(s)
    for e in he:
        e.wait_recv()
    second.start_z()

    def spread(at):
        raw[at, :] = standard(hid[at, :].astype(F32))[0]

    rows_loop(n, 64, spread)
    for s in blocks:
        first.after_two(s)
    first.finish()
    second.after_z(0)
    top = all_one[:, :, :, 0, :, 3 * el : 3 * el + SPARE].reshape(d, SPARE).astype(F32).T
    gains[...] = top
    gain = top[:1]

    def norm(at):
        n1[at, :] = (raw[at, :] * gain).astype(BF)

    rows_loop(n, 64, norm)
    for t in range(nt):
        for c in range(3):
            block = all_one[:, :, :, t, :, c * el : (c + 1) * el]
            wf[:, c * d + t * el : c * d + (t + 1) * el] = block.reshape(d, el)
    swaps = [remote(k, k2, ss.at[1], ss.at[4], buddy), remote(v, v2, ss.at[2], ss.at[5], buddy)]
    for c, out in ((1, k), (2, v), (0, q)):
        raw[...] = dot(n1[...], wf[:, c * d : (c + 1) * d])

        def finish(at, c=c, out=out):
            for j in range(0, d, 128):
                value = raw[at, j : j + 128]
                if c < 2:
                    value = turned(value, cos[at, :], sin[at, :])
                out[at, j : j + 128] = value.astype(BF)

        rows_loop(n, 64, finish)
        if c:
            swaps[c - 1].start()
            second.after_z(c)
    for s in swaps:
        s.wait()
    for s in range(3, nt):
        second.after_z(s)
    start_all(cs)
    pairs = d // (2 * HD)

    def step(i, carry):
        attend_pair(i, q, k, k2, v, v2, augk, augq, mixed, lse)

        @pl.when(i == 0)
        def _():
            for s in range(2):
                second.after_one(s)

        @pl.when(i == pairs // 2 - 1)
        def _():
            for s in range(2, nt):
                second.after_one(s)
            second.after_two(0)

        return carry

    lax.fori_loop(0, pairs, step, 0)
    for s in range(1, nt):
        second.after_two(s)
    for e in ce:
        e.wait_recv()
    second.finish()
    wait_sends(hs)
    wait_sends(cs)


def front(ndp, nt, w_qkv, w_out, w_in, w_down, gains, hid, cot, seg):
    half, d = hid.shape[2:]
    n = nt * half
    r, el, fl = w_qkv.shape[1], w_qkv.shape[2], w_in.shape[2]
    c1, c2 = padded(3 * el + SPARE), padded(3 * fl) + padded(el)
    freq = jnp.tile(THETA ** (-2.0 * jnp.arange(HD // 2, dtype=F32) / HD), 4)[None]
    sds = jax.ShapeDtypeStruct
    dma = pltpu.SemaphoreType.DMA
    vm, hbm = pl.BlockSpec(memory_space=VM), pl.BlockSpec(memory_space=pl.ANY)
    act = sds((n, d), BF)
    return pl.pallas_call(
        functools.partial(front_kernel, ndp, nt),
        in_specs=[vm] * 5 + [hbm] * 2 + [vm] * 2,
        out_specs=[vm, hbm, hbm] + [vm] * 14,
        out_shape=[act, act, sds((2, 2, 2, nt, r, c2), BF)]
        + [act] * 6
        + [sds((d, 3 * d), BF), act, sds((d // (2 * HD), 2, n), F32)]
        + [sds((n, 2 * HD), F32)] * 2
        + [sds((2 * n, 2 * HD), BF), sds((HD, n), BF), sds((SPARE, d), F32)],
        scratch_shapes=[
            VM((r, c1), BF),
            VM((r, c2), BF),
            VM((2, 2, 2, nt, r, c1), BF),
            VM(seg.shape, seg.dtype),
            VM((n, d), F32),
        ]
        + [dma((nt, 6))] * 4
        + [dma((2,))]
        + [dma((4,))] * 4
        + [dma((6,))],
        compiler_params=pltpu.CompilerParams(
            collective_id=0, has_side_effects=True, vmem_limit_bytes=WIDE
        ),
        name="front",
    )(w_qkv, w_out, w_in, w_down, gains, hid, cot, seg, freq)


def split_rows(value, n, rows):
    parts = []
    for _ in range(n):
        part = value.astype(BF).astype(F32)
        parts.append(part)
        value = value - part
    parts.append(jnp.zeros((rows - n, value.shape[1]), F32))
    return jnp.concatenate(parts, axis=0).astype(BF)


def attend_back_pair(i, q, k, k2, v, v2, g, mixed, lse, augk, augq, gq, gk, gk2, gv, gv2):
    at = pl.ds(pl.multiple_of(i * 2 * HD, 2 * HD), 2 * HD)
    rows = q.shape[0]
    grads, query = g[:, at], q[:, at]
    gt, qt = grads.T, query.T
    prod = gt.astype(F32) * mixed[:, at].T.astype(F32)
    gq_parts = []
    sides = [(k, v, gk, gv), (k2, v2, gk2, gv2)]
    low = half_lanes((rows, 2 * HD))
    one = jnp.ones((rows, 2 * HD), BF)
    held = {}
    for h in range(2):
        mine = slice(h * HD, (h + 1) * HD)

        def swapped(a, b, h=h):
            return (a, b) if h == 0 else (b, a)

        inner = jnp.sum(prod[mine], axis=0, keepdims=True)
        neg = split_rows(-lse[i, h : h + 1, :], 3, SEGS)
        extra_q = jnp.concatenate([augq[:SEGS], neg, augq[2 * SEGS :]], axis=0)
        extra_g = jnp.concatenate([split_rows(-inner, 2, 8), jnp.zeros((HD - 8, rows), BF)], axis=0)
        q_h = jnp.concatenate(swapped(qt[mine], extra_q), axis=0)
        g_h = jnp.concatenate(swapped(gt[mine], extra_g), axis=0)
        gq_h = None
        for s, (kr, vr, _, _) in enumerate(sides):
            aug = augk[s * rows : (s + 1) * rows, :]
            keys, values = kr[:, at], vr[:, at]
            probs = jnp.exp2(dot(jnp.where(low, *swapped(keys, aug)), q_h) * TO_EXP2)
            grad_p = dot(jnp.where(low, *swapped(values, one)), g_h)
            held[h, s, "v"] = dot(probs.astype(BF), grads)
            ds = (probs * grad_p).astype(BF)
            held[h, s, "k"] = dot(ds, query)
            part = dot(keys.T[mine], ds)
            gq_h = part if gq_h is None else gq_h + part
        gq_parts.append(gq_h)
    scale = 1.0 / math.sqrt(HD)
    gq[:, at] = jnp.concatenate(gq_parts, axis=0).T * scale
    for s, (_, _, gkr, gvr) in enumerate(sides):
        gkr[:, at] = (jnp.where(low, held[0, s, "k"], held[1, s, "k"]) * scale).astype(gkr.dtype)
        gvr[:, at] = jnp.where(low, held[0, s, "v"], held[1, s, "v"]).astype(gvr.dtype)


def back_kernel(
    ndp, nt,
    hid, cot, all_two, q, k, v, k2, v2, n1, wf, mixed, lse, cos, sin, augk, augq, gains,
    out_o, gin_o, grad_qkv, grad_out, grad_in, grad_down, grad_gains,
    w3, wo, wd, gate, up, gp, prod, gu, n2, low, gres, gtot, gmixed, out, ak, av, gsum, rgain,
    local, ss, so, ro, si, ri, sg, rg, *rest,
):
    n, d = hid.shape
    ff = wd.shape[1]
    el, fl = d // nt, ff // nt
    split = (2, 2, 2, d // 8)
    g2, g3, g1 = rest[0], rest[7], rest[14]
    gin, gk2, gv2 = gmixed, low, n2
    me = Place(ndp, nt)
    b0, b1, b2 = me.b
    ca, cb = g2.shape[5], g3.shape[5]
    loads = [
        pltpu.make_async_copy(all_two.at[:, :, :, :, :, pl.ds(0, ca)], g2, local.at[0]),
        pltpu.make_async_copy(all_two.at[:, :, :, :, :, pl.ds(ca, cb)], g3, local.at[1]),
    ]
    for load in loads:
        load.start()
    me.barrier(True)
    rs2 = Scatter(me, g2, rest[1:5], *rest[5:7])
    rs3 = Scatter(me, g3, rest[8:12], *rest[12:14])
    rs1 = Scatter(me, g1, rest[15:19], *rest[19:21])
    lo_s, lo_e = leave_copies(me, out, out_o, so, ro)
    gi_s, gi_e = leave_copies(me, gin, gin_o, si, ri)
    gain_one, gain_two = gains[0:1, :], gains[1:2, :]
    for load in loads:
        load.wait()
    blocks, pairs = range(nt), d // (2 * HD)
    for t in blocks:
        at = slice(t * fl, (t + 1) * fl)
        wo[:, t * el : (t + 1) * el] = g3[:, :, :, t, :, :el].reshape(d, el)
        w3[:, at] = g2[:, :, :, t, :, :fl].reshape(d, fl)
        w3[:, ff + t * fl : ff + (t + 1) * fl] = g2[:, :, :, t, :, fl : 2 * fl].reshape(d, fl)
        wd[:, at] = g2[:, :, :, t, :, 2 * fl : 3 * fl].reshape(d, fl)
    gres[...] = dot(mixed[...], wo[...], NT)

    def norm(at):
        value = hid[at, :].astype(F32) + gres[at, :]
        gres[at, :] = value
        n2[at, :] = (standard(value)[0] * gain_two).astype(BF)

    rows_loop(n, 64, norm)
    gate[...] = dot(n2[...], w3[:, :ff])
    up[...] = dot(n2[...], w3[:, ff:])
    gp[...] = dot(cot[...], wd[...])

    def geglu(at):
        for j in range(0, ff, 384):
            to = slice(j, j + 384)
            g, u, p = gate[at, to], up[at, to], gp[at, to]
            cdf = 0.5 + 0.5 * erf(g * math.sqrt(0.5))
            pdf = jnp.exp(-0.5 * g * g) * (1.0 / math.sqrt(2 * math.pi))
            act = g * cdf
            prod[at, to] = (act * u).astype(BF)
            gu[at, to] = (p * u * (cdf + g * pdf)).astype(BF)
            gu[at, ff + j : ff + j + 384] = (p * act).astype(BF)

    rows_loop(n, 32, geglu)
    n2t, cott = n2[...].T, cot[...].T
    for t in blocks:
        at = slice(t * fl, (t + 1) * fl)
        also = slice(ff + t * fl, ff + (t + 1) * fl)
        g2[:, :, :, t, :, :fl] = dot(n2t, gu[:, at]).astype(BF).reshape(*split, fl)
        g2[:, :, :, t, :, fl : 2 * fl] = dot(n2t, gu[:, also]).astype(BF).reshape(*split, fl)
        g2[:, :, :, t, :, 2 * fl : 3 * fl] = dot(cott, prod[:, at]).astype(BF).reshape(*split, fl)
        rs2.core[t].start()
    out[...] = (gres[...] + dot(prod[...], wd[...], NT)).astype(BF)
    start_all(lo_s)
    rs2.add_core(0)
    rs2.add_core(1)
    gtot[...] = dot(gu[...], w3[...], NT)
    load_wf = pltpu.make_async_copy(wf, w3, local.at[2])
    load_wf.start()
    gsum[...] = jnp.zeros_like(gsum)
    for t in range(2, nt):
        rs2.add_core(t)

    def back_two(at):
        xhat, scale = standard(gres[at, :])
        e = gtot[at, :]
        gsum[0] += jnp.sum((e * xhat).reshape(-1, 8, d), axis=0)
        total = cot[at, :].astype(F32) + norm_back(e, xhat, scale, gain_two)
        gres[at, :] = total
        low[at, :] = total.astype(BF)

    rows_loop(n, 64, back_two)
    lowt = low[...].T
    for t in blocks:
        to = slice(t * el, (t + 1) * el)
        g3[:, :, :, t, :, :el] = dot(lowt, mixed[:, to]).astype(BF).reshape(*split, el)
        rs3.core[t].start()
    gmixed[...] = dot(low[...], wo[...]).astype(BF)
    rs2.add_one(0)
    rs2.add_one(1)
    gq, gk, gv = gate, up, gp

    buddy = me.pair(1 - me.core, me.z)
    swaps = []
    for i in range(2):
        at = pl.ds(i * d // 2, d // 2)
        for j, (src, dst) in enumerate(((gk2, ak), (gv2, av))):
            m = 2 * i + j
            swaps.append(remote(src.at[:, at], dst.at[:, at], ss.at[m], ss.at[4 + m], buddy))
    raw = gu

    def back_rope(half):
        def body(at):
            c, s = cos[at, :], -sin[at, :]
            for j in range(half * d // 2, (half + 1) * d // 2, 128):
                to = slice(j, j + 128)
                raw[at, j : j + 128] = turned(gq[at, to], c, s).astype(BF)
                keys = gk[at, to] + ak[at, to].astype(F32)
                raw[at, d + j : d + j + 128] = turned(keys, c, s).astype(BF)
                raw[at, 2 * d + j : 2 * d + j + 128] = (gv[at, to] + av[at, to].astype(F32)).astype(BF)

        rows_loop(n, 32, body)

    def grads_one(n1t, t):
        for c in range(3):
            cols = raw[:, c * d + t * el : c * d + (t + 1) * el]
            g1[:, :, :, t, :, c * el : (c + 1) * el] = dot(n1t, cols).astype(BF).reshape(*split, el)

    def step(i, carry):
        attend_back_pair(i, q, k, k2, v, v2, gmixed, mixed, lse, augk, augq, gq, gk, gk2, gv, gv2)

        @pl.when(i == 0)
        def _():
            for t in blocks:
                rs3.add_core(t)

        @pl.when(i == pairs // 2 - 1)
        def _():
            for swap in swaps[:2]:
                swap.start()
            for t in range(2, nt):
                rs2.add_one(t)

        @pl.when(i == pairs // 2)
        def _():
            for swap in swaps[:2]:
                swap.wait()
            back_rope(0)
            n1t = n1[...].T
            for t in range(nt // 2):
                grads_one(n1t, t)
                rs1.core[t].start()
            rs2.add_two(0)
            rs2.add_two(1)
            for t in blocks:
                rs3.add_one(t)

        return carry

    lax.fori_loop(0, pairs, step, 0)
    for swap in swaps[2:]:
        swap.start()
    for t in range(nt // 2):
        rs1.add_core(t)
    for t in range(2, nt):
        rs2.add_two(t)
    for swap in swaps[2:]:
        swap.wait()
    back_rope(1)
    n1t = n1[...].T
    for t in range(nt // 2, nt - 1):
        grads_one(n1t, t)
        rs1.core[t].start()
    load_wf.wait()
    gtot[...] = dot(raw[...], w3[...], NT)
    for t in blocks:
        rs3.add_two(t)
    for t in range(nt // 2):
        rs1.add_one(t)

    def back_one(at):
        xhat, scale = standard(hid[at, :].astype(F32))
        e = gtot[at, :]
        gsum[1] += jnp.sum((e * xhat).reshape(-1, 8, d), axis=0)
        gin[at, :] = (gres[at, :] + norm_back(e, xhat, scale, gain_one)).astype(BF)

    rows_loop(n, 64, back_one)
    start_all(gi_s)
    rows = []
    for v_ in (gsum[1], gsum[0]):
        total = jnp.sum(v_, axis=0, keepdims=True)
        upper = total.astype(BF).astype(F32)
        rows += [upper, total - upper]
    rows.append(jnp.zeros((SPARE - 4, d), F32))
    gain_cols = jnp.concatenate(rows, axis=0).T.astype(BF).reshape(*split, SPARE)
    last = nt - 1
    grads_one(n1t, last)
    g1[:, :, :, last, :, 3 * el : 3 * el + SPARE] = gain_cols
    rs1.core[last].start()
    for t in range(nt // 2, nt):
        rs1.add_core(t)
    for t in range(nt // 2):
        rs1.add_two(t)
    for t in range(nt // 2, nt):
        rs1.add_one(t)
    total = rs3.total()
    grad_out[...] = total[:, :el].T
    total = rs2.total()
    grad_in[0] = total[:, :fl]
    grad_in[1] = total[:, fl : 2 * fl]
    grad_down[...] = total[:, 2 * fl : 3 * fl].T
    for t in range(nt // 2, nt):
        rs1.add_two(t)
    first = 3 * el // 128 * 128
    tile = (b2, b1, b0, last, slice(None), pl.ds(first, 128))
    gain_copies = [
        remote(g1.at[tile], rgain.at[s - 1], sg.at[s - 1], rg.at[s - 1], me.along(s)) for s in range(1, nt)
    ]
    for cp in gain_copies:
        cp.start()
    total = rs1.total()
    for c in range(3):
        grad_qkv[c] = total[:, c * el : (c + 1) * el]
    tail = g1[b2, b1, b0, last, :, first : first + 128].astype(F32)
    for s, cp in enumerate(gain_copies):
        cp.wait()
        tail = tail + rgain[s].astype(F32)
    tail = tail.T[3 * el - first : 3 * el - first + 8]
    grad_gains[...] = jnp.concatenate([tail[0:1] + tail[1:2], tail[2:3] + tail[3:4]], axis=0)
    for e in lo_e + gi_e:
        e.wait_recv()
    rs2.finish()
    rs3.finish()
    rs1.finish()
    wait_sends(lo_s)
    wait_sends(gi_s)


def backward(ndp, nt, half, fl, arrays):
    n, d = arrays[0].shape
    r = d // 8
    el, ff = d // nt, fl * nt
    c1 = padded(3 * el + SPARE)
    sds = jax.ShapeDtypeStruct
    dma = pltpu.SemaphoreType.DMA
    vm, hbm = pl.BlockSpec(memory_space=VM), pl.BlockSpec(memory_space=pl.ANY)
    specs = [vm] * len(arrays)
    specs[2] = specs[9] = hbm
    wide, act = VM((n, ff), F32), VM((n, d), BF)
    return pl.pallas_call(
        functools.partial(back_kernel, ndp, nt),
        in_specs=specs,
        out_specs=[hbm, hbm] + [vm] * 5,
        out_shape=[sds((2, 2, half, d), BF)] * 2
        + [
            sds((3, r, el), F32),
            sds((el, r), F32),
            sds((2, r, fl), F32),
            sds((fl, r), F32),
            sds((2, r), F32),
        ],
        scratch_shapes=[VM((d, 2 * ff), BF), VM((d, d), BF), VM((d, ff), BF)]
        + [wide] * 3
        + [VM((n, ff), BF), VM((n, 2 * ff), BF), act, act, VM((n, d), F32), VM((n, d), F32)]
        + [act] * 4
        + [VM((2, 8, d), F32), VM((nt - 1, r, 128), BF), dma((3,)), dma((8,))]
        + [dma((4,))] * 4
        + [dma((nt - 1,))] * 2
        + scatter_scratch(nt, r, padded(3 * fl))
        + scatter_scratch(nt, r, padded(el))
        + scatter_scratch(nt, r, c1),
        compiler_params=pltpu.CompilerParams(
            collective_id=1, has_side_effects=True, vmem_limit_bytes=WIDE
        ),
        name="backward",
    )(*arrays)


def finish_kernel(count, *refs):
    arrays, outs, held, (sems, more) = refs[:count], refs[count : 2 * count], refs[2 * count : 3 * count], refs[3 * count :]
    ins = [pltpu.make_async_copy(a, h, sems.at[i]) for i, (a, h) in enumerate(zip(arrays, held))]
    ends = [pltpu.make_async_copy(h, o, more.at[i]) for i, (h, o) in enumerate(zip(held, outs))]
    for copy in ins:
        copy.start()
    for copy, end in zip(ins, ends):
        copy.wait()
        end.start()
    for end in ends:
        end.wait()


def finish(arrays):
    hbm = pl.BlockSpec(memory_space=pl.ANY)
    count = len(arrays)
    return pl.pallas_call(
        functools.partial(finish_kernel, count),
        in_specs=[hbm] * count,
        out_specs=[hbm] * count,
        out_shape=[jax.ShapeDtypeStruct(a.shape, a.dtype) for a in arrays],
        scratch_shapes=[VM(a.shape, a.dtype) for a in arrays] + [pltpu.SemaphoreType.DMA((count,))] * 2,
        compiler_params=pltpu.CompilerParams(vmem_limit_bytes=WIDE),
        name="finish",
    )(*arrays)


def shards(hidden_in, cotangent, segment_ids, w_qkv, w_out, w_in, w_down, norm_gains):
    ndp, nt = lax.axis_size("dp"), lax.axis_size("tensor")
    stride = ndp // 8
    rows, local_len, d = hidden_in.shape
    half = local_len // 2
    low_groups = [[h * stride + i for i in range(stride)] for h in range(8)]

    def widen(v, axis):
        if stride == 1:
            return v
        return lax.all_gather(v, "dp", axis_index_groups=low_groups, axis=axis, tiled=True)

    def narrow(v, axis):
        if stride == 1:
            return v
        return lax.psum_scatter(
            v, "dp", scatter_dimension=axis, axis_index_groups=low_groups, tiled=True
        )

    split = lambda v: v.reshape(2, 2, half, d)
    arrays = front(
        ndp, nt,
        widen(w_qkv, 1), widen(w_out, 1), widen(w_in, 1), widen(w_down, 1), widen(norm_gains, 1),
        split(hidden_in), split(cotangent), segment_ids,
    )
    layer_out, grad_input, grad_qkv, grad_out, grad_in, grad_down, grad_gains = finish(
        backward(ndp, nt, half, w_in.shape[2], arrays)
    )
    back = lambda t: t.reshape(rows, local_len, d)
    return (
        back(layer_out),
        back(grad_input),
        narrow(grad_qkv, 1),
        narrow(grad_out, 1),
        narrow(grad_in, 1),
        narrow(grad_down, 1),
        narrow(grad_gains, 1),
    )


def solution(mesh):
    placed = (
        P("dp", "tensor", None),
        P("dp", "tensor", None),
        P("dp", None),
        P(None, "dp", "tensor"),
        P("tensor", "dp"),
        P(None, "dp", "tensor"),
        P("tensor", "dp"),
        P(None, "dp"),
    )
    return jax.shard_map(
        shards,
        mesh=mesh,
        in_specs=placed,
        out_specs=(
            P("dp", "tensor", None),
            P("dp", "tensor", None),
            P(None, "dp", "tensor"),
            P("tensor", "dp"),
            P(None, "dp", "tensor"),
            P("tensor", "dp"),
            P(None, "dp"),
        ),
        check_vma=False,
    )
```

```python
import functools
import math

import jax
import jax.numpy as jnp
from jax import lax
from jax.experimental import pallas as pl
from jax.experimental.pallas import tpu as pltpu
from jax.sharding import PartitionSpec as P

HD = 64
EPS = 1e-05
THETA = 160000.0
BIG = 1e30
SEGS = 8
SPARE = 8
TO_EXP2 = math.log2(math.e) / math.sqrt(HD)
MESH = pl.DeviceIdType.MESH
BF, F32 = jnp.bfloat16, jnp.float32
VM = pltpu.VMEM
WIDE = 60 * 1024 * 1024


def dot(a, b, dims=((1,), (0,))):
    return lax.dot_general(a, b, (dims, ((), ())), preferred_element_type=F32)


NT = ((1,), (1,))


def padded(n):
    return -(-n // 128) * 128


def erf(x):
    x = jnp.clip(x, -3.832506856900711, 3.832506856900711)
    s = x * x
    p = 0.00022905065861350646
    for c in (0.0034082910107109506, 0.050955695062380861, 0.18520832239976145, 1.128379143519084):
        p = p * s + c
    q = -1.1791602954361697e-7
    for c in (
        0.000023547966471313185,
        0.0010179625278914885,
        0.014070470171167667,
        0.11098505178285362,
        0.49746925110067538,
        1.0,
    ):
        q = q * s + c
    return x * p / q


class Place:
    def __init__(self, ndp, nt):
        self.nt = nt
        self.stride = ndp // 8
        self.dp, self.z = lax.axis_index("dp"), lax.axis_index("tensor")
        high = self.dp // self.stride
        self.b = (high % 2, (high // 2) % 2, high // 4)
        self.core = self.dp % 2

    def flip(self, bit):
        return (self.dp + (1 - 2 * self.b[bit]) * self.stride * 2**bit, self.z)

    def along(self, step):
        return (self.dp, (self.z + step) % self.nt)

    def pair(self, core, z):
        return (self.dp - self.core + core, z)

    def barrier(self, group):
        others = [self.along(s) for s in range(1, self.nt)]
        others += [self.flip(1), self.flip(2)]
        if group or self.stride == 1:
            others += [self.pair(1 - self.core, self.z)]
        if self.stride > 1:
            others += [self.flip(0)]
        if group:
            others += [self.pair(1 - self.core, (self.z + s) % self.nt) for s in range(1, self.nt)]
        sem = pltpu.get_barrier_semaphore()
        for device in others:
            pl.semaphore_signal(sem, inc=1, device_id=device, device_id_type=MESH)
        pl.semaphore_wait(sem, len(others))


def remote(src, dst, send, recv, device):
    return pltpu.make_async_remote_copy(
        src_ref=src, dst_ref=dst, send_sem=send, recv_sem=recv, device_id=device, device_id_type=MESH
    )


def enter_copies(me, src, dst, send, recv):
    starts, ends = [], []
    half = src.shape[2]
    slot = lambda z: dst.at[pl.ds(pl.multiple_of(z * half, half), half)]
    for row in range(2):
        for core in range(2):
            z = 2 * me.core + row
            k = 2 * row + core
            here = jnp.logical_and(z == me.z, core == me.core)
            copy = remote(src.at[row, core], slot(me.z), send.at[k], recv.at[me.z], me.pair(core, z))
            local = pltpu.make_async_copy(src.at[row, core], slot(me.z), recv.at[me.z])
            starts.append((here, copy, local))
    for z in range(me.nt):
        ends.append(remote(src.at[0, 0], slot(z), send.at[0], recv.at[z], me.pair(1 - me.core, z)))
    return starts, ends


def leave_copies(me, src, dst, send, recv):
    starts, ends = [], []
    half = dst.shape[2]
    for z in range(me.nt):
        here = jnp.logical_and(z == me.z, me.z // 2 == me.core)
        k = 2 * (me.z % 2) + me.core
        to = dst.at[me.z % 2, me.core]
        copy = remote(src.at[z * half : (z + 1) * half], to, send.at[z], recv.at[k], me.pair(me.z // 2, z))
        local = pltpu.make_async_copy(src.at[z * half : (z + 1) * half], to, recv.at[k])
        starts.append((here, copy, local))
    for k in range(4):
        ends.append(remote(src.at[:half], dst.at[k // 2, k % 2], send.at[0], recv.at[k], me.pair(1 - me.core, me.z)))
    return starts, ends


def start_all(starts):
    for here, copy, local in starts:
        pl.when(here)(local.start)
        pl.when(jnp.logical_not(here))(copy.start)


def wait_sends(starts):
    for here, copy, _ in starts:
        pl.when(jnp.logical_not(here))(copy.wait_send)


class Gather:
    def __init__(self, me, shard, out, send, recv, own):
        self.me, self.shard, self.out = me, shard, out
        b0, b1, b2 = me.b
        nt = me.nt
        both = pl.ds(0, 2)
        x, y, core = me.flip(1), me.flip(2), me.flip(0)
        o0, o1, o2 = 1 - b0, 1 - b1, 1 - b2
        self.mine = pltpu.make_async_copy(shard, out.at[b2, b1, b0, me.z], own)
        self.z, self.one, self.two, self.core = [], [], [], []
        for s in range(nt):
            t = (me.z + nt - s) % nt

            def pair(k, at, other, device, s=s, t=t):
                sems = send.at[s, k], recv.at[s, k]
                cp = remote(out.at[(*at, t)], out.at[(*at, t)], *sems, device)
                return cp, remote(out.at[(*other, t)], out.at[(*other, t)], *sems, device)

            if s:
                sems = send.at[s, 0], recv.at[s, 0]
                to, frm = out.at[b2, b1, b0, me.z], out.at[b2, b1, b0, t]
                self.z.append((remote(shard, to, *sems, me.along(s)), remote(shard, frm, *sems, me.along(s))))
            else:
                self.z.append(None)
            if s % 2 == 0:
                self.one.append(pair(1, (b2, b1, b0), (b2, o1, b0), x))
                self.two.append(pair(2, (b2, both, b0), (o2, both, b0), y))
                got_one, got_two = (b2, o1), (o2, both)
            else:
                self.one.append(pair(1, (b2, b1, b0), (o2, b1, b0), y))
                self.two.append(pair(2, (both, b1, b0), (both, o1, b0), x))
                got_one, got_two = (o2, b1), (both, o1)
            self.core.append(
                [
                    pair(3, (b2, b1, b0), (b2, b1, o0), core),
                    pair(4, (*got_one, b0), (*got_one, o0), core),
                    pair(5, (*got_two, b0), (*got_two, o0), core),
                ]
            )

    def start_z(self):
        self.mine.start()
        for cp, _ in self.z[1:]:
            cp.start()

    def after_z(self, s):
        if s:
            self.z[s][1].wait_recv()
        else:
            self.mine.wait()
        self.one[s][0].start()
        self.core[s][0][0].start()

    def after_one(self, s):
        self.one[s][1].wait_recv()
        self.two[s][0].start()
        self.core[s][1][0].start()

    def after_two(self, s):
        self.two[s][1].wait_recv()
        self.core[s][2][0].start()

    def finish(self):
        for group in self.core:
            for _, back in group:
                back.wait_recv()
        for cp, _ in self.z[1:] + self.one + self.two + sum(self.core, []):
            cp.wait_send()


class Scatter:
    def __init__(self, me, g, bufs, send, recv):
        self.me, self.g = me, g
        self.r0, self.r1, self.r2, self.rz = bufs
        b0, b1, b2 = me.b
        o0, o1, o2 = 1 - b0, 1 - b1, 1 - b2
        nt = me.nt
        both = pl.ds(0, 2)
        x, y, core = me.flip(1), me.flip(2), me.flip(0)
        self.core, self.one, self.two, self.z, self.back = [], [], [], [], []
        for t in range(nt):
            sems = [(send.at[t, k], recv.at[t, k]) for k in range(3)]
            one, two = (g.at[both, o1, b0, t], g.at[o2, b1, b0, t]), (x, y)
            if t % 2:
                one, two = (g.at[o2, both, b0, t], g.at[b2, o1, b0, t]), (y, x)
            self.core.append(remote(g.at[both, both, o0, t], self.r0.at[t], *sems[0], core))
            self.one.append(remote(one[0], self.r1.at[t], *sems[1], two[0]))
            self.two.append(remote(one[1], self.r2.at[t], *sems[2], two[1]))
            slot = (t - me.z + nt - 1) % nt
            slot = jnp.minimum(slot, nt - 2)
            self.z.append(
                remote(g.at[b2, b1, b0, t], self.rz.at[slot], send.at[t, 3], recv.at[slot, 3], (me.dp, t))
            )
        for s in range(nt - 1):
            self.back.append(
                remote(g.at[b2, b1, b0, 0], self.rz.at[s], send.at[s, 3], recv.at[s, 3], me.along(1))
            )

    def add(self, count, at, buf, got):
        tiles = self.g.shape[4] // 32

        def body(i, carry):
            rows = pl.ds(pl.multiple_of(i % tiles * 32, 32), 32)
            here, there = (*at(i // tiles), rows), (*got(i // tiles), rows)
            self.g[here] = (self.g[here].astype(F32) + buf[there].astype(F32)).astype(BF)
            return carry

        lax.fori_loop(0, count * tiles, body, 0)

    def add_core(self, t):
        b0 = self.me.b[0]
        self.core[t].wait_recv()
        self.add(4, lambda i: (i // 2, i % 2, b0, t), self.r0, lambda i: (t, i // 2, i % 2))
        self.one[t].start()

    def add_one(self, t):
        b0, b1, b2 = self.me.b
        self.one[t].wait_recv()
        self.add(2, lambda i: (b2, i, b0, t) if t % 2 else (i, b1, b0, t), self.r1, lambda i: (t, i))
        self.two[t].start()

    def add_two(self, t):
        b0, b1, b2 = self.me.b
        self.two[t].wait_recv()
        self.add(1, lambda i: (b2, b1, b0, t), self.r2, lambda i: (t,))
        pl.when(self.me.z != t)(self.z[t].start)

    def total(self):
        b0, b1, b2 = self.me.b
        total = self.g[b2, b1, b0, self.me.z].astype(F32)
        for s in range(self.me.nt - 1):
            self.back[s].wait_recv()
            total = total + self.rz[s].astype(F32)
        return total

    def finish(self):
        for cp in self.core + self.one + self.two:
            cp.wait_send()
        for t, cp in enumerate(self.z):
            pl.when(self.me.z != t)(cp.wait_send)


def scatter_scratch(nt, r, c):
    dma = pltpu.SemaphoreType.DMA
    return [
        VM((2, 2, 2, nt, r, c), BF),
        VM((nt, 2, 2, r, c), BF),
        VM((nt, 2, r, c), BF),
        VM((nt, r, c), BF),
        VM((nt - 1, r, c), BF),
        dma((nt, 4)),
        dma((nt, 4)),
    ]


def standard(v):
    centred = v - jnp.mean(v, axis=-1, keepdims=True)
    scale = lax.rsqrt(jnp.mean(centred * centred, axis=-1, keepdims=True) + EPS)
    return centred * scale, scale


def norm_back(grad, xhat, scale, gain):
    e = grad * gain
    inner = jnp.mean(e * xhat, axis=-1, keepdims=True)
    return scale * (e - jnp.mean(e, axis=-1, keepdims=True) - xhat * inner)


def rows_loop(total, step, body):
    def run(i, carry):
        body(pl.ds(pl.multiple_of(i * step, step), step))
        return carry

    lax.fori_loop(0, total // step, run, 0)


def turned(v, cosine, sine):
    lane = lax.broadcasted_iota(jnp.int32, v.shape, 1)
    other = jnp.where(lane % HD < HD // 2, pltpu.roll(v, 128 - HD // 2, 1), pltpu.roll(v, HD // 2, 1))
    return v * cosine + other * sine


def half_lanes(shape):
    return lax.broadcasted_iota(jnp.int32, shape, 1) < HD


def attend_pair(i, q, k, k2, v, v2, augk, augq, mixed, lse):
    at = pl.ds(pl.multiple_of(i * 2 * HD, 2 * HD), 2 * HD)
    keys = jnp.concatenate([k[:, at], k2[:, at]], axis=0)
    vt = jnp.concatenate([v[:, at], v2[:, at]], axis=0).T
    qt = q[:, at].T
    low = half_lanes(keys.shape)
    ones = jnp.ones((HD, vt.shape[1]), BF)
    outs = []
    for h in range(2):
        if h == 0:
            keys_h = jnp.where(low, keys, augk[...])
            q_h = jnp.concatenate([qt[:HD], augq[...]], axis=0)
            v_h = jnp.concatenate([vt[:HD], ones], axis=0)
        else:
            keys_h = jnp.where(low, augk[...], keys)
            q_h = jnp.concatenate([augq[...], qt[HD:]], axis=0)
            v_h = jnp.concatenate([ones, vt[HD:]], axis=0)
        scores = dot(keys_h, q_h)
        top = jnp.max(scores, axis=0, keepdims=True)
        expo = jnp.exp2((scores - top) * TO_EXP2).astype(BF)
        got = dot(v_h, expo)
        value, total = (got[:HD], got[HD:]) if h == 0 else (got[HD:], got[:HD])
        outs.append(value / total)
        lse[i, h : h + 1, :] = top + jnp.log2(total[:1]) * (1.0 / TO_EXP2)
    mixed[:, at] = jnp.concatenate(outs, axis=0).T.astype(BF)


def column(row):
    return jnp.concatenate([row] * 8, axis=0).T[:, :1]


def masks(me, row, half, freq, cos, sin, augk, augq):
    n = me.nt * half
    part = lambda core: jnp.concatenate(
        [row[:, (2 * z + core) * half : (2 * z + core + 1) * half] for z in range(me.nt)], axis=1
    ).astype(F32)
    even, odd = part(0), part(1)
    seg_q, seg_o = jnp.where(me.core == 0, even, odd), jnp.where(me.core == 0, odd, even)
    whole = jnp.concatenate([seg_q, seg_o], axis=1)
    mine = column(seg_q)
    spot = lax.broadcasted_iota(jnp.int32, (n, 1), 0)
    spot = spot + (spot // half) * half + me.core * half
    first = jnp.zeros((n, 1), F32)
    for s in range(SEGS - 2):
        count = jnp.sum((whole == s).astype(F32), axis=1, keepdims=True)
        first = first + jnp.where(mine > s, count, 0.0)
    angle = (spot.astype(F32) - first) * freq[...]
    cos[...] = jnp.cos(angle)
    sines = jnp.sin(angle)
    lane = lax.broadcasted_iota(jnp.int32, sines.shape, 1)
    sin[...] = jnp.where(lane % HD < HD // 2, -sines, sines)
    for s, seg in enumerate((mine, column(seg_o))):
        ids = lax.broadcasted_iota(jnp.int32, (n, 2 * HD), 1) % HD
        hot = jnp.logical_or(seg == ids.astype(F32), jnp.logical_and(ids >= SEGS, ids < SEGS + 3))
        augk[s * n : (s + 1) * n, :] = jnp.where(hot, 1.0, 0.0).astype(BF)
    ids = lax.broadcasted_iota(jnp.int32, (HD, n), 0)
    off = jnp.logical_and(ids < SEGS, seg_q != ids.astype(F32))
    augq[...] = jnp.where(off, -BIG, 0.0).astype(BF)


def forward_part(
    me, w_qkv, w_out, w_in, w_down, gains_in, hid_in, cot_in, seg, freq, wf_o,
    hid, cot, q, k, v, k2, v2, n1, wf, mixed, lse, cos, sin, augk, augq, gains,
    w1, w2, w3, seg_o, raw, g1, g2, g3, local, s1, r1, s2, r2, s3, r3, own, se, re, sc, rc, ss,
):
    nt = me.nt
    n, d = hid.shape
    el, fl = w_qkv.shape[2], w_in.shape[2]
    r = w_qkv.shape[1]
    half = n // nt
    first = Gather(me, w1, g1, s1, r1, own.at[0])
    second = Gather(me, w2, g2, s2, r2, own.at[1])
    third = Gather(me, w3, g3, s3, r3, own.at[2])
    all_one = g1
    hs, he = enter_copies(me, hid_in, hid, se, re)
    cs, ce = enter_copies(me, cot_in, cot, sc, rc)
    buddy = me.pair(1 - me.core, me.z)
    swap = remote(seg, seg_o, ss.at[0], ss.at[3], buddy)
    swap.start()
    for c in range(3):
        w1[:, c * el : (c + 1) * el] = w_qkv[c]
    spare = w1.shape[1] - 3 * el
    cols = jnp.concatenate([gains_in[...].astype(F32), jnp.zeros((spare - 2, r), F32)], axis=0)
    w1[:, 3 * el :] = cols.T.astype(BF)
    first.start_z()
    start_all(hs)
    w2[...] = jnp.zeros_like(w2)
    w2[:, :fl] = w_in[0]
    w2[:, fl : 2 * fl] = w_in[1]
    w2[:, 2 * fl : 3 * fl] = w_down[...].astype(F32).T.astype(BF)
    w3[...] = jnp.zeros_like(w3)
    w3[:, :el] = w_out[...].astype(F32).T.astype(BF)
    blocks = range(nt)
    for s in blocks:
        first.after_z(s)
    swap.wait()
    here = me.z // 2 == me.core
    index = me.z % 2
    both = jnp.where(here, seg[...], seg_o[...])
    row = jnp.where(index == 0, both[:1], both[1:2])
    masks(me, row, half, freq, cos, sin, augk, augq)
    for s in blocks:
        first.after_one(s)
    for e in he:
        e.wait_recv()
    third.start_z()
    second.start_z()

    def spread(at):
        raw[at, :] = standard(hid[at, :].astype(F32))[0]

    rows_loop(n, 64, spread)
    for s in blocks:
        first.after_two(s)
    first.finish()
    third.after_z(0)
    second.after_z(0)
    top = all_one[:, :, :, 0, :, 3 * el : 3 * el + SPARE].reshape(d, SPARE).astype(F32).T
    gains[...] = top
    gain = top[:1]

    def norm(at):
        n1[at, :] = (raw[at, :] * gain).astype(BF)

    rows_loop(n, 64, norm)
    for t in range(nt):
        for c in range(3):
            block = all_one[:, :, :, t, :, c * el : (c + 1) * el]
            wf[:, c * d + t * el : c * d + (t + 1) * el] = block.reshape(d, el)
    swaps = [remote(k, k2, ss.at[1], ss.at[4], buddy), remote(v, v2, ss.at[2], ss.at[5], buddy)]
    for c, out in ((1, k), (2, v), (0, q)):
        raw[...] = dot(n1[...], wf[:, c * d : (c + 1) * d])

        def finish(at, c=c, out=out):
            for j in range(0, d, 128):
                value = raw[at, j : j + 128]
                if c < 2:
                    value = turned(value, cos[at, :], sin[at, :])
                out[at, j : j + 128] = value.astype(BF)

        rows_loop(n, 64, finish)
        if c:
            swaps[c - 1].start()
            third.after_z(c)
            second.after_z(c)
    save = pltpu.make_async_copy(wf, wf_o, local.at[0])
    save.start()
    for s in swaps:
        s.wait()
    for s in range(3, nt):
        third.after_z(s)
        second.after_z(s)
    start_all(cs)
    pairs = d // (2 * HD)

    def step(i, carry):
        attend_pair(i, q, k, k2, v, v2, augk, augq, mixed, lse)

        @pl.when(i == 0)
        def _():
            for s in range(2):
                third.after_one(s)
                second.after_one(s)

        @pl.when(i == pairs // 2 - 1)
        def _():
            for s in range(2, nt):
                third.after_one(s)
                second.after_one(s)
            third.after_two(0)
            second.after_two(0)

        return carry

    lax.fori_loop(0, pairs, step, 0)
    for s in range(1, nt):
        third.after_two(s)
        second.after_two(s)
    return second, third, save, hs, cs, ce


def split_rows(value, n, rows):
    parts = []
    for _ in range(n):
        part = value.astype(BF).astype(F32)
        parts.append(part)
        value = value - part
    parts.append(jnp.zeros((rows - n, value.shape[1]), F32))
    return jnp.concatenate(parts, axis=0).astype(BF)


def attend_back_pair(i, q, k, k2, v, v2, g, mixed, lse, augk, augq, gq, gk, gk2, gv, gv2):
    at = pl.ds(pl.multiple_of(i * 2 * HD, 2 * HD), 2 * HD)
    rows = q.shape[0]
    grads, query = g[:, at], q[:, at]
    gt, qt = grads.T, query.T
    prod = gt.astype(F32) * mixed[:, at].T.astype(F32)
    gq_parts = []
    sides = [(k, v, gk, gv), (k2, v2, gk2, gv2)]
    low = half_lanes((rows, 2 * HD))
    one = jnp.ones((rows, 2 * HD), BF)
    held = {}
    for h in range(2):
        mine = slice(h * HD, (h + 1) * HD)

        def swapped(a, b, h=h):
            return (a, b) if h == 0 else (b, a)

        inner = jnp.sum(prod[mine], axis=0, keepdims=True)
        neg = split_rows(-lse[i, h : h + 1, :], 3, SEGS)
        extra_q = jnp.concatenate([augq[:SEGS], neg, augq[2 * SEGS :]], axis=0)
        extra_g = jnp.concatenate([split_rows(-inner, 2, 8), jnp.zeros((HD - 8, rows), BF)], axis=0)
        q_h = jnp.concatenate(swapped(qt[mine], extra_q), axis=0)
        g_h = jnp.concatenate(swapped(gt[mine], extra_g), axis=0)
        gq_h = None
        for s, (kr, vr, _, _) in enumerate(sides):
            aug = augk[s * rows : (s + 1) * rows, :]
            keys, values = kr[:, at], vr[:, at]
            probs = jnp.exp2(dot(jnp.where(low, *swapped(keys, aug)), q_h) * TO_EXP2)
            grad_p = dot(jnp.where(low, *swapped(values, one)), g_h)
            held[h, s, "v"] = dot(probs.astype(BF), grads)
            ds = (probs * grad_p).astype(BF)
            held[h, s, "k"] = dot(ds, query)
            part = dot(keys.T[mine], ds)
            gq_h = part if gq_h is None else gq_h + part
        gq_parts.append(gq_h)
    scale = 1.0 / math.sqrt(HD)
    gq[:, at] = jnp.concatenate(gq_parts, axis=0).T * scale
    for s, (_, _, gkr, gvr) in enumerate(sides):
        gkr[:, at] = (jnp.where(low, held[0, s, "k"], held[1, s, "k"]) * scale).astype(gkr.dtype)
        gvr[:, at] = jnp.where(low, held[0, s, "v"], held[1, s, "v"]).astype(gvr.dtype)


def layer_kernel(
    ndp, nt,
    w_qkv, w_out, w_in, w_down, gains_in, hid_in, cot_in, seg, freq,
    out_o, gin_o, wf_o, grad_qkv, grad_out, grad_in, grad_down, grad_gains,
    hid, cot, q, k, v, k2, v2, n1, mixed, lse, cos, sin, augk, augq, gains,
    sh1, sh2, sh3, seg_o,
    w3, wo, wd, gate, up, gp, prod, gu, n2, low, gres, gtot, gmixed, out, ak, av, gsum, rgain,
    local, ss, so, ro, si, ri, sg, rg, *rest,
):
    n, d = hid.shape
    ff = wd.shape[1]
    el, fl = d // nt, ff // nt
    split = (2, 2, 2, d // 8)
    g2, g3, g1 = rest[0], rest[7], rest[14]
    gin, gk2, gv2 = gmixed, low, n2
    me = Place(ndp, nt)
    b0, b1, b2 = me.b
    me.barrier(True)
    second, third, save, hs, cs, ce = forward_part(
        me, w_qkv, w_out, w_in, w_down, gains_in, hid_in, cot_in, seg, freq, wf_o,
        hid, cot, q, k, v, k2, v2, n1, w3, mixed, lse, cos, sin, augk, augq, gains,
        sh1, sh2, sh3, seg_o, gtot, g1, g2, g3, local, *rest[21:],
    )
    rs2 = Scatter(me, g2, rest[1:5], *rest[5:7])
    rs3 = Scatter(me, g3, rest[8:12], *rest[12:14])
    rs1 = Scatter(me, g1, rest[15:19], *rest[19:21])
    lo_s, lo_e = leave_copies(me, out, out_o, so, ro)
    gi_s, gi_e = leave_copies(me, gin, gin_o, si, ri)
    gain_one, gain_two = gains[0:1, :], gains[1:2, :]
    blocks, pairs = range(nt), d // (2 * HD)
    third.finish()
    for t in blocks:
        wo[:, t * el : (t + 1) * el] = g3[:, :, :, t, :, :el].reshape(d, el)
    gres[...] = dot(mixed[...], wo[...], NT)

    def norm(at):
        value = hid[at, :].astype(F32) + gres[at, :]
        gres[at, :] = value
        n2[at, :] = (standard(value)[0] * gain_two).astype(BF)

    rows_loop(n, 64, norm)
    save.wait()
    second.finish()
    for t in blocks:
        at = slice(t * fl, (t + 1) * fl)
        w3[:, at] = g2[:, :, :, t, :, :fl].reshape(d, fl)
        w3[:, ff + t * fl : ff + (t + 1) * fl] = g2[:, :, :, t, :, fl : 2 * fl].reshape(d, fl)
        wd[:, at] = g2[:, :, :, t, :, 2 * fl : 3 * fl].reshape(d, fl)
    for e in ce:
        e.wait_recv()
    wait_sends(hs)
    wait_sends(cs)
    gate[...] = dot(n2[...], w3[:, :ff])
    up[...] = dot(n2[...], w3[:, ff:])
    gp[...] = dot(cot[...], wd[...])

    def geglu(at):
        for j in range(0, ff, 384):
            to = slice(j, j + 384)
            g, u, p = gate[at, to], up[at, to], gp[at, to]
            cdf = 0.5 + 0.5 * erf(g * math.sqrt(0.5))
            pdf = jnp.exp(-0.5 * g * g) * (1.0 / math.sqrt(2 * math.pi))
            act = g * cdf
            prod[at, to] = (act * u).astype(BF)
            gu[at, to] = (p * u * (cdf + g * pdf)).astype(BF)
            gu[at, ff + j : ff + j + 384] = (p * act).astype(BF)

    rows_loop(n, 32, geglu)
    n2t, cott = n2[...].T, cot[...].T
    for t in blocks:
        at = slice(t * fl, (t + 1) * fl)
        also = slice(ff + t * fl, ff + (t + 1) * fl)
        g2[:, :, :, t, :, :fl] = dot(n2t, gu[:, at]).astype(BF).reshape(*split, fl)
        g2[:, :, :, t, :, fl : 2 * fl] = dot(n2t, gu[:, also]).astype(BF).reshape(*split, fl)
        g2[:, :, :, t, :, 2 * fl : 3 * fl] = dot(cott, prod[:, at]).astype(BF).reshape(*split, fl)
        rs2.core[t].start()
    out[...] = (gres[...] + dot(prod[...], wd[...], NT)).astype(BF)
    start_all(lo_s)
    rs2.add_core(0)
    rs2.add_core(1)
    gtot[...] = dot(gu[...], w3[...], NT)
    load_wf = pltpu.make_async_copy(wf_o, w3, local.at[1])
    load_wf.start()
    gsum[...] = jnp.zeros_like(gsum)
    for t in range(2, nt):
        rs2.add_core(t)

    def back_two(at):
        xhat, scale = standard(gres[at, :])
        e = gtot[at, :]
        gsum[0] += jnp.sum((e * xhat).reshape(-1, 8, d), axis=0)
        total = cot[at, :].astype(F32) + norm_back(e, xhat, scale, gain_two)
        gres[at, :] = total
        low[at, :] = total.astype(BF)

    rows_loop(n, 64, back_two)
    lowt = low[...].T
    for t in blocks:
        to = slice(t * el, (t + 1) * el)
        g3[:, :, :, t, :, :el] = dot(lowt, mixed[:, to]).astype(BF).reshape(*split, el)
        rs3.core[t].start()
    gmixed[...] = dot(low[...], wo[...]).astype(BF)
    rs2.add_one(0)
    rs2.add_one(1)
    gq, gk, gv = gate, up, gp

    buddy = me.pair(1 - me.core, me.z)
    swaps = []
    for i in range(2):
        at = pl.ds(i * d // 2, d // 2)
        for j, (src, dst) in enumerate(((gk2, ak), (gv2, av))):
            m = 2 * i + j
            swaps.append(remote(src.at[:, at], dst.at[:, at], ss.at[m], ss.at[4 + m], buddy))
    raw = gu

    def back_rope(half):
        def body(at):
            c, s = cos[at, :], -sin[at, :]
            for j in range(half * d // 2, (half + 1) * d // 2, 128):
                to = slice(j, j + 128)
                raw[at, j : j + 128] = turned(gq[at, to], c, s).astype(BF)
                keys = gk[at, to] + ak[at, to].astype(F32)
                raw[at, d + j : d + j + 128] = turned(keys, c, s).astype(BF)
                raw[at, 2 * d + j : 2 * d + j + 128] = (gv[at, to] + av[at, to].astype(F32)).astype(BF)

        rows_loop(n, 32, body)

    def grads_one(n1t, t):
        for c in range(3):
            cols = raw[:, c * d + t * el : c * d + (t + 1) * el]
            g1[:, :, :, t, :, c * el : (c + 1) * el] = dot(n1t, cols).astype(BF).reshape(*split, el)

    def step(i, carry):
        attend_back_pair(i, q, k, k2, v, v2, gmixed, mixed, lse, augk, augq, gq, gk, gk2, gv, gv2)

        @pl.when(i == 0)
        def _():
            for t in blocks:
                rs3.add_core(t)

        @pl.when(i == pairs // 2 - 1)
        def _():
            for swap in swaps[:2]:
                swap.start()
            for t in range(2, nt):
                rs2.add_one(t)

        @pl.when(i == pairs // 2)
        def _():
            for swap in swaps[:2]:
                swap.wait()
            back_rope(0)
            n1t = n1[...].T
            for t in range(nt // 2):
                grads_one(n1t, t)
                rs1.core[t].start()
            rs2.add_two(0)
            rs2.add_two(1)
            for t in blocks:
                rs3.add_one(t)

        return carry

    lax.fori_loop(0, pairs, step, 0)
    for swap in swaps[2:]:
        swap.start()
    for t in range(nt // 2):
        rs1.add_core(t)
    for t in range(2, nt):
        rs2.add_two(t)
    for swap in swaps[2:]:
        swap.wait()
    back_rope(1)
    n1t = n1[...].T
    for t in range(nt // 2, nt - 1):
        grads_one(n1t, t)
        rs1.core[t].start()
    load_wf.wait()
    gtot[...] = dot(raw[...], w3[...], NT)
    for t in blocks:
        rs3.add_two(t)
    for t in range(nt // 2):
        rs1.add_one(t)

    def back_one(at):
        xhat, scale = standard(hid[at, :].astype(F32))
        e = gtot[at, :]
        gsum[1] += jnp.sum((e * xhat).reshape(-1, 8, d), axis=0)
        gin[at, :] = (gres[at, :] + norm_back(e, xhat, scale, gain_one)).astype(BF)

    rows_loop(n, 64, back_one)
    start_all(gi_s)
    rows = []
    for v_ in (gsum[1], gsum[0]):
        total = jnp.sum(v_, axis=0, keepdims=True)
        upper = total.astype(BF).astype(F32)
        rows += [upper, total - upper]
    rows.append(jnp.zeros((SPARE - 4, d), F32))
    gain_cols = jnp.concatenate(rows, axis=0).T.astype(BF).reshape(*split, SPARE)
    last = nt - 1
    grads_one(n1t, last)
    g1[:, :, :, last, :, 3 * el : 3 * el + SPARE] = gain_cols
    rs1.core[last].start()
    for t in range(nt // 2, nt):
        rs1.add_core(t)
    for t in range(nt // 2):
        rs1.add_two(t)
    for t in range(nt // 2, nt):
        rs1.add_one(t)
    total = rs3.total()
    grad_out[...] = total[:, :el].T
    total = rs2.total()
    grad_in[0] = total[:, :fl]
    grad_in[1] = total[:, fl : 2 * fl]
    grad_down[...] = total[:, 2 * fl : 3 * fl].T
    for t in range(nt // 2, nt):
        rs1.add_two(t)
    first = 3 * el // 128 * 128
    tile = (b2, b1, b0, last, slice(None), pl.ds(first, 128))
    gain_copies = [
        remote(g1.at[tile], rgain.at[s - 1], sg.at[s - 1], rg.at[s - 1], me.along(s)) for s in range(1, nt)
    ]
    for cp in gain_copies:
        cp.start()
    total = rs1.total()
    for c in range(3):
        grad_qkv[c] = total[:, c * el : (c + 1) * el]
    tail = g1[b2, b1, b0, last, :, first : first + 128].astype(F32)
    for s, cp in enumerate(gain_copies):
        cp.wait()
        tail = tail + rgain[s].astype(F32)
    tail = tail.T[3 * el - first : 3 * el - first + 8]
    grad_gains[...] = jnp.concatenate([tail[0:1] + tail[1:2], tail[2:3] + tail[3:4]], axis=0)
    for e in lo_e + gi_e:
        e.wait_recv()
    rs2.finish()
    rs3.finish()
    rs1.finish()
    wait_sends(lo_s)
    wait_sends(gi_s)


def layer(ndp, nt, w_qkv, w_out, w_in, w_down, gains, hid, cot, seg):
    half, d = hid.shape[2:]
    n = nt * half
    r, el, fl = w_qkv.shape[1], w_qkv.shape[2], w_in.shape[2]
    ff = fl * nt
    c1, c2, c3 = padded(3 * el + SPARE), padded(3 * fl), padded(el)
    freq = jnp.tile(THETA ** (-2.0 * jnp.arange(HD // 2, dtype=F32) / HD), 4)[None]
    sds = jax.ShapeDtypeStruct
    dma = pltpu.SemaphoreType.DMA
    vm, hbm = pl.BlockSpec(memory_space=VM), pl.BlockSpec(memory_space=pl.ANY)
    wide, act, act32 = VM((n, ff), F32), VM((n, d), BF), VM((n, d), F32)
    return pl.pallas_call(
        functools.partial(layer_kernel, ndp, nt),
        in_specs=[vm] * 5 + [hbm] * 2 + [vm] * 2,
        out_specs=[hbm] * 3 + [vm] * 5,
        out_shape=[sds((2, 2, half, d), BF)] * 2
        + [
            sds((d, 3 * d), BF),
            sds((3, r, el), F32),
            sds((el, r), F32),
            sds((2, r, fl), F32),
            sds((fl, r), F32),
            sds((2, r), F32),
        ],
        scratch_shapes=[act] * 9
        + [VM((d // (2 * HD), 2, n), F32)]
        + [VM((n, 2 * HD), F32)] * 2
        + [VM((2 * n, 2 * HD), BF), VM((HD, n), BF), VM((SPARE, d), F32)]
        + [VM((r, c), BF) for c in (c1, c2, c3)]
        + [VM(seg.shape, seg.dtype)]
        + [VM((d, 2 * ff), BF), VM((d, d), BF), VM((d, ff), BF)]
        + [wide] * 3
        + [VM((n, ff), BF), VM((n, 2 * ff), BF), act, act, act32, act32]
        + [act] * 4
        + [VM((2, 8, d), F32), VM((nt - 1, r, 128), BF), dma((2,)), dma((8,))]
        + [dma((4,))] * 4
        + [dma((nt - 1,))] * 2
        + scatter_scratch(nt, r, c2)
        + scatter_scratch(nt, r, c3)
        + scatter_scratch(nt, r, c1)
        + [dma((nt, 6))] * 6
        + [dma((3,))]
        + [dma((4,))] * 4
        + [dma((6,))],
        compiler_params=pltpu.CompilerParams(
            collective_id=0, has_side_effects=True, vmem_limit_bytes=WIDE
        ),
        name="layer",
    )(w_qkv, w_out, w_in, w_down, gains, hid, cot, seg, freq)


def finish_kernel(count, *refs):
    arrays, outs, held, (sems, more) = refs[:count], refs[count : 2 * count], refs[2 * count : 3 * count], refs[3 * count :]
    ins = [pltpu.make_async_copy(a, h, sems.at[i]) for i, (a, h) in enumerate(zip(arrays, held))]
    ends = [pltpu.make_async_copy(h, o, more.at[i]) for i, (h, o) in enumerate(zip(held, outs))]
    for copy in ins:
        copy.start()
    for copy, end in zip(ins, ends):
        copy.wait()
        end.start()
    for end in ends:
        end.wait()


def finish(arrays):
    hbm = pl.BlockSpec(memory_space=pl.ANY)
    count = len(arrays)
    return pl.pallas_call(
        functools.partial(finish_kernel, count),
        in_specs=[hbm] * count,
        out_specs=[hbm] * count,
        out_shape=[jax.ShapeDtypeStruct(a.shape, a.dtype) for a in arrays],
        scratch_shapes=[VM(a.shape, a.dtype) for a in arrays] + [pltpu.SemaphoreType.DMA((count,))] * 2,
        compiler_params=pltpu.CompilerParams(vmem_limit_bytes=WIDE),
        name="finish",
    )(*arrays)


def shards(hidden_in, cotangent, segment_ids, w_qkv, w_out, w_in, w_down, norm_gains):
    ndp, nt = lax.axis_size("dp"), lax.axis_size("tensor")
    stride = ndp // 8
    rows, local_len, d = hidden_in.shape
    half = local_len // 2
    low_groups = [[h * stride + i for i in range(stride)] for h in range(8)]

    def widen(v, axis):
        if stride == 1:
            return v
        return lax.all_gather(v, "dp", axis_index_groups=low_groups, axis=axis, tiled=True)

    def narrow(v, axis):
        if stride == 1:
            return v
        return lax.psum_scatter(
            v, "dp", scatter_dimension=axis, axis_index_groups=low_groups, tiled=True
        )

    split = lambda v: v.reshape(2, 2, half, d)
    out, gin, _, *grads = layer(
        ndp, nt,
        widen(w_qkv, 1), widen(w_out, 1), widen(w_in, 1), widen(w_down, 1), widen(norm_gains, 1),
        split(hidden_in), split(cotangent), segment_ids,
    )
    layer_out, grad_input, grad_qkv, grad_out, grad_in, grad_down, grad_gains = finish([out, gin, *grads])
    back = lambda t: t.reshape(rows, local_len, d)
    return (
        back(layer_out),
        back(grad_input),
        narrow(grad_qkv, 1),
        narrow(grad_out, 1),
        narrow(grad_in, 1),
        narrow(grad_down, 1),
        narrow(grad_gains, 1),
    )


def solution(mesh):
    placed = (
        P("dp", "tensor", None),
        P("dp", "tensor", None),
        P("dp", None),
        P(None, "dp", "tensor"),
        P("tensor", "dp"),
        P(None, "dp", "tensor"),
        P("tensor", "dp"),
        P(None, "dp"),
    )
    return jax.shard_map(
        shards,
        mesh=mesh,
        in_specs=placed,
        out_specs=(
            P("dp", "tensor", None),
            P("dp", "tensor", None),
            P(None, "dp", "tensor"),
            P("tensor", "dp"),
            P(None, "dp", "tensor"),
            P("tensor", "dp"),
            P(None, "dp"),
        ),
        check_vma=False,
    )
```

```python
import functools
import math

import jax
import jax.numpy as jnp
from jax import lax
from jax.experimental import pallas as pl
from jax.experimental.pallas import tpu as pltpu
from jax.sharding import PartitionSpec as P

HD = 64
EPS = 1e-05
THETA = 160000.0
BIG = 1e30
SEGS = 8
SPARE = 8
TO_EXP2 = math.log2(math.e) / math.sqrt(HD)
MESH = pl.DeviceIdType.MESH
BF, F32 = jnp.bfloat16, jnp.float32
VM = pltpu.VMEM
WIDE = 60 * 1024 * 1024


def dot(a, b, dims=((1,), (0,))):
    return lax.dot_general(a, b, (dims, ((), ())), preferred_element_type=F32)


NT = ((1,), (1,))


def padded(n):
    return -(-n // 128) * 128


def erf(x):
    x = jnp.clip(x, -3.832506856900711, 3.832506856900711)
    s = x * x
    p = 0.00022905065861350646
    for c in (0.0034082910107109506, 0.050955695062380861, 0.18520832239976145, 1.128379143519084):
        p = p * s + c
    q = -1.1791602954361697e-7
    for c in (
        0.000023547966471313185,
        0.0010179625278914885,
        0.014070470171167667,
        0.11098505178285362,
        0.49746925110067538,
        1.0,
    ):
        q = q * s + c
    return x * p / q


class Place:
    def __init__(self, ndp, nt):
        self.nt = nt
        self.stride = ndp // 8
        self.dp, self.z = lax.axis_index("dp"), lax.axis_index("tensor")
        high = self.dp // self.stride
        self.b = (high % 2, (high // 2) % 2, high // 4)
        self.core = self.dp % 2

    def flip(self, bit):
        return (self.dp + (1 - 2 * self.b[bit]) * self.stride * 2**bit, self.z)

    def along(self, step):
        return (self.dp, (self.z + step) % self.nt)

    def pair(self, core, z):
        return (self.dp - self.core + core, z)

    def barrier(self, group):
        others = [self.along(s) for s in range(1, self.nt)]
        others += [self.flip(1), self.flip(2)]
        if group or self.stride == 1:
            others += [self.pair(1 - self.core, self.z)]
        if self.stride > 1:
            others += [self.flip(0)]
        if group:
            others += [self.pair(1 - self.core, (self.z + s) % self.nt) for s in range(1, self.nt)]
        sem = pltpu.get_barrier_semaphore()
        for device in others:
            pl.semaphore_signal(sem, inc=1, device_id=device, device_id_type=MESH)
        pl.semaphore_wait(sem, len(others))


def remote(src, dst, send, recv, device):
    return pltpu.make_async_remote_copy(
        src_ref=src, dst_ref=dst, send_sem=send, recv_sem=recv, device_id=device, device_id_type=MESH
    )


def enter_copies(me, src, dst, send, recv):
    starts, ends = [], []
    half = src.shape[2]
    slot = lambda z: dst.at[pl.ds(pl.multiple_of(z * half, half), half)]
    for row in range(2):
        for core in range(2):
            z = 2 * me.core + row
            k = 2 * row + core
            here = jnp.logical_and(z == me.z, core == me.core)
            copy = remote(src.at[row, core], slot(me.z), send.at[k], recv.at[me.z], me.pair(core, z))
            local = pltpu.make_async_copy(src.at[row, core], slot(me.z), recv.at[me.z])
            starts.append((here, copy, local))
    for z in range(me.nt):
        ends.append(remote(src.at[0, 0], slot(z), send.at[0], recv.at[z], me.pair(1 - me.core, z)))
    return starts, ends


def leave_copies(me, src, dst, send, recv):
    starts, ends = [], []
    half = dst.shape[2]
    for z in range(me.nt):
        here = jnp.logical_and(z == me.z, me.z // 2 == me.core)
        k = 2 * (me.z % 2) + me.core
        to = dst.at[me.z % 2, me.core]
        copy = remote(src.at[z * half : (z + 1) * half], to, send.at[z], recv.at[k], me.pair(me.z // 2, z))
        local = pltpu.make_async_copy(src.at[z * half : (z + 1) * half], to, recv.at[k])
        starts.append((here, copy, local))
    for k in range(4):
        ends.append(remote(src.at[:half], dst.at[k // 2, k % 2], send.at[0], recv.at[k], me.pair(1 - me.core, me.z)))
    return starts, ends


def start_all(starts):
    for here, copy, local in starts:
        pl.when(here)(local.start)
        pl.when(jnp.logical_not(here))(copy.start)


def wait_sends(starts):
    for here, copy, _ in starts:
        pl.when(jnp.logical_not(here))(copy.wait_send)


class Gather:
    def __init__(self, me, shard, out, send, recv, own):
        self.me, self.shard, self.out = me, shard, out
        b0, b1, b2 = me.b
        nt = me.nt
        both = pl.ds(0, 2)
        x, y, core = me.flip(1), me.flip(2), me.flip(0)
        o0, o1, o2 = 1 - b0, 1 - b1, 1 - b2
        self.mine = pltpu.make_async_copy(shard, out.at[b2, b1, b0, me.z], own)
        self.z, self.one, self.two, self.core = [], [], [], []
        for s in range(nt):
            t = (me.z + nt - s) % nt

            def pair(k, at, other, device, s=s, t=t):
                sems = send.at[s, k], recv.at[s, k]
                cp = remote(out.at[(*at, t)], out.at[(*at, t)], *sems, device)
                return cp, remote(out.at[(*other, t)], out.at[(*other, t)], *sems, device)

            if s:
                sems = send.at[s, 0], recv.at[s, 0]
                to, frm = out.at[b2, b1, b0, me.z], out.at[b2, b1, b0, t]
                self.z.append((remote(shard, to, *sems, me.along(s)), remote(shard, frm, *sems, me.along(s))))
            else:
                self.z.append(None)
            if s % 2 == 0:
                self.one.append(pair(1, (b2, b1, b0), (b2, o1, b0), x))
                self.two.append(pair(2, (b2, both, b0), (o2, both, b0), y))
                got_one, got_two = (b2, o1), (o2, both)
            else:
                self.one.append(pair(1, (b2, b1, b0), (o2, b1, b0), y))
                self.two.append(pair(2, (both, b1, b0), (both, o1, b0), x))
                got_one, got_two = (o2, b1), (both, o1)
            self.core.append(
                [
                    pair(3, (b2, b1, b0), (b2, b1, o0), core),
                    pair(4, (*got_one, b0), (*got_one, o0), core),
                    pair(5, (*got_two, b0), (*got_two, o0), core),
                ]
            )

    def start_z(self):
        self.mine.start()
        for cp, _ in self.z[1:]:
            cp.start()

    def after_z(self, s):
        if s:
            self.z[s][1].wait_recv()
        else:
            self.mine.wait()
        self.one[s][0].start()
        self.core[s][0][0].start()

    def after_one(self, s):
        self.one[s][1].wait_recv()
        self.two[s][0].start()
        self.core[s][1][0].start()

    def after_two(self, s):
        self.two[s][1].wait_recv()
        self.core[s][2][0].start()

    def finish(self):
        for group in self.core:
            for _, back in group:
                back.wait_recv()
        for cp, _ in self.z[1:] + self.one + self.two + sum(self.core, []):
            cp.wait_send()


class Scatter:
    def __init__(self, me, g, bufs, send, recv, spread=True):
        self.me, self.g, self.spread = me, g, spread
        self.r0, self.r1, self.r2, self.rz = bufs
        b0, b1, b2 = me.b
        o0, o1, o2 = 1 - b0, 1 - b1, 1 - b2
        nt = me.nt
        both = pl.ds(0, 2)
        x, y, core = me.flip(1), me.flip(2), me.flip(0)
        self.core, self.one, self.two, self.z, self.back = [], [], [], [], []
        for t in range(g.shape[3]):
            sems = [(send.at[t, k], recv.at[t, k]) for k in range(3)]
            one, two = (g.at[both, o1, b0, t], g.at[o2, b1, b0, t]), (x, y)
            if t % 2:
                one, two = (g.at[o2, both, b0, t], g.at[b2, o1, b0, t]), (y, x)
            self.core.append(remote(g.at[both, both, o0, t], self.r0.at[t], *sems[0], core))
            self.one.append(remote(one[0], self.r1.at[t], *sems[1], two[0]))
            self.two.append(remote(one[1], self.r2.at[t], *sems[2], two[1]))
            if not spread:
                continue
            slot = (t - me.z + nt - 1) % nt
            slot = jnp.minimum(slot, nt - 2)
            self.z.append(
                remote(g.at[b2, b1, b0, t], self.rz.at[slot], send.at[t, 3], recv.at[slot, 3], (me.dp, t))
            )
        for s in range(nt - 1 if spread else 0):
            self.back.append(
                remote(g.at[b2, b1, b0, 0], self.rz.at[s], send.at[s, 3], recv.at[s, 3], me.along(1))
            )

    def add(self, count, at, buf, got):
        tiles = self.g.shape[4] // 32

        def body(i, carry):
            rows = pl.ds(pl.multiple_of(i % tiles * 32, 32), 32)
            here, there = (*at(i // tiles), rows), (*got(i // tiles), rows)
            self.g[here] = (self.g[here].astype(F32) + buf[there].astype(F32)).astype(BF)
            return carry

        lax.fori_loop(0, count * tiles, body, 0)

    def add_core(self, t):
        b0 = self.me.b[0]
        self.core[t].wait_recv()
        self.add(4, lambda i: (i // 2, i % 2, b0, t), self.r0, lambda i: (t, i // 2, i % 2))
        self.one[t].start()

    def add_one(self, t):
        b0, b1, b2 = self.me.b
        self.one[t].wait_recv()
        self.add(2, lambda i: (b2, i, b0, t) if t % 2 else (i, b1, b0, t), self.r1, lambda i: (t, i))
        self.two[t].start()

    def add_two(self, t):
        b0, b1, b2 = self.me.b
        self.two[t].wait_recv()
        self.add(1, lambda i: (b2, b1, b0, t), self.r2, lambda i: (t,))
        if self.spread:
            pl.when(self.me.z != t)(self.z[t].start)

    def total(self):
        b0, b1, b2 = self.me.b
        total = self.g[b2, b1, b0, self.me.z].astype(F32)
        for s in range(self.me.nt - 1):
            self.back[s].wait_recv()
            total = total + self.rz[s].astype(F32)
        return total

    def finish(self):
        for cp in self.core + self.one + self.two:
            cp.wait_send()
        for t, cp in enumerate(self.z):
            pl.when(self.me.z != t)(cp.wait_send)


def scatter_scratch(nt, r, c, count):
    dma = pltpu.SemaphoreType.DMA
    return [
        VM((2, 2, 2, count, r, c), BF),
        VM((count, 2, 2, r, c), BF),
        VM((count, 2, r, c), BF),
        VM((count, r, c), BF),
        VM((nt - 1, r, c), BF),
        dma((nt, 4)),
        dma((nt, 4)),
    ]


def standard(v):
    centred = v - jnp.mean(v, axis=-1, keepdims=True)
    scale = lax.rsqrt(jnp.mean(centred * centred, axis=-1, keepdims=True) + EPS)
    return centred * scale, scale


def norm_back(grad, xhat, scale, gain):
    e = grad * gain
    inner = jnp.mean(e * xhat, axis=-1, keepdims=True)
    return scale * (e - jnp.mean(e, axis=-1, keepdims=True) - xhat * inner)


def rows_loop(total, step, body, start=0):
    def run(i, carry):
        body(pl.ds(pl.multiple_of(start + i * step, step), step))
        return carry

    lax.fori_loop(0, total // step, run, 0)


def turned(v, cosine, sine):
    lane = lax.broadcasted_iota(jnp.int32, v.shape, 1)
    other = jnp.where(lane % HD < HD // 2, pltpu.roll(v, 128 - HD // 2, 1), pltpu.roll(v, HD // 2, 1))
    return v * cosine + other * sine


def half_lanes(shape):
    return lax.broadcasted_iota(jnp.int32, shape, 1) < HD


def attend_pair(i, q, k, k2, v, v2, augk, augq, mixed, lse):
    at = pl.ds(pl.multiple_of(i * 2 * HD, 2 * HD), 2 * HD)
    keys = jnp.concatenate([k[:, at], k2[:, at]], axis=0)
    vt = jnp.concatenate([v[:, at], v2[:, at]], axis=0).T
    qt = q[:, at].T
    low = half_lanes(keys.shape)
    ones = jnp.ones((HD, vt.shape[1]), BF)
    outs = []
    for h in range(2):
        if h == 0:
            keys_h = jnp.where(low, keys, augk[...])
            q_h = jnp.concatenate([qt[:HD], augq[...]], axis=0)
            v_h = jnp.concatenate([vt[:HD], ones], axis=0)
        else:
            keys_h = jnp.where(low, augk[...], keys)
            q_h = jnp.concatenate([augq[...], qt[HD:]], axis=0)
            v_h = jnp.concatenate([ones, vt[HD:]], axis=0)
        scores = dot(keys_h, q_h)
        top = jnp.max(scores, axis=0, keepdims=True)
        expo = jnp.exp2((scores - top) * TO_EXP2).astype(BF)
        got = dot(v_h, expo)
        value, total = (got[:HD], got[HD:]) if h == 0 else (got[HD:], got[:HD])
        outs.append(value / total)
        lse[i, h : h + 1, :] = top + jnp.log2(total[:1]) * (1.0 / TO_EXP2)
    mixed[:, at] = jnp.concatenate(outs, axis=0).T.astype(BF)


def column(row):
    return jnp.concatenate([row] * 8, axis=0).T[:, :1]


def masks(me, row, half, freq, cos, sin, augk, augq):
    n = me.nt * half
    part = lambda core: jnp.concatenate(
        [row[:, (2 * z + core) * half : (2 * z + core + 1) * half] for z in range(me.nt)], axis=1
    ).astype(F32)
    even, odd = part(0), part(1)
    seg_q, seg_o = jnp.where(me.core == 0, even, odd), jnp.where(me.core == 0, odd, even)
    whole = jnp.concatenate([seg_q, seg_o], axis=1)
    mine = column(seg_q)
    spot = lax.broadcasted_iota(jnp.int32, (n, 1), 0)
    spot = spot + (spot // half) * half + me.core * half
    first = jnp.zeros((n, 1), F32)
    for s in range(SEGS - 2):
        count = jnp.sum((whole == s).astype(F32), axis=1, keepdims=True)
        first = first + jnp.where(mine > s, count, 0.0)
    angle = (spot.astype(F32) - first) * freq[...]
    cos[...] = jnp.cos(angle)
    sines = jnp.sin(angle)
    lane = lax.broadcasted_iota(jnp.int32, sines.shape, 1)
    sin[...] = jnp.where(lane % HD < HD // 2, -sines, sines)
    for s, seg in enumerate((mine, column(seg_o))):
        ids = lax.broadcasted_iota(jnp.int32, (n, 2 * HD), 1) % HD
        hot = jnp.logical_or(seg == ids.astype(F32), jnp.logical_and(ids >= SEGS, ids < SEGS + 3))
        augk[s * n : (s + 1) * n, :] = jnp.where(hot, 1.0, 0.0).astype(BF)
    ids = lax.broadcasted_iota(jnp.int32, (HD, n), 0)
    off = jnp.logical_and(ids < SEGS, seg_q != ids.astype(F32))
    augq[...] = jnp.where(off, -BIG, 0.0).astype(BF)


def forward_part(
    me, w_qkv, w_out, w_in, w_down, gains_in, hid_in, cot_in, seg, freq, wf_o,
    hid, cot, q, k, v, k2, v2, n1, wf, mixed, lse, cos, sin, augk, augq, gains,
    w1, w2, w3, seg_o, raw, g1, g2, g3, local, s1, r1, s2, r2, s3, r3, own, se, re, sc, rc, ss,
):
    nt = me.nt
    n, d = hid.shape
    el, fl = w_qkv.shape[2], w_in.shape[2]
    r = w_qkv.shape[1]
    half = n // nt
    first = Gather(me, w1, g1, s1, r1, own.at[0])
    second = Gather(me, w2, g2, s2, r2, own.at[1])
    third = Gather(me, w3, g3, s3, r3, own.at[2])
    all_one = g1
    hs, he = enter_copies(me, hid_in, hid, se, re)
    cs, ce = enter_copies(me, cot_in, cot, sc, rc)
    buddy = me.pair(1 - me.core, me.z)
    swap = remote(seg, seg_o, ss.at[0], ss.at[3], buddy)
    swap.start()
    for c in range(3):
        w1[:, c * el : (c + 1) * el] = w_qkv[c]
    spare = w1.shape[1] - 3 * el
    cols = jnp.concatenate([gains_in[...].astype(F32), jnp.zeros((spare - 2, r), F32)], axis=0)
    w1[:, 3 * el :] = cols.T.astype(BF)
    first.start_z()
    w2[...] = jnp.zeros_like(w2)
    w2[:, :fl] = w_in[0]
    w2[:, fl : 2 * fl] = w_in[1]
    w2[:, 2 * fl : 3 * fl] = w_down[...].astype(F32).T.astype(BF)
    w3[...] = jnp.zeros_like(w3)
    w3[:, :el] = w_out[...].astype(F32).T.astype(BF)
    blocks = range(nt)
    for s in blocks:
        first.after_z(s)
        if s == 1:
            start_all(hs)
    swap.wait()
    here = me.z // 2 == me.core
    index = me.z % 2
    both = jnp.where(here, seg[...], seg_o[...])
    row = jnp.where(index == 0, both[:1], both[1:2])
    masks(me, row, half, freq, cos, sin, augk, augq)
    for s in blocks:
        first.after_one(s)
    for e in he:
        e.wait_recv()
    third.start_z()
    second.start_z()

    def spread(at):
        raw[at, :] = standard(hid[at, :].astype(F32))[0]

    rows_loop(n, 64, spread)
    for s in blocks:
        first.after_two(s)
    first.finish()
    third.after_z(0)
    second.after_z(0)
    top = all_one[:, :, :, 0, :, 3 * el : 3 * el + SPARE].reshape(d, SPARE).astype(F32).T
    gains[...] = top
    gain = top[:1]

    def norm(at):
        n1[at, :] = (raw[at, :] * gain).astype(BF)

    rows_loop(n, 64, norm)
    for t in range(nt):
        for c in range(3):
            block = all_one[:, :, :, t, :, c * el : (c + 1) * el]
            wf[:, c * d + t * el : c * d + (t + 1) * el] = block.reshape(d, el)
    swaps = [remote(k, k2, ss.at[1], ss.at[4], buddy), remote(v, v2, ss.at[2], ss.at[5], buddy)]
    for c, out in ((1, k), (2, v), (0, q)):
        raw[...] = dot(n1[...], wf[:, c * d : (c + 1) * d])

        def finish(at, c=c, out=out):
            for j in range(0, d, 128):
                value = raw[at, j : j + 128]
                if c < 2:
                    value = turned(value, cos[at, :], sin[at, :])
                out[at, j : j + 128] = value.astype(BF)

        rows_loop(n, 64, finish)
        if c:
            swaps[c - 1].start()
            third.after_z(c)
            second.after_z(c)
    save = pltpu.make_async_copy(wf, wf_o, local.at[0])
    save.start()
    for s in swaps:
        s.wait()
    for s in range(3, nt):
        third.after_z(s)
        second.after_z(s)
    start_all(cs)
    pairs = d // (2 * HD)

    def step(i, carry):
        attend_pair(i, q, k, k2, v, v2, augk, augq, mixed, lse)

        @pl.when(i == 0)
        def _():
            for s in range(2):
                third.after_one(s)
                second.after_one(s)

        @pl.when(i == pairs // 2 - 1)
        def _():
            for s in range(2, nt):
                third.after_one(s)
                second.after_one(s)
            third.after_two(0)
            second.after_two(0)

        return carry

    lax.fori_loop(0, pairs, step, 0)
    for s in range(1, nt):
        third.after_two(s)
        second.after_two(s)
    return second, third, save, hs, cs, ce


def split_rows(value, n, rows):
    parts = []
    for _ in range(n):
        part = value.astype(BF).astype(F32)
        parts.append(part)
        value = value - part
    parts.append(jnp.zeros((rows - n, value.shape[1]), F32))
    return jnp.concatenate(parts, axis=0).astype(BF)


def attend_back_pair(i, q, k, k2, v, v2, g, mixed, lse, augk, augq, gq, gk, gk2, gv, gv2):
    at = pl.ds(pl.multiple_of(i * 2 * HD, 2 * HD), 2 * HD)
    rows = q.shape[0]
    grads, query = g[:, at], q[:, at]
    gt, qt = grads.T, query.T
    prod = gt.astype(F32) * mixed[:, at].T.astype(F32)
    gq_parts = []
    sides = [(k, v, gk, gv), (k2, v2, gk2, gv2)]
    low = half_lanes((rows, 2 * HD))
    one = jnp.ones((rows, 2 * HD), BF)
    held = {}
    for h in range(2):
        mine = slice(h * HD, (h + 1) * HD)

        def swapped(a, b, h=h):
            return (a, b) if h == 0 else (b, a)

        inner = jnp.sum(prod[mine], axis=0, keepdims=True)
        neg = split_rows(-lse[i, h : h + 1, :], 3, SEGS)
        extra_q = jnp.concatenate([augq[:SEGS], neg, augq[2 * SEGS :]], axis=0)
        extra_g = jnp.concatenate([split_rows(-inner, 2, 8), jnp.zeros((HD - 8, rows), BF)], axis=0)
        q_h = jnp.concatenate(swapped(qt[mine], extra_q), axis=0)
        g_h = jnp.concatenate(swapped(gt[mine], extra_g), axis=0)
        gq_h = None
        for s, (kr, vr, _, _) in enumerate(sides):
            aug = augk[s * rows : (s + 1) * rows, :]
            keys, values = kr[:, at], vr[:, at]
            probs = jnp.exp2(dot(jnp.where(low, *swapped(keys, aug)), q_h) * TO_EXP2)
            grad_p = dot(jnp.where(low, *swapped(values, one)), g_h)
            held[h, s, "v"] = dot(probs.astype(BF), grads)
            ds = (probs * grad_p).astype(BF)
            held[h, s, "k"] = dot(ds, query)
            part = dot(keys.T[mine], ds)
            gq_h = part if gq_h is None else gq_h + part
        gq_parts.append(gq_h)
    scale = 1.0 / math.sqrt(HD)
    gq[:, at] = jnp.concatenate(gq_parts, axis=0).T * scale
    for s, (_, _, gkr, gvr) in enumerate(sides):
        gkr[:, at] = (jnp.where(low, held[0, s, "k"], held[1, s, "k"]) * scale).astype(gkr.dtype)
        gvr[:, at] = jnp.where(low, held[0, s, "v"], held[1, s, "v"]).astype(gvr.dtype)


def layer_kernel(
    ndp, nt,
    w_qkv, w_out, w_in, w_down, gains_in, hid_in, cot_in, seg, freq,
    out_o, gin_o, wf_o, grad_qkv, grad_out, grad_in, grad_down, grad_gains,
    hid, cot, q, k, v, k2, v2, n1, mixed, lse, cos, sin, augk, augq, gains,
    sh1, sh2, sh3, seg_o,
    w3, wo, wd, gate, up, gp, prod, gu, n2, low, gres, gtot, gmixed, out, ak, av, gsum,
    local, ss, so, ro, si, ri, sg, rg, *rest,
):
    n, d = hid.shape
    ff = wd.shape[1]
    el, fl = d // nt, ff // nt
    split = (2, 2, 2, d // 8)
    g2, g3, g1, g0 = rest[0], rest[7], rest[14], rest[21]
    gin, gk2, gv2 = gmixed, low, n2
    me = Place(ndp, nt)
    b0, b1, b2 = me.b
    me.barrier(True)
    second, third, save, hs, cs, ce = forward_part(
        me, w_qkv, w_out, w_in, w_down, gains_in, hid_in, cot_in, seg, freq, wf_o,
        hid, cot, q, k, v, k2, v2, n1, w3, mixed, lse, cos, sin, augk, augq, gains,
        sh1, sh2, sh3, seg_o, gtot, g1, g2, g3, local, *rest[28:],
    )
    rs2 = Scatter(me, g2, rest[1:5], *rest[5:7])
    rs3 = Scatter(me, g3, rest[8:12], *rest[12:14])
    rs1 = Scatter(me, g1, rest[15:19], *rest[19:21])
    rs0 = Scatter(me, g0, rest[22:26], *rest[26:28], spread=False)
    lo_s, lo_e = leave_copies(me, out, out_o, so, ro)
    gi_s, gi_e = leave_copies(me, gin, gin_o, si, ri)
    gain_one, gain_two = gains[0:1, :], gains[1:2, :]
    blocks, pairs = range(nt), d // (2 * HD)
    third.finish()
    for t in blocks:
        wo[:, t * el : (t + 1) * el] = g3[:, :, :, t, :, :el].reshape(d, el)
    gres[...] = dot(mixed[...], wo[...], NT)

    def norm(at):
        value = hid[at, :].astype(F32) + gres[at, :]
        gres[at, :] = value
        n2[at, :] = (standard(value)[0] * gain_two).astype(BF)

    rows_loop(n, 64, norm)
    save.wait()
    second.finish()
    for t in blocks:
        at = slice(t * fl, (t + 1) * fl)
        w3[:, at] = g2[:, :, :, t, :, :fl].reshape(d, fl)
        w3[:, ff + t * fl : ff + (t + 1) * fl] = g2[:, :, :, t, :, fl : 2 * fl].reshape(d, fl)
        wd[:, at] = g2[:, :, :, t, :, 2 * fl : 3 * fl].reshape(d, fl)
    for e in ce:
        e.wait_recv()
    wait_sends(hs)
    wait_sends(cs)
    gate[...] = dot(n2[...], w3[:, :ff])
    up[...] = dot(n2[...], w3[:, ff:])
    gp[...] = dot(cot[...], wd[...])

    def geglu(at):
        for j in range(0, ff, 384):
            to = slice(j, j + 384)
            g, u, p = gate[at, to], up[at, to], gp[at, to]
            cdf = 0.5 + 0.5 * erf(g * math.sqrt(0.5))
            pdf = jnp.exp(-0.5 * g * g) * (1.0 / math.sqrt(2 * math.pi))
            act = g * cdf
            prod[at, to] = (act * u).astype(BF)
            gu[at, to] = (p * u * (cdf + g * pdf)).astype(BF)
            gu[at, ff + j : ff + j + 384] = (p * act).astype(BF)

    rows_loop(n, 32, geglu)
    n2t, cott = n2[...].T, cot[...].T
    for t in blocks:
        at = slice(t * fl, (t + 1) * fl)
        also = slice(ff + t * fl, ff + (t + 1) * fl)
        g2[:, :, :, t, :, :fl] = dot(n2t, gu[:, at]).astype(BF).reshape(*split, fl)
        g2[:, :, :, t, :, fl : 2 * fl] = dot(n2t, gu[:, also]).astype(BF).reshape(*split, fl)
        g2[:, :, :, t, :, 2 * fl : 3 * fl] = dot(cott, prod[:, at]).astype(BF).reshape(*split, fl)
        rs2.core[t].start()
    out[...] = (gres[...] + dot(prod[...], wd[...], NT)).astype(BF)
    start_all(lo_s)
    rs2.add_core(0)
    rs2.add_core(1)
    gtot[...] = dot(gu[...], w3[...], NT)
    load_wf = pltpu.make_async_copy(wf_o, w3, local.at[1])
    load_wf.start()
    gsum[...] = jnp.zeros_like(gsum)
    for t in range(2, nt):
        rs2.add_core(t)

    def back_two(at):
        xhat, scale = standard(gres[at, :])
        e = gtot[at, :]
        gsum[0] += jnp.sum((e * xhat).reshape(-1, 8, d), axis=0)
        total = cot[at, :].astype(F32) + norm_back(e, xhat, scale, gain_two)
        gres[at, :] = total
        low[at, :] = total.astype(BF)

    rows_loop(n, 64, back_two)
    lowt = low[...].T
    for t in blocks:
        to = slice(t * el, (t + 1) * el)
        g3[:, :, :, t, :, :el] = dot(lowt, mixed[:, to]).astype(BF).reshape(*split, el)
        rs3.core[t].start()
    gmixed[...] = dot(low[...], wo[...]).astype(BF)
    rs2.add_one(0)
    rs2.add_one(1)
    gq, gk, gv = gate, up, gp

    buddy = me.pair(1 - me.core, me.z)
    swaps = []
    for i in range(2):
        at = pl.ds(i * d // 2, d // 2)
        for j, (src, dst) in enumerate(((gk2, ak), (gv2, av))):
            m = 2 * i + j
            swaps.append(remote(src.at[:, at], dst.at[:, at], ss.at[m], ss.at[4 + m], buddy))
    raw = gu

    def back_rope(half):
        def body(at):
            c, s = cos[at, :], -sin[at, :]
            for j in range(half * d // 2, (half + 1) * d // 2, 128):
                to = slice(j, j + 128)
                raw[at, j : j + 128] = turned(gq[at, to], c, s).astype(BF)
                keys = gk[at, to] + ak[at, to].astype(F32)
                raw[at, d + j : d + j + 128] = turned(keys, c, s).astype(BF)
                raw[at, 2 * d + j : 2 * d + j + 128] = (gv[at, to] + av[at, to].astype(F32)).astype(BF)

        rows_loop(n, 32, body)

    def grads_one(n1t, t):
        for c in range(3):
            cols = raw[:, c * d + t * el : c * d + (t + 1) * el]
            g1[:, :, :, t, :, c * el : (c + 1) * el] = dot(n1t, cols).astype(BF).reshape(*split, el)

    def step(i, carry):
        attend_back_pair(i, q, k, k2, v, v2, gmixed, mixed, lse, augk, augq, gq, gk, gk2, gv, gv2)

        @pl.when(i == 0)
        def _():
            for t in blocks:
                rs3.add_core(t)

        @pl.when(i == pairs // 2 - 1)
        def _():
            for swap in swaps[:2]:
                swap.start()
            for t in range(2, nt):
                rs2.add_one(t)

        @pl.when(i == pairs // 2)
        def _():
            for swap in swaps[:2]:
                swap.wait()
            back_rope(0)
            n1t = n1[...].T
            for t in range(nt // 2):
                grads_one(n1t, t)
                rs1.core[t].start()
            rs2.add_two(0)
            rs2.add_two(1)
            for t in blocks:
                rs3.add_one(t)

        return carry

    lax.fori_loop(0, pairs, step, 0)
    for swap in swaps[2:]:
        swap.start()
    for t in range(nt // 2):
        rs1.add_core(t)
    for t in range(2, nt):
        rs2.add_two(t)
    for swap in swaps[2:]:
        swap.wait()
    back_rope(1)
    n1t = n1[...].T
    for t in range(nt // 2, nt):
        grads_one(n1t, t)
        rs1.core[t].start()
    load_wf.wait()
    gtot[...] = dot(raw[...], w3[...], NT)
    for t in blocks:
        rs3.add_two(t)
    for t in range(nt // 2):
        rs1.add_one(t)
    for t in range(nt // 2, nt):
        rs1.add_core(t)

    def back_one(at):
        xhat, scale = standard(hid[at, :].astype(F32))
        e = gtot[at, :]
        gsum[1] += jnp.sum((e * xhat).reshape(-1, 8, d), axis=0)
        gin[at, :] = (gres[at, :] + norm_back(e, xhat, scale, gain_one)).astype(BF)

    for t in blocks:
        rows_loop(n // nt, 64, back_one, t * (n // nt))
        start_all(gi_s[t : t + 1])
    rows = []
    for v_ in (gsum[1], gsum[0]):
        total = jnp.sum(v_, axis=0, keepdims=True)
        upper = total.astype(BF).astype(F32)
        rows += [upper, total - upper]
    rows.append(jnp.zeros((SPARE - 4, d), F32))
    g0[...] = jnp.zeros_like(g0)
    g0[:, :, :, 0, :, :SPARE] = jnp.concatenate(rows, axis=0).T.astype(BF).reshape(*split, SPARE)
    rs0.core[0].start()
    for t in range(nt // 2):
        rs1.add_two(t)
    rs0.add_core(0)
    for t in range(nt // 2, nt):
        rs1.add_one(t)
    total = rs3.total()
    grad_out[...] = total[:, :el].T
    rs0.add_one(0)
    total = rs2.total()
    grad_in[0] = total[:, :fl]
    grad_in[1] = total[:, fl : 2 * fl]
    grad_down[...] = total[:, 2 * fl : 3 * fl].T
    for t in range(nt // 2, nt):
        rs1.add_two(t)
    rs0.add_two(0)
    mine = g0.at[b2, b1, b0, 0]
    gain_copies = [
        remote(mine, rs0.rz.at[s - 1], sg.at[s - 1], rg.at[s - 1], me.along(s)) for s in range(1, nt)
    ]
    for cp in gain_copies:
        cp.start()
    total = rs1.total()
    for c in range(3):
        grad_qkv[c] = total[:, c * el : (c + 1) * el]
    tail = mine[...].astype(F32)
    for s, cp in enumerate(gain_copies):
        cp.wait()
        tail = tail + rs0.rz[s].astype(F32)
    tail = tail.T[:SPARE]
    grad_gains[...] = jnp.concatenate([tail[0:1] + tail[1:2], tail[2:3] + tail[3:4]], axis=0)
    for e in lo_e + gi_e:
        e.wait_recv()
    rs2.finish()
    rs3.finish()
    rs1.finish()
    rs0.finish()
    wait_sends(lo_s)
    wait_sends(gi_s)


def layer(ndp, nt, w_qkv, w_out, w_in, w_down, gains, hid, cot, seg):
    half, d = hid.shape[2:]
    n = nt * half
    r, el, fl = w_qkv.shape[1], w_qkv.shape[2], w_in.shape[2]
    ff = fl * nt
    c1, c2, c3 = padded(3 * el + SPARE), padded(3 * fl), padded(el)
    freq = jnp.tile(THETA ** (-2.0 * jnp.arange(HD // 2, dtype=F32) / HD), 4)[None]
    sds = jax.ShapeDtypeStruct
    dma = pltpu.SemaphoreType.DMA
    vm, hbm = pl.BlockSpec(memory_space=VM), pl.BlockSpec(memory_space=pl.ANY)
    wide, act, act32 = VM((n, ff), F32), VM((n, d), BF), VM((n, d), F32)
    return pl.pallas_call(
        functools.partial(layer_kernel, ndp, nt),
        in_specs=[vm] * 5 + [hbm] * 2 + [vm] * 2,
        out_specs=[hbm] * 3 + [vm] * 5,
        out_shape=[sds((2, 2, half, d), BF)] * 2
        + [
            sds((d, 3 * d), BF),
            sds((3, r, el), F32),
            sds((el, r), F32),
            sds((2, r, fl), F32),
            sds((fl, r), F32),
            sds((2, r), F32),
        ],
        scratch_shapes=[act] * 9
        + [VM((d // (2 * HD), 2, n), F32)]
        + [VM((n, 2 * HD), F32)] * 2
        + [VM((2 * n, 2 * HD), BF), VM((HD, n), BF), VM((SPARE, d), F32)]
        + [VM((r, c), BF) for c in (c1, c2, c3)]
        + [VM(seg.shape, seg.dtype)]
        + [VM((d, 2 * ff), BF), VM((d, d), BF), VM((d, ff), BF)]
        + [wide] * 3
        + [VM((n, ff), BF), VM((n, 2 * ff), BF), act, act, act32, act32]
        + [act] * 4
        + [VM((2, 8, d), F32), dma((2,)), dma((8,))]
        + [dma((4,))] * 4
        + [dma((nt - 1,))] * 2
        + scatter_scratch(nt, r, c2, nt)
        + scatter_scratch(nt, r, c3, nt)
        + scatter_scratch(nt, r, c1, nt)
        + scatter_scratch(nt, r, 128, 1)
        + [dma((nt, 6))] * 6
        + [dma((3,))]
        + [dma((4,))] * 4
        + [dma((6,))],
        compiler_params=pltpu.CompilerParams(
            collective_id=0, has_side_effects=True, vmem_limit_bytes=WIDE
        ),
        name="layer",
    )(w_qkv, w_out, w_in, w_down, gains, hid, cot, seg, freq)


def finish_kernel(count, *refs):
    arrays, outs, held, (sems, more) = refs[:count], refs[count : 2 * count], refs[2 * count : 3 * count], refs[3 * count :]
    ins = [pltpu.make_async_copy(a, h, sems.at[i]) for i, (a, h) in enumerate(zip(arrays, held))]
    ends = [pltpu.make_async_copy(h, o, more.at[i]) for i, (h, o) in enumerate(zip(held, outs))]
    for copy in ins:
        copy.start()
    for copy, end in zip(ins, ends):
        copy.wait()
        end.start()
    for end in ends:
        end.wait()


def finish(arrays):
    hbm = pl.BlockSpec(memory_space=pl.ANY)
    count = len(arrays)
    return pl.pallas_call(
        functools.partial(finish_kernel, count),
        in_specs=[hbm] * count,
        out_specs=[hbm] * count,
        out_shape=[jax.ShapeDtypeStruct(a.shape, a.dtype) for a in arrays],
        scratch_shapes=[VM(a.shape, a.dtype) for a in arrays] + [pltpu.SemaphoreType.DMA((count,))] * 2,
        compiler_params=pltpu.CompilerParams(vmem_limit_bytes=WIDE),
        name="finish",
    )(*arrays)


def shards(hidden_in, cotangent, segment_ids, w_qkv, w_out, w_in, w_down, norm_gains):
    ndp, nt = lax.axis_size("dp"), lax.axis_size("tensor")
    stride = ndp // 8
    rows, local_len, d = hidden_in.shape
    half = local_len // 2
    low_groups = [[h * stride + i for i in range(stride)] for h in range(8)]

    def widen(v, axis):
        if stride == 1:
            return v
        return lax.all_gather(v, "dp", axis_index_groups=low_groups, axis=axis, tiled=True)

    def narrow(v, axis):
        if stride == 1:
            return v
        return lax.psum_scatter(
            v, "dp", scatter_dimension=axis, axis_index_groups=low_groups, tiled=True
        )

    split = lambda v: v.reshape(2, 2, half, d)
    out, gin, _, *grads = layer(
        ndp, nt,
        widen(w_qkv, 1), widen(w_out, 1), widen(w_in, 1), widen(w_down, 1), widen(norm_gains, 1),
        split(hidden_in), split(cotangent), segment_ids,
    )
    layer_out, grad_input, grad_qkv, grad_out, grad_in, grad_down, grad_gains = finish([out, gin, *grads])
    back = lambda t: t.reshape(rows, local_len, d)
    return (
        back(layer_out),
        back(grad_input),
        narrow(grad_qkv, 1),
        narrow(grad_out, 1),
        narrow(grad_in, 1),
        narrow(grad_down, 1),
        narrow(grad_gains, 1),
    )


def solution(mesh):
    placed = (
        P("dp", "tensor", None),
        P("dp", "tensor", None),
        P("dp", None),
        P(None, "dp", "tensor"),
        P("tensor", "dp"),
        P(None, "dp", "tensor"),
        P("tensor", "dp"),
        P(None, "dp"),
    )
    return jax.shard_map(
        shards,
        mesh=mesh,
        in_specs=placed,
        out_specs=(
            P("dp", "tensor", None),
            P("dp", "tensor", None),
            P(None, "dp", "tensor"),
            P("tensor", "dp"),
            P(None, "dp", "tensor"),
            P("tensor", "dp"),
            P(None, "dp"),
        ),
        check_vma=False,
    )
```

```python
import functools
import math

import jax
import jax.numpy as jnp
from jax import lax
from jax.experimental import pallas as pl
from jax.experimental.pallas import tpu as pltpu
from jax.sharding import PartitionSpec as P

HD = 64
EPS = 1e-05
THETA = 160000.0
BIG = 1e30
SEGS = 8
SPARE = 8
TO_EXP2 = math.log2(math.e) / math.sqrt(HD)
MESH = pl.DeviceIdType.MESH
BF, F32 = jnp.bfloat16, jnp.float32
VM = pltpu.VMEM
WIDE = 60 * 1024 * 1024


def dot(a, b, dims=((1,), (0,))):
    return lax.dot_general(a, b, (dims, ((), ())), preferred_element_type=F32)


NT = ((1,), (1,))


def padded(n):
    return -(-n // 128) * 128


def erf(x):
    x = jnp.clip(x, -3.832506856900711, 3.832506856900711)
    s = x * x
    p = 0.00022905065861350646
    for c in (0.0034082910107109506, 0.050955695062380861, 0.18520832239976145, 1.128379143519084):
        p = p * s + c
    q = -1.1791602954361697e-7
    for c in (
        0.000023547966471313185,
        0.0010179625278914885,
        0.014070470171167667,
        0.11098505178285362,
        0.49746925110067538,
        1.0,
    ):
        q = q * s + c
    return x * p / q


class Place:
    def __init__(self, ndp, nt):
        self.nt = nt
        self.stride = ndp // 8
        self.dp, self.z = lax.axis_index("dp"), lax.axis_index("tensor")
        high = self.dp // self.stride
        self.b = (high % 2, (high // 2) % 2, high // 4)
        self.core = self.dp % 2

    def flip(self, bit):
        return (self.dp + (1 - 2 * self.b[bit]) * self.stride * 2**bit, self.z)

    def along(self, step):
        return (self.dp, (self.z + step) % self.nt)

    def pair(self, core, z):
        return (self.dp - self.core + core, z)

    def barrier(self, group):
        others = [self.along(s) for s in range(1, self.nt)]
        others += [self.flip(1), self.flip(2)]
        if group or self.stride == 1:
            others += [self.pair(1 - self.core, self.z)]
        if self.stride > 1:
            others += [self.flip(0)]
        if group:
            others += [self.pair(1 - self.core, (self.z + s) % self.nt) for s in range(1, self.nt)]
        sem = pltpu.get_barrier_semaphore()
        for device in others:
            pl.semaphore_signal(sem, inc=1, device_id=device, device_id_type=MESH)
        pl.semaphore_wait(sem, len(others))


def remote(src, dst, send, recv, device):
    return pltpu.make_async_remote_copy(
        src_ref=src, dst_ref=dst, send_sem=send, recv_sem=recv, device_id=device, device_id_type=MESH
    )


def enter_copies(me, src, dst, send, recv):
    starts, ends = [], []
    half = src.shape[2]
    slot = lambda z: dst.at[pl.ds(pl.multiple_of(z * half, half), half)]
    for row in range(2):
        for core in range(2):
            z = 2 * me.core + row
            k = 2 * row + core
            here = jnp.logical_and(z == me.z, core == me.core)
            copy = remote(src.at[row, core], slot(me.z), send.at[k], recv.at[me.z], me.pair(core, z))
            local = pltpu.make_async_copy(src.at[row, core], slot(me.z), recv.at[me.z])
            starts.append((here, copy, local))
    for z in range(me.nt):
        ends.append(remote(src.at[0, 0], slot(z), send.at[0], recv.at[z], me.pair(1 - me.core, z)))
    return starts, ends


def leave_copies(me, src, dst, send, recv):
    starts, ends = [], []
    half = dst.shape[2]
    for z in range(me.nt):
        here = jnp.logical_and(z == me.z, me.z // 2 == me.core)
        k = 2 * (me.z % 2) + me.core
        to = dst.at[me.z % 2, me.core]
        copy = remote(src.at[z * half : (z + 1) * half], to, send.at[z], recv.at[k], me.pair(me.z // 2, z))
        local = pltpu.make_async_copy(src.at[z * half : (z + 1) * half], to, recv.at[k])
        starts.append((here, copy, local))
    for k in range(4):
        ends.append(remote(src.at[:half], dst.at[k // 2, k % 2], send.at[0], recv.at[k], me.pair(1 - me.core, me.z)))
    return starts, ends


def start_all(starts):
    for here, copy, local in starts:
        pl.when(here)(local.start)
        pl.when(jnp.logical_not(here))(copy.start)


def wait_sends(starts):
    for here, copy, _ in starts:
        pl.when(jnp.logical_not(here))(copy.wait_send)


class Gather:
    def __init__(self, me, shard, out, send, recv, own):
        self.me, self.shard, self.out = me, shard, out
        b0, b1, b2 = me.b
        nt = me.nt
        both = pl.ds(0, 2)
        x, y, core = me.flip(1), me.flip(2), me.flip(0)
        o0, o1, o2 = 1 - b0, 1 - b1, 1 - b2
        self.mine = pltpu.make_async_copy(shard, out.at[b2, b1, b0, me.z], own)
        self.z, self.one, self.two, self.core = [], [], [], []
        for s in range(nt):
            t = (me.z + nt - s) % nt

            def pair(k, at, other, device, s=s, t=t):
                sems = send.at[s, k], recv.at[s, k]
                cp = remote(out.at[(*at, t)], out.at[(*at, t)], *sems, device)
                return cp, remote(out.at[(*other, t)], out.at[(*other, t)], *sems, device)

            if s:
                sems = send.at[s, 0], recv.at[s, 0]
                to, frm = out.at[b2, b1, b0, me.z], out.at[b2, b1, b0, t]
                self.z.append((remote(shard, to, *sems, me.along(s)), remote(shard, frm, *sems, me.along(s))))
            else:
                self.z.append(None)
            if s % 2 == 0:
                self.one.append(pair(1, (b2, b1, b0), (b2, o1, b0), x))
                self.two.append(pair(2, (b2, both, b0), (o2, both, b0), y))
                got_one, got_two = (b2, o1), (o2, both)
            else:
                self.one.append(pair(1, (b2, b1, b0), (o2, b1, b0), y))
                self.two.append(pair(2, (both, b1, b0), (both, o1, b0), x))
                got_one, got_two = (o2, b1), (both, o1)
            self.core.append(
                [
                    pair(3, (b2, b1, b0), (b2, b1, o0), core),
                    pair(4, (*got_one, b0), (*got_one, o0), core),
                    pair(5, (*got_two, b0), (*got_two, o0), core),
                ]
            )

    def start_z(self):
        self.mine.start()
        for cp, _ in self.z[1:]:
            cp.start()

    def after_z(self, s):
        if s:
            self.z[s][1].wait_recv()
        else:
            self.mine.wait()
        self.one[s][0].start()
        self.core[s][0][0].start()

    def after_one(self, s):
        self.one[s][1].wait_recv()
        self.two[s][0].start()
        self.core[s][1][0].start()

    def after_two(self, s):
        self.two[s][1].wait_recv()
        self.core[s][2][0].start()

    def finish(self):
        for group in self.core:
            for _, back in group:
                back.wait_recv()
        for cp, _ in self.z[1:] + self.one + self.two + sum(self.core, []):
            cp.wait_send()


class Scatter:
    def __init__(self, me, g, bufs, send, recv):
        self.me, self.g = me, g
        self.r0, self.r1, self.r2, self.rz = bufs
        b0, b1, b2 = me.b
        o0, o1, o2 = 1 - b0, 1 - b1, 1 - b2
        nt = me.nt
        both = pl.ds(0, 2)
        x, y, core = me.flip(1), me.flip(2), me.flip(0)
        self.core, self.one, self.two, self.z, self.back = [], [], [], [], []
        for t in range(nt):
            sems = [(send.at[t, k], recv.at[t, k]) for k in range(3)]
            one, two = (g.at[both, o1, b0, t], g.at[o2, b1, b0, t]), (x, y)
            if t % 2:
                one, two = (g.at[o2, both, b0, t], g.at[b2, o1, b0, t]), (y, x)
            self.core.append(remote(g.at[both, both, o0, t], self.r0.at[t], *sems[0], core))
            self.one.append(remote(one[0], self.r1.at[t], *sems[1], two[0]))
            self.two.append(remote(one[1], self.r2.at[t], *sems[2], two[1]))
            slot = (t - me.z + nt - 1) % nt
            slot = jnp.minimum(slot, nt - 2)
            self.z.append(
                remote(g.at[b2, b1, b0, t], self.rz.at[slot], send.at[t, 3], recv.at[slot, 3], (me.dp, t))
            )
        for s in range(nt - 1):
            self.back.append(
                remote(g.at[b2, b1, b0, 0], self.rz.at[s], send.at[s, 3], recv.at[s, 3], me.along(1))
            )

    def add(self, count, at, buf, got):
        tiles = self.g.shape[4] // 32

        def body(i, carry):
            rows = pl.ds(pl.multiple_of(i % tiles * 32, 32), 32)
            here, there = (*at(i // tiles), rows), (*got(i // tiles), rows)
            self.g[here] = (self.g[here].astype(F32) + buf[there].astype(F32)).astype(BF)
            return carry

        lax.fori_loop(0, count * tiles, body, 0)

    def add_core(self, t):
        b0 = self.me.b[0]
        self.core[t].wait_recv()
        self.add(4, lambda i: (i // 2, i % 2, b0, t), self.r0, lambda i: (t, i // 2, i % 2))
        self.one[t].start()

    def add_one(self, t):
        b0, b1, b2 = self.me.b
        self.one[t].wait_recv()
        self.add(2, lambda i: (b2, i, b0, t) if t % 2 else (i, b1, b0, t), self.r1, lambda i: (t, i))
        self.two[t].start()

    def add_two(self, t):
        b0, b1, b2 = self.me.b
        self.two[t].wait_recv()
        self.add(1, lambda i: (b2, b1, b0, t), self.r2, lambda i: (t,))
        pl.when(self.me.z != t)(self.z[t].start)

    def total(self):
        b0, b1, b2 = self.me.b
        total = self.g[b2, b1, b0, self.me.z].astype(F32)
        for s in range(self.me.nt - 1):
            self.back[s].wait_recv()
            total = total + self.rz[s].astype(F32)
        return total

    def finish(self):
        for cp in self.core + self.one + self.two:
            cp.wait_send()
        for t, cp in enumerate(self.z):
            pl.when(self.me.z != t)(cp.wait_send)


def scatter_scratch(nt, r, c):
    dma = pltpu.SemaphoreType.DMA
    return [
        VM((2, 2, 2, nt, r, c), BF),
        VM((nt, 2, 2, r, c), BF),
        VM((nt, 2, r, c), BF),
        VM((nt, r, c), BF),
        VM((nt - 1, r, c), BF),
        dma((nt, 4)),
        dma((nt, 4)),
    ]


def standard(v):
    centred = v - jnp.mean(v, axis=-1, keepdims=True)
    scale = lax.rsqrt(jnp.mean(centred * centred, axis=-1, keepdims=True) + EPS)
    return centred * scale, scale


def norm_back(grad, xhat, scale, gain):
    e = grad * gain
    inner = jnp.mean(e * xhat, axis=-1, keepdims=True)
    return scale * (e - jnp.mean(e, axis=-1, keepdims=True) - xhat * inner)


def rows_loop(total, step, body, start=0):
    def run(i, carry):
        body(pl.ds(pl.multiple_of(start + i * step, step), step))
        return carry

    lax.fori_loop(0, total // step, run, 0)


def turned(v, cosine, sine):
    lane = lax.broadcasted_iota(jnp.int32, v.shape, 1)
    other = jnp.where(lane % HD < HD // 2, pltpu.roll(v, 128 - HD // 2, 1), pltpu.roll(v, HD // 2, 1))
    return v * cosine + other * sine


def half_lanes(shape):
    return lax.broadcasted_iota(jnp.int32, shape, 1) < HD


def attend_pair(i, q, k, k2, v, v2, augk, augq, mixed, lse):
    at = pl.ds(pl.multiple_of(i * 2 * HD, 2 * HD), 2 * HD)
    keys = jnp.concatenate([k[:, at], k2[:, at]], axis=0)
    vt = jnp.concatenate([v[:, at], v2[:, at]], axis=0).T
    qt = q[:, at].T
    low = half_lanes(keys.shape)
    ones = jnp.ones((HD, vt.shape[1]), BF)
    outs = []
    for h in range(2):
        if h == 0:
            keys_h = jnp.where(low, keys, augk[...])
            q_h = jnp.concatenate([qt[:HD], augq[...]], axis=0)
            v_h = jnp.concatenate([vt[:HD], ones], axis=0)
        else:
            keys_h = jnp.where(low, augk[...], keys)
            q_h = jnp.concatenate([augq[...], qt[HD:]], axis=0)
            v_h = jnp.concatenate([ones, vt[HD:]], axis=0)
        scores = dot(keys_h, q_h)
        top = jnp.max(scores, axis=0, keepdims=True)
        expo = jnp.exp2((scores - top) * TO_EXP2).astype(BF)
        got = dot(v_h, expo)
        value, total = (got[:HD], got[HD:]) if h == 0 else (got[HD:], got[:HD])
        outs.append(value / total)
        lse[i, h : h + 1, :] = top + jnp.log2(total[:1]) * (1.0 / TO_EXP2)
    mixed[:, at] = jnp.concatenate(outs, axis=0).T.astype(BF)


def column(row):
    return jnp.concatenate([row] * 8, axis=0).T[:, :1]


def masks(me, row, half, freq, cos, sin, augk, augq):
    n = me.nt * half
    part = lambda core: jnp.concatenate(
        [row[:, (2 * z + core) * half : (2 * z + core + 1) * half] for z in range(me.nt)], axis=1
    ).astype(F32)
    even, odd = part(0), part(1)
    seg_q, seg_o = jnp.where(me.core == 0, even, odd), jnp.where(me.core == 0, odd, even)
    whole = jnp.concatenate([seg_q, seg_o], axis=1)
    mine = column(seg_q)
    spot = lax.broadcasted_iota(jnp.int32, (n, 1), 0)
    spot = spot + (spot // half) * half + me.core * half
    first = jnp.zeros((n, 1), F32)
    for s in range(SEGS - 2):
        count = jnp.sum((whole == s).astype(F32), axis=1, keepdims=True)
        first = first + jnp.where(mine > s, count, 0.0)
    angle = (spot.astype(F32) - first) * freq[...]
    cos[...] = jnp.cos(angle)
    sines = jnp.sin(angle)
    lane = lax.broadcasted_iota(jnp.int32, sines.shape, 1)
    sin[...] = jnp.where(lane % HD < HD // 2, -sines, sines)
    for s, seg in enumerate((mine, column(seg_o))):
        ids = lax.broadcasted_iota(jnp.int32, (n, 2 * HD), 1) % HD
        hot = jnp.logical_or(seg == ids.astype(F32), jnp.logical_and(ids >= SEGS, ids < SEGS + 3))
        augk[s * n : (s + 1) * n, :] = jnp.where(hot, 1.0, 0.0).astype(BF)
    ids = lax.broadcasted_iota(jnp.int32, (HD, n), 0)
    off = jnp.logical_and(ids < SEGS, seg_q != ids.astype(F32))
    augq[...] = jnp.where(off, -BIG, 0.0).astype(BF)


def forward_part(
    me, w_qkv, w_out, w_in, w_down, gains_in, hid_in, cot_in, seg, freq, wf_o,
    hid, cot, q, k, v, k2, v2, n1, wf, mixed, lse, cos, sin, augk, augq, gains,
    w1, w2, w3, seg_o, raw, g1, g2, g3, local, s1, r1, s2, r2, s3, r3, own, se, re, sc, rc, ss,
):
    nt = me.nt
    n, d = hid.shape
    el, fl = w_qkv.shape[2], w_in.shape[2]
    r = w_qkv.shape[1]
    half = n // nt
    first = Gather(me, w1, g1, s1, r1, own.at[0])
    second = Gather(me, w2, g2, s2, r2, own.at[1])
    third = Gather(me, w3, g3, s3, r3, own.at[2])
    all_one = g1
    hs, he = enter_copies(me, hid_in, hid, se, re)
    cs, ce = enter_copies(me, cot_in, cot, sc, rc)
    buddy = me.pair(1 - me.core, me.z)
    swap = remote(seg, seg_o, ss.at[0], ss.at[3], buddy)
    swap.start()
    for c in range(3):
        w1[:, c * el : (c + 1) * el] = w_qkv[c]
    spare = w1.shape[1] - 3 * el
    cols = jnp.concatenate([gains_in[...].astype(F32), jnp.zeros((spare - 2, r), F32)], axis=0)
    w1[:, 3 * el :] = cols.T.astype(BF)
    first.start_z()
    start_all(hs)
    w2[...] = jnp.zeros_like(w2)
    w2[:, :fl] = w_in[0]
    w2[:, fl : 2 * fl] = w_in[1]
    w2[:, 2 * fl : 3 * fl] = w_down[...].astype(F32).T.astype(BF)
    w3[...] = jnp.zeros_like(w3)
    w3[:, :el] = w_out[...].astype(F32).T.astype(BF)
    blocks = range(nt)
    for s in blocks:
        first.after_z(s)
    swap.wait()
    here = me.z // 2 == me.core
    index = me.z % 2
    both = jnp.where(here, seg[...], seg_o[...])
    row = jnp.where(index == 0, both[:1], both[1:2])
    masks(me, row, half, freq, cos, sin, augk, augq)
    for s in blocks:
        first.after_one(s)
    for e in he:
        e.wait_recv()
    third.start_z()
    second.start_z()

    def spread(at):
        raw[at, :] = standard(hid[at, :].astype(F32))[0]

    rows_loop(n, 64, spread)
    for s in blocks:
        first.after_two(s)
    first.finish()
    third.after_z(0)
    second.after_z(0)
    top = all_one[:, :, :, 0, :, 3 * el : 3 * el + SPARE].reshape(d, SPARE).astype(F32).T
    gains[...] = top
    gain = top[:1]

    def norm(at):
        n1[at, :] = (raw[at, :] * gain).astype(BF)

    rows_loop(n, 64, norm)
    for t in range(nt):
        for c in range(3):
            block = all_one[:, :, :, t, :, c * el : (c + 1) * el]
            wf[:, c * d + t * el : c * d + (t + 1) * el] = block.reshape(d, el)
    swaps = [remote(k, k2, ss.at[1], ss.at[4], buddy), remote(v, v2, ss.at[2], ss.at[5], buddy)]
    for c, out in ((1, k), (2, v), (0, q)):
        raw[...] = dot(n1[...], wf[:, c * d : (c + 1) * d])

        def finish(at, c=c, out=out):
            for j in range(0, d, 128):
                value = raw[at, j : j + 128]
                if c < 2:
                    value = turned(value, cos[at, :], sin[at, :])
                out[at, j : j + 128] = value.astype(BF)

        rows_loop(n, 64, finish)
        if c:
            swaps[c - 1].start()
            third.after_z(c)
            second.after_z(c)
    save = pltpu.make_async_copy(wf, wf_o, local.at[0])
    save.start()
    for s in swaps:
        s.wait()
    for s in range(3, nt):
        third.after_z(s)
        second.after_z(s)
    start_all(cs)
    pairs = d // (2 * HD)

    def step(i, carry):
        attend_pair(i, q, k, k2, v, v2, augk, augq, mixed, lse)

        @pl.when(i == 0)
        def _():
            for s in range(2):
                third.after_one(s)
                second.after_one(s)

        @pl.when(i == pairs // 2 - 1)
        def _():
            for s in range(2, nt):
                third.after_one(s)
                second.after_one(s)
            third.after_two(0)
            second.after_two(0)

        return carry

    lax.fori_loop(0, pairs, step, 0)
    for s in range(1, nt):
        third.after_two(s)
        second.after_two(s)
    return second, third, save, hs, cs, ce


def split_rows(value, n, rows):
    parts = []
    for _ in range(n):
        part = value.astype(BF).astype(F32)
        parts.append(part)
        value = value - part
    parts.append(jnp.zeros((rows - n, value.shape[1]), F32))
    return jnp.concatenate(parts, axis=0).astype(BF)


def attend_back_pair(i, q, k, k2, v, v2, g, mixed, lse, augk, augq, gq, gk, gk2, gv, gv2):
    at = pl.ds(pl.multiple_of(i * 2 * HD, 2 * HD), 2 * HD)
    rows = q.shape[0]
    grads, query = g[:, at], q[:, at]
    gt, qt = grads.T, query.T
    prod = gt.astype(F32) * mixed[:, at].T.astype(F32)
    gq_parts = []
    sides = [(k, v, gk, gv), (k2, v2, gk2, gv2)]
    low = half_lanes((rows, 2 * HD))
    one = jnp.ones((rows, 2 * HD), BF)
    held = {}
    for h in range(2):
        mine = slice(h * HD, (h + 1) * HD)

        def swapped(a, b, h=h):
            return (a, b) if h == 0 else (b, a)

        inner = jnp.sum(prod[mine], axis=0, keepdims=True)
        neg = split_rows(-lse[i, h : h + 1, :], 3, SEGS)
        extra_q = jnp.concatenate([augq[:SEGS], neg, augq[2 * SEGS :]], axis=0)
        extra_g = jnp.concatenate([split_rows(-inner, 2, 8), jnp.zeros((HD - 8, rows), BF)], axis=0)
        q_h = jnp.concatenate(swapped(qt[mine], extra_q), axis=0)
        g_h = jnp.concatenate(swapped(gt[mine], extra_g), axis=0)
        gq_h = None
        for s, (kr, vr, _, _) in enumerate(sides):
            aug = augk[s * rows : (s + 1) * rows, :]
            keys, values = kr[:, at], vr[:, at]
            probs = jnp.exp2(dot(jnp.where(low, *swapped(keys, aug)), q_h) * TO_EXP2)
            grad_p = dot(jnp.where(low, *swapped(values, one)), g_h)
            held[h, s, "v"] = dot(probs.astype(BF), grads)
            ds = (probs * grad_p).astype(BF)
            held[h, s, "k"] = dot(ds, query)
            part = dot(keys.T[mine], ds)
            gq_h = part if gq_h is None else gq_h + part
        gq_parts.append(gq_h)
    scale = 1.0 / math.sqrt(HD)
    gq[:, at] = jnp.concatenate(gq_parts, axis=0).T * scale
    for s, (_, _, gkr, gvr) in enumerate(sides):
        gkr[:, at] = (jnp.where(low, held[0, s, "k"], held[1, s, "k"]) * scale).astype(gkr.dtype)
        gvr[:, at] = jnp.where(low, held[0, s, "v"], held[1, s, "v"]).astype(gvr.dtype)


def layer_kernel(
    ndp, nt,
    w_qkv, w_out, w_in, w_down, gains_in, hid_in, cot_in, seg, freq,
    out_o, gin_o, wf_o, grad_qkv, grad_out, grad_in, grad_down, grad_gains,
    hid, cot, q, k, v, k2, v2, n1, mixed, lse, cos, sin, augk, augq, gains,
    sh1, sh2, sh3, seg_o,
    w3, wo, wd, gate, up, gp, prod, gu, n2, low, gres, gtot, gmixed, out, ak, av, gsum, rgain,
    local, ss, so, ro, si, ri, sg, rg, *rest,
):
    n, d = hid.shape
    ff = wd.shape[1]
    el, fl = d // nt, ff // nt
    split = (2, 2, 2, d // 8)
    g2, g3, g1 = rest[0], rest[7], rest[14]
    gin, gk2, gv2 = gmixed, low, n2
    me = Place(ndp, nt)
    b0, b1, b2 = me.b
    me.barrier(True)
    second, third, save, hs, cs, ce = forward_part(
        me, w_qkv, w_out, w_in, w_down, gains_in, hid_in, cot_in, seg, freq, wf_o,
        hid, cot, q, k, v, k2, v2, n1, w3, mixed, lse, cos, sin, augk, augq, gains,
        sh1, sh2, sh3, seg_o, gtot, g1, g2, g3, local, *rest[21:],
    )
    rs2 = Scatter(me, g2, rest[1:5], *rest[5:7])
    rs3 = Scatter(me, g3, rest[8:12], *rest[12:14])
    rs1 = Scatter(me, g1, rest[15:19], *rest[19:21])
    lo_s, lo_e = leave_copies(me, out, out_o, so, ro)
    gi_s, gi_e = leave_copies(me, gin, gin_o, si, ri)
    gain_one, gain_two = gains[0:1, :], gains[1:2, :]
    blocks, pairs = range(nt), d // (2 * HD)
    third.finish()
    for t in blocks:
        wo[:, t * el : (t + 1) * el] = g3[:, :, :, t, :, :el].reshape(d, el)
    gres[...] = dot(mixed[...], wo[...], NT)

    def norm(at):
        value = hid[at, :].astype(F32) + gres[at, :]
        gres[at, :] = value
        n2[at, :] = (standard(value)[0] * gain_two).astype(BF)

    rows_loop(n, 64, norm)
    save.wait()
    second.finish()
    for t in blocks:
        at = slice(t * fl, (t + 1) * fl)
        w3[:, at] = g2[:, :, :, t, :, :fl].reshape(d, fl)
        w3[:, ff + t * fl : ff + (t + 1) * fl] = g2[:, :, :, t, :, fl : 2 * fl].reshape(d, fl)
        wd[:, at] = g2[:, :, :, t, :, 2 * fl : 3 * fl].reshape(d, fl)
    for e in ce:
        e.wait_recv()
    wait_sends(hs)
    wait_sends(cs)
    gate[...] = dot(n2[...], w3[:, :ff])
    up[...] = dot(n2[...], w3[:, ff:])
    gp[...] = dot(cot[...], wd[...])

    def geglu(at):
        for j in range(0, ff, 384):
            to = slice(j, j + 384)
            g, u, p = gate[at, to], up[at, to], gp[at, to]
            cdf = 0.5 + 0.5 * erf(g * math.sqrt(0.5))
            pdf = jnp.exp(-0.5 * g * g) * (1.0 / math.sqrt(2 * math.pi))
            act = g * cdf
            prod[at, to] = (act * u).astype(BF)
            gu[at, to] = (p * u * (cdf + g * pdf)).astype(BF)
            gu[at, ff + j : ff + j + 384] = (p * act).astype(BF)

    rows_loop(n, 32, geglu)
    n2t, cott = n2[...].T, cot[...].T
    for t in blocks:
        at = slice(t * fl, (t + 1) * fl)
        also = slice(ff + t * fl, ff + (t + 1) * fl)
        g2[:, :, :, t, :, :fl] = dot(n2t, gu[:, at]).astype(BF).reshape(*split, fl)
        g2[:, :, :, t, :, fl : 2 * fl] = dot(n2t, gu[:, also]).astype(BF).reshape(*split, fl)
        g2[:, :, :, t, :, 2 * fl : 3 * fl] = dot(cott, prod[:, at]).astype(BF).reshape(*split, fl)
        rs2.core[t].start()
    out[...] = (gres[...] + dot(prod[...], wd[...], NT)).astype(BF)
    start_all(lo_s)
    rs2.add_core(0)
    rs2.add_core(1)
    gtot[...] = dot(gu[...], w3[...], NT)
    load_wf = pltpu.make_async_copy(wf_o, w3, local.at[1])
    load_wf.start()
    gsum[...] = jnp.zeros_like(gsum)
    for t in range(2, nt):
        rs2.add_core(t)

    def back_two(at):
        xhat, scale = standard(gres[at, :])
        e = gtot[at, :]
        gsum[0] += jnp.sum((e * xhat).reshape(-1, 8, d), axis=0)
        total = cot[at, :].astype(F32) + norm_back(e, xhat, scale, gain_two)
        gres[at, :] = total
        low[at, :] = total.astype(BF)

    rows_loop(n, 64, back_two)
    lowt = low[...].T
    for t in blocks:
        to = slice(t * el, (t + 1) * el)
        g3[:, :, :, t, :, :el] = dot(lowt, mixed[:, to]).astype(BF).reshape(*split, el)
        rs3.core[t].start()
    gmixed[...] = dot(low[...], wo[...]).astype(BF)
    rs2.add_one(0)
    rs2.add_one(1)
    gq, gk, gv = gate, up, gp

    buddy = me.pair(1 - me.core, me.z)
    swaps = []
    for i in range(2):
        at = pl.ds(i * d // 2, d // 2)
        for j, (src, dst) in enumerate(((gk2, ak), (gv2, av))):
            m = 2 * i + j
            swaps.append(remote(src.at[:, at], dst.at[:, at], ss.at[m], ss.at[4 + m], buddy))
    raw = gu

    def back_rope(half):
        def body(at):
            c, s = cos[at, :], -sin[at, :]
            for j in range(half * d // 2, (half + 1) * d // 2, 128):
                to = slice(j, j + 128)
                raw[at, j : j + 128] = turned(gq[at, to], c, s).astype(BF)
                keys = gk[at, to] + ak[at, to].astype(F32)
                raw[at, d + j : d + j + 128] = turned(keys, c, s).astype(BF)
                raw[at, 2 * d + j : 2 * d + j + 128] = (gv[at, to] + av[at, to].astype(F32)).astype(BF)

        rows_loop(n, 32, body)

    def grads_one(n1t, t):
        for c in range(3):
            cols = raw[:, c * d + t * el : c * d + (t + 1) * el]
            g1[:, :, :, t, :, c * el : (c + 1) * el] = dot(n1t, cols).astype(BF).reshape(*split, el)

    def step(i, carry):
        attend_back_pair(i, q, k, k2, v, v2, gmixed, mixed, lse, augk, augq, gq, gk, gk2, gv, gv2)

        @pl.when(i == 0)
        def _():
            for t in blocks:
                rs3.add_core(t)

        @pl.when(i == pairs // 2 - 1)
        def _():
            for swap in swaps[:2]:
                swap.start()
            for t in range(2, nt):
                rs2.add_one(t)

        @pl.when(i == pairs // 2)
        def _():
            for swap in swaps[:2]:
                swap.wait()
            back_rope(0)
            n1t = n1[...].T
            for t in range(nt // 2):
                grads_one(n1t, t)
                rs1.core[t].start()
            rs2.add_two(0)
            rs2.add_two(1)
            for t in blocks:
                rs3.add_one(t)

        return carry

    lax.fori_loop(0, pairs, step, 0)
    for swap in swaps[2:]:
        swap.start()
    for t in range(nt // 2):
        rs1.add_core(t)
    for t in range(2, nt):
        rs2.add_two(t)
    for swap in swaps[2:]:
        swap.wait()
    back_rope(1)
    n1t = n1[...].T
    for t in range(nt // 2, nt - 1):
        grads_one(n1t, t)
        rs1.core[t].start()
    grads_one(n1t, nt - 1)
    load_wf.wait()
    gtot[...] = dot(raw[...], w3[...], NT)
    for t in blocks:
        rs3.add_two(t)
    for t in range(nt // 2):
        rs1.add_one(t)

    def back_one(at):
        xhat, scale = standard(hid[at, :].astype(F32))
        e = gtot[at, :]
        gsum[1] += jnp.sum((e * xhat).reshape(-1, 8, d), axis=0)
        gin[at, :] = (gres[at, :] + norm_back(e, xhat, scale, gain_one)).astype(BF)

    for t in blocks:
        rows_loop(n // nt, 64, back_one, t * (n // nt))
        start_all(gi_s[t : t + 1])
    rows = []
    for v_ in (gsum[1], gsum[0]):
        total = jnp.sum(v_, axis=0, keepdims=True)
        upper = total.astype(BF).astype(F32)
        rows += [upper, total - upper]
    rows.append(jnp.zeros((SPARE - 4, d), F32))
    gain_cols = jnp.concatenate(rows, axis=0).T.astype(BF).reshape(*split, SPARE)
    last = nt - 1
    g1[:, :, :, last, :, 3 * el : 3 * el + SPARE] = gain_cols
    rs1.core[last].start()
    for t in range(nt // 2, nt):
        rs1.add_core(t)
    for t in range(nt // 2):
        rs1.add_two(t)
    for t in range(nt // 2, nt):
        rs1.add_one(t)
    total = rs3.total()
    grad_out[...] = total[:, :el].T
    total = rs2.total()
    grad_in[0] = total[:, :fl]
    grad_in[1] = total[:, fl : 2 * fl]
    grad_down[...] = total[:, 2 * fl : 3 * fl].T
    for t in range(nt // 2, nt):
        rs1.add_two(t)
    first = 3 * el // 128 * 128
    tile = (b2, b1, b0, last, slice(None), pl.ds(first, 128))
    gain_copies = [
        remote(g1.at[tile], rgain.at[s - 1], sg.at[s - 1], rg.at[s - 1], me.along(s)) for s in range(1, nt)
    ]
    for cp in gain_copies:
        cp.start()
    total = rs1.total()
    for c in range(3):
        grad_qkv[c] = total[:, c * el : (c + 1) * el]
    tail = g1[b2, b1, b0, last, :, first : first + 128].astype(F32)
    for s, cp in enumerate(gain_copies):
        cp.wait()
        tail = tail + rgain[s].astype(F32)
    tail = tail.T[3 * el - first : 3 * el - first + 8]
    grad_gains[...] = jnp.concatenate([tail[0:1] + tail[1:2], tail[2:3] + tail[3:4]], axis=0)
    for e in lo_e + gi_e:
        e.wait_recv()
    rs2.finish()
    rs3.finish()
    rs1.finish()
    wait_sends(lo_s)
    wait_sends(gi_s)


def layer(ndp, nt, w_qkv, w_out, w_in, w_down, gains, hid, cot, seg):
    half, d = hid.shape[2:]
    n = nt * half
    r, el, fl = w_qkv.shape[1], w_qkv.shape[2], w_in.shape[2]
    ff = fl * nt
    c1, c2, c3 = padded(3 * el + SPARE), padded(3 * fl), padded(el)
    freq = jnp.tile(THETA ** (-2.0 * jnp.arange(HD // 2, dtype=F32) / HD), 4)[None]
    sds = jax.ShapeDtypeStruct
    dma = pltpu.SemaphoreType.DMA
    vm, hbm = pl.BlockSpec(memory_space=VM), pl.BlockSpec(memory_space=pl.ANY)
    wide, act, act32 = VM((n, ff), F32), VM((n, d), BF), VM((n, d), F32)
    return pl.pallas_call(
        functools.partial(layer_kernel, ndp, nt),
        in_specs=[vm] * 5 + [hbm] * 2 + [vm] * 2,
        out_specs=[hbm] * 3 + [vm] * 5,
        out_shape=[sds((2, 2, half, d), BF)] * 2
        + [
            sds((d, 3 * d), BF),
            sds((3, r, el), F32),
            sds((el, r), F32),
            sds((2, r, fl), F32),
            sds((fl, r), F32),
            sds((2, r), F32),
        ],
        scratch_shapes=[act] * 9
        + [VM((d // (2 * HD), 2, n), F32)]
        + [VM((n, 2 * HD), F32)] * 2
        + [VM((2 * n, 2 * HD), BF), VM((HD, n), BF), VM((SPARE, d), F32)]
        + [VM((r, c), BF) for c in (c1, c2, c3)]
        + [VM(seg.shape, seg.dtype)]
        + [VM((d, 2 * ff), BF), VM((d, d), BF), VM((d, ff), BF)]
        + [wide] * 3
        + [VM((n, ff), BF), VM((n, 2 * ff), BF), act, act, act32, act32]
        + [act] * 4
        + [VM((2, 8, d), F32), VM((nt - 1, r, 128), BF), dma((2,)), dma((8,))]
        + [dma((4,))] * 4
        + [dma((nt - 1,))] * 2
        + scatter_scratch(nt, r, c2)
        + scatter_scratch(nt, r, c3)
        + scatter_scratch(nt, r, c1)
        + [dma((nt, 6))] * 6
        + [dma((3,))]
        + [dma((4,))] * 4
        + [dma((6,))],
        compiler_params=pltpu.CompilerParams(
            collective_id=0, has_side_effects=True, vmem_limit_bytes=WIDE
        ),
        name="layer",
    )(w_qkv, w_out, w_in, w_down, gains, hid, cot, seg, freq)


def finish_kernel(count, *refs):
    arrays, outs, held, (sems, more) = refs[:count], refs[count : 2 * count], refs[2 * count : 3 * count], refs[3 * count :]
    ins = [pltpu.make_async_copy(a, h, sems.at[i]) for i, (a, h) in enumerate(zip(arrays, held))]
    ends = [pltpu.make_async_copy(h, o, more.at[i]) for i, (h, o) in enumerate(zip(held, outs))]
    for copy in ins:
        copy.start()
    for copy, end in zip(ins, ends):
        copy.wait()
        end.start()
    for end in ends:
        end.wait()


def finish(arrays):
    hbm = pl.BlockSpec(memory_space=pl.ANY)
    count = len(arrays)
    return pl.pallas_call(
        functools.partial(finish_kernel, count),
        in_specs=[hbm] * count,
        out_specs=[hbm] * count,
        out_shape=[jax.ShapeDtypeStruct(a.shape, a.dtype) for a in arrays],
        scratch_shapes=[VM(a.shape, a.dtype) for a in arrays] + [pltpu.SemaphoreType.DMA((count,))] * 2,
        compiler_params=pltpu.CompilerParams(vmem_limit_bytes=WIDE),
        name="finish",
    )(*arrays)


def shards(hidden_in, cotangent, segment_ids, w_qkv, w_out, w_in, w_down, norm_gains):
    ndp, nt = lax.axis_size("dp"), lax.axis_size("tensor")
    stride = ndp // 8
    rows, local_len, d = hidden_in.shape
    half = local_len // 2
    low_groups = [[h * stride + i for i in range(stride)] for h in range(8)]

    def widen(v, axis):
        if stride == 1:
            return v
        return lax.all_gather(v, "dp", axis_index_groups=low_groups, axis=axis, tiled=True)

    def narrow(v, axis):
        if stride == 1:
            return v
        return lax.psum_scatter(
            v, "dp", scatter_dimension=axis, axis_index_groups=low_groups, tiled=True
        )

    split = lambda v: v.reshape(2, 2, half, d)
    out, gin, _, *grads = layer(
        ndp, nt,
        widen(w_qkv, 1), widen(w_out, 1), widen(w_in, 1), widen(w_down, 1), widen(norm_gains, 1),
        split(hidden_in), split(cotangent), segment_ids,
    )
    layer_out, grad_input, grad_qkv, grad_out, grad_in, grad_down, grad_gains = finish([out, gin, *grads])
    back = lambda t: t.reshape(rows, local_len, d)
    return (
        back(layer_out),
        back(grad_input),
        narrow(grad_qkv, 1),
        narrow(grad_out, 1),
        narrow(grad_in, 1),
        narrow(grad_down, 1),
        narrow(grad_gains, 1),
    )


def solution(mesh):
    placed = (
        P("dp", "tensor", None),
        P("dp", "tensor", None),
        P("dp", None),
        P(None, "dp", "tensor"),
        P("tensor", "dp"),
        P(None, "dp", "tensor"),
        P("tensor", "dp"),
        P(None, "dp"),
    )
    return jax.shard_map(
        shards,
        mesh=mesh,
        in_specs=placed,
        out_specs=(
            P("dp", "tensor", None),
            P("dp", "tensor", None),
            P(None, "dp", "tensor"),
            P("tensor", "dp"),
            P(None, "dp", "tensor"),
            P("tensor", "dp"),
            P(None, "dp"),
        ),
        check_vma=False,
    )
```
